32 devices in a mesh: dp: 2 (over core), expert: 16 (over z, y, x).
Axes of the slice: x: 2, y: 2, z: 4, core: 2. Of those that a mesh axis runs over, the one named last changes fastest.
Arguments:
- tokens: bfloat16 [4096, 1152], P(('dp', 'expert')), may hold values from -6 to 6
- out_grad: bfloat16 [4096, 1152], P(('dp', 'expert')), may hold values from -6 to 6
- gates: float32 [4096, 2], P(('dp', 'expert')), may hold values from 0.05 to 1
- expert_ids: int32 [4096, 2], P(('dp', 'expert')), may hold values from 0 to 15, all different within a row; in each aligned block of 128 rows (0 to 127, 128 to 255, ...) at most 24 rows name the same one
- swap_list: int32 [16], replicated, may hold values from 0 to 15, as said below
- w_in: bfloat16 [16, 1152, 3072], P('expert', None, 'dp'), may hold values from -0.1875 to 0.1875
- w_out: bfloat16 [16, 3072, 1152], P('expert', 'dp'), may hold values from -0.109375 to 0.109375
- first_moment: float32 [16, 1152, 3072], P('expert', None, 'dp'), may hold values from -12 to 12
- second_moment: float32 [16, 1152, 3072], P('expert', None, 'dp'), may hold values from 1 to 100
Outputs:
- x_grad: bfloat16 [4096, 1152], P(('dp', 'expert'))
- adam_out: bfloat16 [16, 1152, 3072], P('expert', None, 'dp')
The draws below stay inside these ranges and needn't reach their ends.
Inputs may be any that keep to these rules, and one draw needn't show every extreme that they name: `expert_ids`: among the 128 tokens of one device no expert is named by more than 24 rows; a token's two experts differ. swap_list[e] is e or e XOR 16/2, and swap_list[swap_list[e]] = e; swap_list[0] = 8 and swap_list[15] = 7.
All inputs are finite; a program needn't handle non-finite values.
Results may differ from the reference program's by a relative error of at most 0.015.
Values may be sent and summed in bfloat16 or wider, within the bound.
No kernel may reach another device: no remote copies, remote signals or barrier semaphores. Data moves between devices by JAX's collectives and lax.ppermute only.
A program may use at most 128 MiB of HBM per device.

```python
import math
import jax
import jax.numpy as jnp
import numpy as np
from jax import lax

D = 1152
FF = 3072
TOK_DEV = 128
ADAM_STEP = 100
EXPERTS = 16
CAP = 24
TOKENS = 4096
N_DP = 2
N_EXPERT = 16


def draw_swap_list(key, part):
    half_count = EXPERTS // 2
    flags = jax.random.randint(key, (half_count,), 0, 2).astype(jnp.int32)
    first_half = jnp.arange(half_count, dtype=jnp.int32)
    forced = jnp.logical_or(first_half == 0, first_half == half_count - 1)
    flags = jnp.where(forced, jnp.ones_like(flags), flags).astype(jnp.int32)
    low_part = first_half + flags * half_count
    high_part = first_half + half_count - flags * half_count
    return jnp.concatenate([low_part, high_part]).astype(jnp.int32)


def steps_of(stream_key, dims, pieces, smallest, top_value):
    level, own = 1.0, jax.random.fold_in(stream_key, 6)
    for axis_at, blocks in pieces:
        heights = jnp.exp(jax.random.uniform(jax.random.fold_in(own, axis_at), (blocks,), jnp.float32, smallest / len(pieces), top_value / len(pieces)))
        level = level * jnp.repeat(heights, dims[axis_at] // blocks).reshape([-1 if axis == axis_at else 1 for axis in range(len(dims))])
    return level


def deal_out(stream_key, own, number, rows, number_of, top, most, slope):
    ranking = jax.random.permutation(stream_key, number_of)
    packed, ordinary = portions_of(number_of, rows * top, most, slope, True), portions_of(number_of, rows * top, most, slope, False)
    places = jnp.arange(number_of)

    def named(lengths, offset_by):
        used = int((lengths > 0).sum())
        fixed = max(1, used // 4)
        passed = fixed + (places - fixed + offset_by * (used - fixed)) % max(1, number_of - fixed)
        return jnp.zeros((number_of,), jnp.int32).at[ranking[jnp.where(places < fixed, places, passed)]].set(jnp.asarray(lengths, jnp.int32))

    lengths = jnp.where(number % 4 == 0, named(packed, number // 4), named(ordinary, number - number // 4 - 1))
    mixed = jax.random.permutation(jax.random.fold_in(own, 3), number_of)
    giver, taker = mixed[0:number_of // 2 * 2:2], mixed[1:number_of // 2 * 2:2]
    slack = jnp.minimum(lengths[giver] - 1, most - lengths[taker]) // 2
    slack = jnp.where((giver == ranking[0]) | (taker == ranking[0]) | (lengths[taker] == 0), 0, jnp.maximum(slack, 0))
    passed = jax.random.randint(jax.random.fold_in(own, 4), (number_of // 2,), 0, 1 << 20) % (slack + 1)
    lengths = lengths.at[giver].add(-passed).at[taker].add(passed)
    items = jnp.searchsorted(jnp.cumsum(lengths), jnp.arange(rows * top), side="right").astype(jnp.int32)
    grid = items.reshape(top, rows).T
    grid = grid[jax.random.permutation(jax.random.fold_in(own, 1), rows)]
    offset_by = jax.random.randint(jax.random.fold_in(own, 2), (rows, 1), 0, top)
    return jnp.take_along_axis(grid, (jnp.arange(top)[None, :] + offset_by) % top, axis=1)


def portions_of(amount, total, bound, skew, full):
    portions = [(1 << 20) // math.isqrt(standing ** skew) + 1 for standing in range(1, amount + 1)]
    largest = bound if full else min(bound, max(-(-total // amount), total * portions[0] // sum(portions)))
    least = 1 if total - largest >= amount - 1 else 0
    holding, surplus = [largest] + [least] * (amount - 1), total - largest - least * (amount - 1)
    while surplus > 0:
        movable = [i for i in range(1, amount) if holding[i] < largest] or [i for i in range(1, amount) if holding[i] < bound]
        mass, budget = sum([portions[i] for i in movable]), surplus
        for i in movable:
            addition = min(bound - holding[i], max(1, budget * portions[i] // mass), surplus)
            holding[i] = holding[i] + addition
            surplus = surplus - addition
    return np.array(holding)


def centred(own_key, extent, deviation, reach, pieces=(), held_as=jnp.bfloat16):
    result = jax.random.normal(own_key, extent, jnp.float32) * deviation
    if len(pieces) > 0:
        result = steps_of(own_key, extent, pieces, -0.22, 0.18) * result
    return jnp.clip(result, min=-reach, max=reach).astype(held_as)


def setup_inputs(seed: int = 0) -> dict:
    key_list = jax.random.split(jax.random.key(seed), 10)
    tokens = centred(key_list[0], (TOKENS, D), 1.0, 6.0, ((0, 32),))
    out_grad = centred(key_list[1], (TOKENS, D), 1.0, 6.0, ((0, 32),))
    gates = jnp.clip(0.05 + 0.95 * jax.random.uniform(key_list[2], (TOKENS, 2), jnp.float32) ** steps_of(key_list[2], (TOKENS, 2), ((0, 32),), -0.2, 0.2), 0.05, 1.0)
    expert_ids_keys = jax.random.split(jax.random.fold_in(key_list[3], 1), TOKENS // TOK_DEV)
    expert_ids_turns = jax.random.permutation(jax.random.fold_in(key_list[3], 3), TOKENS // TOK_DEV)
    expert_ids = jax.vmap(lambda own, number: deal_out(jax.random.fold_in(key_list[3], 2), own, number, TOK_DEV, EXPERTS, 2, CAP, 1))(expert_ids_keys, expert_ids_turns).reshape((TOKENS, 2))
    swap_list = draw_swap_list(jax.random.fold_in(key_list[9], 71), 0)
    w_in = centred(key_list[5], (EXPERTS, D, FF), D ** -0.5, 0.1875, ((0, 16), (2, 2)))
    w_out = centred(key_list[6], (EXPERTS, FF, D), FF ** -0.5, 0.109375, ((0, 16), (1, 2)))
    first_moment = centred(key_list[7], (EXPERTS, D, FF), 2.0, 12.0, ((0, 16), (2, 2)), jnp.float32)
    second_moment = jnp.clip(jnp.exp(math.log(100.0) - 4.6051702 * jax.random.uniform(key_list[8], (EXPERTS, D, FF), jnp.float32) ** steps_of(key_list[8], (EXPERTS, D, FF), ((0, 16), (2, 2)), -0.2, 0.2)), 1.0, 100.0)
    return {"tokens": tokens, "out_grad": out_grad, "gates": gates, "expert_ids": expert_ids, "swap_list": swap_list, "w_in": w_in, "w_out": w_out, "first_moment": first_moment, "second_moment": second_moment}


coef_c = 0.7978845608028654
coef_a = 0.044715
beta_one = 0.9
beta_two = 0.999
adam_eps = 1e-08

def gelu_slope(pre_act):
    inner_arg = coef_c * (pre_act + coef_a * pre_act * pre_act * pre_act)
    tanh_val = jnp.tanh(inner_arg)
    return 0.5 * (1.0 + tanh_val) + 0.5 * pre_act * (1.0 - tanh_val * tanh_val) * coef_c * (1.0 + 3.0 * coef_a * pre_act * pre_act)

def reference(tokens, out_grad, gates, expert_ids, swap_list, w_in, w_out, first_moment, second_moment):
    assigned = TOKENS * 2
    flat_ids = expert_ids.reshape(-1)
    grad_pair = (gates[:, :, None] * out_grad[:, None, :].astype(jnp.float32)).astype(jnp.bfloat16).reshape(assigned, D)
    rows_most = N_DP * N_EXPERT * CAP
    group_size = FF // N_DP

    def one_expert(expert):
        hits = flat_ids == expert
        hit_count = jnp.sum(hits.astype(jnp.int32))
        picks = jnp.nonzero(hits, size=rows_most, fill_value=0)[0].astype(jnp.int32)
        valid = jnp.arange(rows_most, dtype=jnp.int32) < hit_count
        x_rows = jnp.where(valid[:, None], jnp.take(tokens, picks // 2, axis=0), jnp.zeros((), jnp.bfloat16)).astype(jnp.bfloat16)
        g_rows = jnp.where(valid[:, None], jnp.take(grad_pair, picks, axis=0), jnp.zeros((), jnp.bfloat16)).astype(jnp.bfloat16)
        w_in_e = lax.dynamic_index_in_dim(w_in, expert, 0, keepdims=False)
        w_out_e = lax.dynamic_index_in_dim(w_out, expert, 0, keepdims=False)
        pre_act = jnp.dot(x_rows, w_in_e, preferred_element_type=jnp.float32)
        act_grad = jnp.dot(g_rows, w_out_e.T, preferred_element_type=jnp.float32)
        pre_grad = (act_grad * gelu_slope(pre_act)).astype(jnp.bfloat16)
        parts = jnp.einsum('rgf,dgf->rgd', pre_grad.reshape(rows_most, N_DP, group_size).astype(jnp.float32), w_in_e.reshape(D, N_DP, group_size).astype(jnp.float32)).astype(jnp.bfloat16)
        row_grad = lax.optimization_barrier(jnp.sum(parts.astype(jnp.float32), axis=1)).astype(jnp.bfloat16)
        weight_grad = jnp.dot(x_rows.T, pre_grad, preferred_element_type=jnp.float32)
        return (picks, valid, row_grad, weight_grad)
    picks, valid, row_grads, weight_grads = lax.map(one_expert, jnp.arange(EXPERTS, dtype=jnp.int32))
    row_values = jnp.where(valid.reshape(-1)[:, None], row_grads.reshape(-1, D).astype(jnp.float32), jnp.zeros((), jnp.float32))
    grad_acc = jnp.zeros((assigned, D), jnp.float32).at[picks.reshape(-1)].add(row_values)
    x_grad = lax.optimization_barrier(jnp.sum(grad_acc.reshape(TOKENS, 2, D), axis=1)).astype(jnp.bfloat16)
    first_new = beta_one * first_moment + (1.0 - beta_one) * weight_grads
    second_new = beta_two * second_moment + (1.0 - beta_two) * weight_grads * weight_grads
    adam_full = first_new / (1.0 - beta_one ** ADAM_STEP) / (jnp.sqrt(second_new / (1.0 - beta_two ** ADAM_STEP)) + adam_eps)
    adam_full = adam_full.astype(jnp.bfloat16)
    return (x_grad, jnp.take(adam_full, swap_list.astype(jnp.int32), axis=0))
```

```python
import functools

import jax
import jax.numpy as jnp
from jax import lax
from jax.experimental import pallas as pl
from jax.experimental.pallas import tpu as pltpu
from jax.sharding import PartitionSpec as P

ADAM_STEP = 100


coef_c = 0.7978845608028654
coef_a = 0.044715
beta_one = 0.9
beta_two = 0.999
adam_eps = 1e-08


f32 = jnp.float32
bf16 = jnp.bfloat16
NN = (((1,), (0,)), ((), ()))
NT = (((1,), (1,)), ((), ()))
TN = (((0,), (0,)), ((), ()))


def mxu(a, b, dims):
    return lax.dot_general(a, b, dims, preferred_element_type=f32)


def gelu_slope(pre_act):
    inner_arg = coef_c * (pre_act + coef_a * pre_act * pre_act * pre_act)
    tanh_val = jnp.tanh(inner_arg)
    return 0.5 * (1.0 + tanh_val) + 0.5 * pre_act * (1.0 - tanh_val * tanh_val) * coef_c * (
        1.0 + 3.0 * coef_a * pre_act * pre_act
    )


def adam_step(weight_grad, first_moment, second_moment):
    first_new = beta_one * first_moment + (1.0 - beta_one) * weight_grad
    second_new = beta_two * second_moment + (1.0 - beta_two) * weight_grad * weight_grad
    return (
        first_new
        / (1.0 - beta_one**ADAM_STEP)
        / (jnp.sqrt(second_new / (1.0 - beta_two**ADAM_STEP)) + adam_eps)
    ).astype(bf16)


def pack_kernel(expert_count, capacity, ids_ref, gates_ref, x_ref, g_ref, rows_ref, where_ref):
    tok_count, width = x_ref.shape
    slots = expert_count * capacity
    first = ids_ref[0:1, :]
    second = ids_ref[1:2, :]
    experts = lax.broadcasted_iota(jnp.int32, (expert_count, tok_count), 0)
    hit_first = experts == first
    hit_second = experts == second
    hits = jnp.where(hit_first | hit_second, 1.0, 0.0).astype(bf16)
    earlier = lax.broadcasted_iota(jnp.int32, (tok_count, tok_count), 0)
    later = lax.broadcasted_iota(jnp.int32, (tok_count, tok_count), 1)
    upper = jnp.where(earlier < later, 1.0, 0.0).astype(bf16)
    before = mxu(hits, upper, NN)
    slot_first = jnp.sum(jnp.where(hit_first, before, 0.0), axis=0, keepdims=True)
    slot_second = jnp.sum(jnp.where(hit_second, before, 0.0), axis=0, keepdims=True)
    pos_first = first * capacity + slot_first.astype(jnp.int32)
    pos_second = second * capacity + slot_second.astype(jnp.int32)
    where_ref[0:1, :] = pos_first
    where_ref[1:2, :] = pos_second
    row = lax.broadcasted_iota(jnp.int32, (slots, tok_count), 0)
    at_first = row == pos_first
    at_second = row == pos_second
    pick = jnp.where(at_first | at_second, 1.0, 0.0).astype(bf16)
    gate = jnp.sum(
        jnp.where(at_first, gates_ref[0:1, :], 0.0) + jnp.where(at_second, gates_ref[1:2, :], 0.0),
        axis=1,
        keepdims=True,
    )
    rows_ref[:, :width] = mxu(pick, x_ref[...], NN).astype(bf16)
    rows_ref[:, width:] = (gate * mxu(pick, g_ref[...], NN)).astype(bf16)


def pack_rows(id_rows, gate_rows, tokens, out_grad, expert_count, capacity):
    tok_count, width = tokens.shape
    slots = expert_count * capacity
    return pl.pallas_call(
        functools.partial(pack_kernel, expert_count, capacity),
        out_shape=(
            jax.ShapeDtypeStruct((slots, 2 * width), bf16),
            jax.ShapeDtypeStruct((2, tok_count), jnp.int32),
        ),
        name="pack_rows",
    )(id_rows, gate_rows, tokens, out_grad)


def chunk_kernel(blocks, make_xt, *refs):
    rows = refs[:blocks]
    refs = refs[blocks:]
    if make_xt:
        w_in_ref, w_out_ref, m_ref, v_ref, adam_ref, pre_ref, xt_ref = refs
    else:
        xt_ref, w_in_ref, w_out_ref, m_ref, v_ref, adam_ref, pre_ref = refs
    width = m_ref.shape[0]
    per = rows[0].shape[0]
    if make_xt:

        @pl.when(pl.program_id(0) == 0)
        def _():
            for b in range(blocks):
                xt_ref[:, b * per : (b + 1) * per] = rows[b][:, :width].T

    for b in range(blocks):
        pre_act = mxu(rows[b][:, :width], w_in_ref[...], NN)
        act_grad = mxu(rows[b][:, width:], w_out_ref[...], NT)
        pre_ref[b * per : (b + 1) * per, :] = (act_grad * gelu_slope(pre_act)).astype(bf16)
    weight_grad = mxu(xt_ref[...], pre_ref[...], NN)
    adam_ref[...] = adam_step(weight_grad, m_ref[...], v_ref[...])


def chunk_step(rows, x_t, w_in, w_out, first_moment, second_moment, start, tiles, tile):
    blocks = len(rows)
    per, width = rows[0].shape[0], rows[0].shape[1] // 2
    total = blocks * per
    first = start // tile
    whole = lambda j: (0, 0)
    in_specs = [pl.BlockSpec(r.shape, whole, pipeline_mode=pl.Buffered(1)) for r in rows]
    args = list(rows)
    make_xt = x_t is None
    if not make_xt:
        in_specs.append(pl.BlockSpec((width, total), whole, pipeline_mode=pl.Buffered(1)))
        args.append(x_t)
    columns = pl.BlockSpec((width, tile), lambda j: (0, first + j))
    in_specs += [columns, pl.BlockSpec((tile, width), lambda j: (first + j, 0)), columns, columns]
    args += [w_in, w_out, first_moment, second_moment]
    out_shape = [
        jax.ShapeDtypeStruct((width, tiles * tile), bf16),
        jax.ShapeDtypeStruct((total, tiles * tile), bf16),
    ]
    out_specs = [
        pl.BlockSpec((width, tile), lambda j: (0, j)),
        pl.BlockSpec((total, tile), lambda j: (0, j)),
    ]
    if make_xt:
        out_shape.append(jax.ShapeDtypeStruct((width, total), bf16))
        out_specs.append(pl.BlockSpec((width, total), whole))
    flops = 6 * total * width * tile * tiles
    return pl.pallas_call(
        functools.partial(chunk_kernel, blocks, make_xt),
        grid=(tiles,),
        in_specs=in_specs,
        out_specs=out_specs,
        out_shape=out_shape,
        compiler_params=pltpu.CompilerParams(vmem_limit_bytes=50 * 2**20),
        cost_estimate=pl.CostEstimate(
            flops=flops, bytes_accessed=tiles * tile * width * 14, transcendentals=0
        ),
        name="chunk_step",
    )(*args)


def part_kernel(count, *refs):
    pre, w_in_ref, out_ref = refs[:count], refs[count], refs[count + 1]
    total = None
    at = 0
    for p in pre:
        size = p.shape[1]
        term = mxu(p[...], w_in_ref[:, at : at + size], NT)
        total = term if total is None else total + term
        at += size
    out_ref[...] = total.astype(bf16)


def part_rows(pre_chunks, w_in, steps):
    width, inner = w_in.shape
    total = pre_chunks[0].shape[0]
    rows = total // steps
    return pl.pallas_call(
        functools.partial(part_kernel, len(pre_chunks)),
        grid=(steps,),
        in_specs=[pl.BlockSpec((rows, p.shape[1]), lambda i: (i, 0)) for p in pre_chunks]
        + [pl.BlockSpec((width, inner), lambda i: (0, 0), pipeline_mode=pl.Buffered(1))],
        out_specs=pl.BlockSpec((rows, width), lambda i: (i, 0)),
        out_shape=jax.ShapeDtypeStruct((total, width), bf16),
        compiler_params=pltpu.CompilerParams(vmem_limit_bytes=40 * 2**20),
        cost_estimate=pl.CostEstimate(
            flops=2 * total * width * inner,
            bytes_accessed=2 * (total * inner + width * inner + total * width),
            transcendentals=0,
        ),
        name="part_rows",
    )(*pre_chunks, w_in)


def combine_kernel(where_ref, back_ref, out_ref):
    slots, tok_count = back_ref.shape[0], out_ref.shape[0]
    row = lax.broadcasted_iota(jnp.int32, (slots, tok_count), 0)
    pick = (row == where_ref[0:1, :]) | (row == where_ref[1:2, :])
    pick = jnp.where(pick, 1.0, 0.0).astype(bf16)
    out_ref[...] = mxu(pick, back_ref[...], TN).astype(bf16)


def combine_rows(where_to, returned, tok_count):
    return pl.pallas_call(
        combine_kernel,
        out_shape=jax.ShapeDtypeStruct((tok_count, returned.shape[1]), bf16),
        name="combine_rows",
    )(where_to, returned)


def dp_shift(block, apart):
    count = lax.axis_size("dp")
    return lax.ppermute(block, "dp", [(i, i ^ apart) for i in range(count)])


def split_columns(inner, tile):
    tiles = inner // tile
    sizes = []
    size = 1
    while tiles > 0:
        size = min(size, tiles)
        sizes.append(size)
        tiles -= size
        size += 1
    return sizes


def shards(
    tokens, out_grad, gates, expert_ids, swap_list, w_in, w_out, first_moment, second_moment
):
    expert_count = lax.axis_size("expert")
    dp_count = lax.axis_size("dp")
    half = 1 << (expert_count.bit_length() - 2)
    own_index = lax.axis_index("expert")
    lane_ids = jnp.arange(expert_count, dtype=jnp.int32)
    partner_me = jnp.sum(jnp.where(lane_ids == own_index, swap_list, 0))
    is_moved = partner_me != own_index
    tok_count, width = tokens.shape
    capacity = 3 * tok_count // expert_count
    slots = expert_count * capacity

    rows, where_to = pack_rows(
        expert_ids.T, gates.T, tokens, out_grad, expert_count, capacity
    )
    own = lax.all_to_all(
        rows.reshape(expert_count, capacity, 2 * width),
        "expert",
        split_axis=0,
        concat_axis=0,
        tiled=True,
    ).reshape(slots, 2 * width)
    all_rows = [own] + [dp_shift(own, d) for d in range(1, dp_count)]

    inner = w_in.shape[2]
    tile = 256 if inner % 256 == 0 else 128
    route = [(e, e ^ half) for e in range(expert_count)]
    x_t = None
    at = 0
    adam_own, adam_got, pre_chunks = [], [], []
    for tiles in split_columns(inner, tile):
        done = chunk_step(
            all_rows, x_t, w_in[0], w_out[0], first_moment[0], second_moment[0], at, tiles, tile
        )
        if x_t is None:
            x_t = done[2]
        adam_own.append(done[0])
        pre_chunks.append(done[1])
        adam_got.append(lax.ppermute(done[0], "expert", route))
        at += tiles * tile

    part = part_rows(pre_chunks, w_in[0], 2 * dp_count)
    total = part[:slots].astype(f32)
    for d in range(1, dp_count):
        total = total + dp_shift(part[d * slots : (d + 1) * slots], d).astype(f32)
    returned = lax.all_to_all(
        total.astype(bf16).reshape(expert_count, capacity, width),
        "expert",
        split_axis=0,
        concat_axis=0,
        tiled=True,
    ).reshape(slots, width)
    x_grad = combine_rows(where_to, returned, tok_count)

    adam_out = jnp.concatenate(
        [jnp.where(is_moved, got, kept) for got, kept in zip(adam_got, adam_own)], axis=1
    )
    return (x_grad, adam_out[None])


def solution(mesh):
    in_specs = (
        P(("dp", "expert"), None),
        P(("dp", "expert"), None),
        P(("dp", "expert"), None),
        P(("dp", "expert"), None),
        P(),
        P("expert", None, "dp"),
        P("expert", "dp", None),
        P("expert", None, "dp"),
        P("expert", None, "dp"),
    )
    out_specs = (P(("dp", "expert"), None), P("expert", None, "dp"))
    return jax.shard_map(shards, mesh=mesh, in_specs=in_specs, out_specs=out_specs, check_vma=False)
```

```python
import functools
import itertools
import math

import jax
import jax.numpy as jnp
from jax import lax
from jax.experimental import pallas as pl
from jax.experimental.pallas import tpu as pltpu
from jax.sharding import PartitionSpec as P

ADAM_STEP = 100


coef_c = 0.7978845608028654
coef_a = 0.044715
beta_one = 0.9
beta_two = 0.999
adam_eps = 1e-08


VMEM_LIMIT = 60 * 1024 * 1024

f32 = jnp.float32
bf16 = jnp.bfloat16
NN = (((1,), (0,)), ((), ()))
NT = (((1,), (1,)), ((), ()))
TN = (((0,), (0,)), ((), ()))


def mxu(a, b, dims):
    return lax.dot_general(a, b, dims, preferred_element_type=f32)


def gelu_slope(pre_act):
    inner_arg = coef_c * (pre_act + coef_a * pre_act * pre_act * pre_act)
    tanh_val = jnp.tanh(inner_arg)
    return 0.5 * (1.0 + tanh_val) + 0.5 * pre_act * (1.0 - tanh_val * tanh_val) * coef_c * (
        1.0 + 3.0 * coef_a * pre_act * pre_act
    )


def adam_step(weight_grad, first_moment, second_moment):
    first_new = beta_one * first_moment + (1.0 - beta_one) * weight_grad
    second_new = beta_two * second_moment + (1.0 - beta_two) * weight_grad * weight_grad
    return (
        first_new
        / (1.0 - beta_one**ADAM_STEP)
        / (jnp.sqrt(second_new / (1.0 - beta_two**ADAM_STEP)) + adam_eps)
    ).astype(bf16)


def pack_kernel(expert_count, capacity, ids_ref, gates_ref, x_ref, g_ref, rows_ref, where_ref):
    tok_count, width = x_ref.shape
    slots = expert_count * capacity
    first = ids_ref[0:1, :]
    second = ids_ref[1:2, :]
    experts = lax.broadcasted_iota(jnp.int32, (expert_count, tok_count), 0)
    hit_first = experts == first
    hit_second = experts == second
    hits = jnp.where(hit_first | hit_second, 1.0, 0.0).astype(bf16)
    earlier = lax.broadcasted_iota(jnp.int32, (tok_count, tok_count), 0)
    later = lax.broadcasted_iota(jnp.int32, (tok_count, tok_count), 1)
    upper = jnp.where(earlier < later, 1.0, 0.0).astype(bf16)
    before = mxu(hits, upper, NN)
    slot_first = jnp.sum(jnp.where(hit_first, before, 0.0), axis=0, keepdims=True)
    slot_second = jnp.sum(jnp.where(hit_second, before, 0.0), axis=0, keepdims=True)
    pos_first = first * capacity + slot_first.astype(jnp.int32)
    pos_second = second * capacity + slot_second.astype(jnp.int32)
    where_ref[0:1, :] = pos_first
    where_ref[1:2, :] = pos_second
    row = lax.broadcasted_iota(jnp.int32, (slots, tok_count), 0)
    at_first = row == pos_first
    at_second = row == pos_second
    pick = jnp.where(at_first | at_second, 1.0, 0.0).astype(bf16)
    gate = jnp.sum(
        jnp.where(at_first, gates_ref[0:1, :], 0.0) + jnp.where(at_second, gates_ref[1:2, :], 0.0),
        axis=1,
        keepdims=True,
    )
    rows_ref[:, :width] = mxu(pick, x_ref[...], NN).astype(bf16)
    rows_ref[:, width:] = (gate * mxu(pick, g_ref[...], NN)).astype(bf16)


def pack_rows(id_rows, gate_rows, tokens, out_grad, expert_count, capacity):
    tok_count, width = tokens.shape
    slots = expert_count * capacity
    return pl.pallas_call(
        functools.partial(pack_kernel, expert_count, capacity),
        out_shape=(
            jax.ShapeDtypeStruct((slots, 2 * width), bf16),
            jax.ShapeDtypeStruct((2, tok_count), jnp.int32),
        ),
        name="pack_rows",
    )(id_rows, gate_rows, tokens, out_grad)


def pre_tile(rows, w_in, w_out, pre_ref):
    per, width = rows[0].shape[0], rows[0].shape[1] // 2
    for b, block in enumerate(rows):
        pre_act = mxu(block[:, :width], w_in, NN)
        act_grad = mxu(block[:, width:], w_out, NT)
        pre_ref[b * per : (b + 1) * per, :] = (act_grad * gelu_slope(pre_act)).astype(bf16)


def first_kernel(blocks, *refs):
    rows = refs[:blocks]
    w_in_ref, w_out_ref, m_ref, v_ref, adam_ref, pre_ref, xt_ref = refs[blocks:]
    width, per = m_ref.shape[0], rows[0].shape[0]
    for b in range(blocks):
        xt_ref[:, b * per : (b + 1) * per] = rows[b][:, :width].T
    pre_tile(rows, w_in_ref[...], w_out_ref[...], pre_ref)
    weight_grad = mxu(xt_ref[...], pre_ref[...], NN)
    adam_ref[...] = adam_step(weight_grad, m_ref[...], v_ref[...])


def first_step(rows, w_in, w_out, first_moment, second_moment, tile):
    per, width = rows[0].shape[0], rows[0].shape[1] // 2
    total = len(rows) * per
    corner = lambda i: (0, 0)
    columns = pl.BlockSpec((width, tile), corner)
    return pl.pallas_call(
        functools.partial(first_kernel, len(rows)),
        grid=(1,),
        in_specs=[pl.BlockSpec(r.shape, corner) for r in rows]
        + [columns, pl.BlockSpec((tile, width), corner), columns, columns],
        out_specs=[
            columns,
            pl.BlockSpec((total, tile), corner),
            pl.BlockSpec((width, total), corner),
        ],
        out_shape=[
            jax.ShapeDtypeStruct((width, tile), bf16),
            jax.ShapeDtypeStruct((total, tile), bf16),
            jax.ShapeDtypeStruct((width, total), bf16),
        ],
        compiler_params=pltpu.CompilerParams(vmem_limit_bytes=VMEM_LIMIT),
        cost_estimate=pl.CostEstimate(
            flops=6 * total * width * tile, bytes_accessed=14 * tile * width, transcendentals=0
        ),
        name="first_step",
    )(*rows, w_in, w_out, first_moment, second_moment)


def rest_kernel(blocks, *refs):
    rows = refs[:blocks]
    first_ref, w_first_ref, w_in_ref, w_out_ref, pre_ref = refs[blocks : blocks + 5]
    parts = refs[blocks + 5 : -1]
    total_ref = refs[-1]
    per = rows[0].shape[0]
    step = pl.program_id(0)

    @pl.when(step == 0)
    def _():
        total_ref[...] = mxu(first_ref[...], w_first_ref[...], NT)

    pre_tile(rows, w_in_ref[...], w_out_ref[...], pre_ref)
    total_ref[...] += mxu(pre_ref[...], w_in_ref[...], NT)

    @pl.when(step == pl.num_programs(0) - 1)
    def _():
        for b in range(blocks):
            parts[b][...] = total_ref[b * per : (b + 1) * per, :].astype(bf16)


def rest_step(rows, pre_first, w_in, w_out, tile):
    per, width = rows[0].shape[0], rows[0].shape[1] // 2
    total = len(rows) * per
    tiles = w_in.shape[1] // tile - 1
    corner = lambda j: (0, 0)
    return pl.pallas_call(
        functools.partial(rest_kernel, len(rows)),
        grid=(tiles,),
        in_specs=[pl.BlockSpec(r.shape, corner) for r in rows]
        + [
            pl.BlockSpec((total, tile), corner),
            pl.BlockSpec((width, tile), corner),
            pl.BlockSpec((width, tile), lambda j: (0, j + 1)),
            pl.BlockSpec((tile, width), lambda j: (j + 1, 0)),
        ],
        out_specs=[pl.BlockSpec((total, tile), lambda j: (0, j))]
        + [pl.BlockSpec((per, width), corner) for _ in rows],
        out_shape=[jax.ShapeDtypeStruct((total, tiles * tile), bf16)]
        + [jax.ShapeDtypeStruct((per, width), bf16) for _ in rows],
        scratch_shapes=[pltpu.VMEM((total, width), f32)],
        compiler_params=pltpu.CompilerParams(vmem_limit_bytes=VMEM_LIMIT),
        cost_estimate=pl.CostEstimate(
            flops=6 * total * width * tile * tiles,
            bytes_accessed=4 * tile * width * tiles,
            transcendentals=0,
        ),
        name="rest_step",
    )(*rows, pre_first, w_in, w_in, w_out)


def adam_kernel(xt_ref, pre_ref, m_ref, v_ref, *outs):
    weight_grad = mxu(xt_ref[...], pre_ref[...], NN)
    step = adam_step(weight_grad, m_ref[...], v_ref[...])
    at = 0
    for out in outs:
        out[...] = step[at : at + out.shape[0], :]
        at += out.shape[0]


def adam_columns(x_t, pre_rest, first_moment, second_moment, start, tiles, tile, pieces):
    width, total = x_t.shape
    rows = width // pieces
    columns = pl.BlockSpec((width, tile), lambda j: (0, start + j))
    return pl.pallas_call(
        adam_kernel,
        grid=(tiles,),
        in_specs=[
            pl.BlockSpec((width, total), lambda j: (0, 0)),
            pl.BlockSpec((total, tile), lambda j: (0, start - 1 + j)),
            columns,
            columns,
        ],
        out_specs=[pl.BlockSpec((rows, tile), lambda j: (0, j)) for _ in range(pieces)],
        out_shape=[jax.ShapeDtypeStruct((rows, tiles * tile), bf16) for _ in range(pieces)],
        compiler_params=pltpu.CompilerParams(vmem_limit_bytes=VMEM_LIMIT),
        cost_estimate=pl.CostEstimate(
            flops=2 * total * width * tile * tiles,
            bytes_accessed=10 * tile * width * tiles,
            transcendentals=0,
        ),
        name="adam_columns",
    )(x_t, pre_rest, first_moment, second_moment)


def place_kernel(boxes, rows, moved_ref, *refs):
    out_ref = refs[-1]
    step = pl.program_id(0)
    for n, (row, col, high, wide) in enumerate(boxes):
        inside = (step >= row // rows) & (step < (row + high) // rows)

        @pl.when(inside & (moved_ref[0] == 0))
        def _(n=n, col=col, wide=wide):
            out_ref[:, col : col + wide] = refs[2 * n][...]

        @pl.when(inside & (moved_ref[0] != 0))
        def _(n=n, col=col, wide=wide):
            out_ref[:, col : col + wide] = refs[2 * n + 1][...]


def place(moved, pieces, width, inner, rows):
    boxes = [piece[:4] for piece in pieces]
    in_specs, args = [], []

    def spec(row, high, wide, wanted):
        def block(i, moved_ref):
            near = jnp.clip(i - row // rows, 0, high // rows - 1)
            return (jnp.where(moved_ref[0] == wanted, near, 0), 0)

        return pl.BlockSpec((rows, wide), block)

    for row, col, high, wide, kept, got in pieces:
        in_specs += [spec(row, high, wide, 0), spec(row, high, wide, 1)]
        args += [kept, got]
    return pl.pallas_call(
        functools.partial(place_kernel, boxes, rows),
        grid_spec=pltpu.PrefetchScalarGridSpec(
            num_scalar_prefetch=1,
            grid=(width // rows,),
            in_specs=in_specs,
            out_specs=pl.BlockSpec((rows, inner), lambda i, moved_ref: (i, 0)),
        ),
        out_shape=jax.ShapeDtypeStruct((width, inner), bf16),
        name="place",
    )(moved, *args)


def swap_plans(half):
    line = half >> 1
    groups = {}
    for e in range(half):
        groups.setdefault(e & ~(line | 1), []).append(e)
    groups = list(groups.values())
    forced = {0, half - 1}
    size = len(groups[0])

    def sets(members, k):
        must = forced & set(members)
        return [set(s) for s in itertools.combinations(members, k) if must <= set(s)]

    choices = [[sets(g, k) for g in groups] for k in range(1, size + 1)]
    if half < 4 or sum(math.prod(len(c) for c in by_k) for by_k in choices) > 32:
        return None, None
    plans = [set().union(*picked) for by_k in choices for picked in itertools.product(*by_k)]
    table = []
    for mask in range(1 << half):
        moved = forced | {e for e in range(half) if mask >> e & 1}
        table.append(next(n for n, plan in enumerate(plans) if moved <= plan))
    return plans, table


def combine_kernel(where_ref, back_ref, out_ref):
    slots, tok_count = back_ref.shape[0], out_ref.shape[0]
    row = lax.broadcasted_iota(jnp.int32, (slots, tok_count), 0)
    pick = (row == where_ref[0:1, :]) | (row == where_ref[1:2, :])
    pick = jnp.where(pick, 1.0, 0.0).astype(bf16)
    out_ref[...] = mxu(pick, back_ref[...], TN).astype(bf16)


def combine_rows(where_to, returned, tok_count):
    return pl.pallas_call(
        combine_kernel,
        out_shape=jax.ShapeDtypeStruct((tok_count, returned.shape[1]), bf16),
        name="combine_rows",
    )(where_to, returned)


def dp_shift(block, apart):
    count = lax.axis_size("dp")
    return lax.ppermute(block, "dp", [(i, i ^ apart) for i in range(count)])


def shards(
    tokens, out_grad, gates, expert_ids, swap_list, w_in, w_out, first_moment, second_moment
):
    expert_count = lax.axis_size("expert")
    dp_count = lax.axis_size("dp")
    half = 1 << (expert_count.bit_length() - 2)
    own_index = lax.axis_index("expert")
    lane_ids = jnp.arange(expert_count, dtype=jnp.int32)
    partner_me = jnp.sum(jnp.where(lane_ids == own_index, swap_list, 0))
    is_moved = (partner_me != own_index).astype(jnp.int32).reshape(1)
    moved_bits = jnp.where((swap_list != lane_ids) & (lane_ids < half), 1 << lane_ids, 0)
    moved_mask = jnp.sum(moved_bits)
    tok_count, width = tokens.shape
    capacity = 3 * tok_count // expert_count
    slots = expert_count * capacity

    rows, where_to = pack_rows(expert_ids.T, gates.T, tokens, out_grad, expert_count, capacity)
    own = lax.all_to_all(
        rows.reshape(expert_count, capacity, 2 * width),
        "expert",
        split_axis=0,
        concat_axis=0,
        tiled=True,
    ).reshape(slots, 2 * width)
    all_rows = [own] + [dp_shift(own, d) for d in range(1, dp_count)]

    inner = w_in.shape[2]
    tile = 256 if inner % 256 == 0 else 128
    tiles = inner // tile
    plans, table = swap_plans(half)
    route = [(e, e ^ half) for e in range(expert_count)]
    across = [(e, e ^ 1) for e in range(expert_count)]

    first, pre_first, x_t = first_step(
        all_rows, w_in[0], w_out[0], first_moment[0], second_moment[0], tile
    )
    first_got = lax.ppermute(first, "expert", route)
    pieces = [(0, 0, width, tile, first, first_got)]

    pre_rest, *parts = rest_step(all_rows, pre_first, w_in[0], w_out[0], tile)
    total = parts[0].astype(f32)
    for d in range(1, dp_count):
        total = total + dp_shift(parts[d], d).astype(f32)
    returned = lax.all_to_all(
        total.astype(bf16).reshape(expert_count, capacity, width),
        "expert",
        split_axis=0,
        concat_axis=0,
        tiled=True,
    ).reshape(slots, width)

    chunks = [n for n in (2 * (tiles - 1) // 5, tiles - 1 - 2 * (tiles - 1) // 5) if n > 0]
    at = 1
    near, far, boxes = [], [], []
    for n in chunks:
        done = adam_columns(
            x_t, pre_rest, first_moment[0], second_moment[0], at, n, tile, 2 if plans else 1
        )
        if plans:
            near.append(done[0])
            far.append(done[1])
            boxes.append((at * tile, n * tile))
        else:
            got = lax.ppermute(done[0], "expert", route)
            pieces.append((0, at * tile, width, n * tile, done[0], got))
        at += n
    if plans:
        lent = [lax.ppermute(f, "expert", across) for f in far]

        def branch(plan):
            pairs = [(e, e ^ half) for p in plan for e in (p, p ^ half)]
            skew = [(e ^ 1, f) for e, f in pairs]

            def run(near, lent):
                return (
                    [lax.ppermute(a, "expert", pairs) for a in near],
                    [lax.ppermute(b, "expert", skew) for b in lent],
                )

            return run

        choice = jnp.asarray(table, jnp.int32)[moved_mask]
        near_got, far_got = lax.switch(choice, [branch(p) for p in plans], near, lent)
        for n, (col, wide) in enumerate(boxes):
            pieces.append((0, col, width // 2, wide, near[n], near_got[n]))
            pieces.append((width // 2, col, width // 2, wide, far[n], far_got[n]))

    x_grad = combine_rows(where_to, returned, tok_count)
    adam_out = place(is_moved, pieces, width, inner, width // 8)
    return (x_grad, adam_out[None])


def solution(mesh):
    in_specs = (
        P(("dp", "expert"), None),
        P(("dp", "expert"), None),
        P(("dp", "expert"), None),
        P(("dp", "expert"), None),
        P(),
        P("expert", None, "dp"),
        P("expert", "dp", None),
        P("expert", None, "dp"),
        P("expert", None, "dp"),
    )
    out_specs = (P(("dp", "expert"), None), P("expert", None, "dp"))
    return jax.shard_map(shards, mesh=mesh, in_specs=in_specs, out_specs=out_specs, check_vma=False)
```

```python
import functools
import itertools

import jax
import jax.numpy as jnp
from jax import lax
from jax.experimental import pallas as pl
from jax.experimental.pallas import tpu as pltpu
from jax.sharding import PartitionSpec as P


ADAM_STEP = 100


coef_c = 0.7978845608028654
coef_a = 0.044715
beta_one = 0.9
beta_two = 0.999
adam_eps = 1e-08


VMEM_LIMIT = 60 * 1024 * 1024

f32 = jnp.float32
bf16 = jnp.bfloat16
NN = (((1,), (0,)), ((), ()))
NT = (((1,), (1,)), ((), ()))
TN = (((0,), (0,)), ((), ()))


def mxu(a, b, dims):
    return lax.dot_general(a, b, dims, preferred_element_type=f32)


def gelu_slope(pre_act):
    inner_arg = coef_c * (pre_act + coef_a * pre_act * pre_act * pre_act)
    tanh_val = jnp.tanh(inner_arg)
    return 0.5 * (1.0 + tanh_val) + 0.5 * pre_act * (1.0 - tanh_val * tanh_val) * coef_c * (
        1.0 + 3.0 * coef_a * pre_act * pre_act
    )


def adam_step(weight_grad, first_moment, second_moment):
    first_new = beta_one * first_moment + (1.0 - beta_one) * weight_grad
    second_new = beta_two * second_moment + (1.0 - beta_two) * weight_grad * weight_grad
    return (
        first_new
        / (1.0 - beta_one**ADAM_STEP)
        / (jnp.sqrt(second_new / (1.0 - beta_two**ADAM_STEP)) + adam_eps)
    ).astype(bf16)


def pack_kernel(expert_count, capacity, ids_ref, gates_ref, x_ref, g_ref, rows_ref, where_ref):
    tok_count, width = x_ref.shape
    slots = expert_count * capacity
    first = ids_ref[0:1, :]
    second = ids_ref[1:2, :]
    experts = lax.broadcasted_iota(jnp.int32, (expert_count, tok_count), 0)
    hit_first = experts == first
    hit_second = experts == second
    hits = jnp.where(hit_first | hit_second, 1.0, 0.0).astype(bf16)
    earlier = lax.broadcasted_iota(jnp.int32, (tok_count, tok_count), 0)
    later = lax.broadcasted_iota(jnp.int32, (tok_count, tok_count), 1)
    upper = jnp.where(earlier < later, 1.0, 0.0).astype(bf16)
    before = mxu(hits, upper, NN)
    slot_first = jnp.sum(jnp.where(hit_first, before, 0.0), axis=0, keepdims=True)
    slot_second = jnp.sum(jnp.where(hit_second, before, 0.0), axis=0, keepdims=True)
    pos_first = first * capacity + slot_first.astype(jnp.int32)
    pos_second = second * capacity + slot_second.astype(jnp.int32)
    where_ref[0:1, :] = pos_first
    where_ref[1:2, :] = pos_second
    row = lax.broadcasted_iota(jnp.int32, (slots, tok_count), 0)
    at_first = row == pos_first
    at_second = row == pos_second
    pick = jnp.where(at_first | at_second, 1.0, 0.0).astype(bf16)
    gate = jnp.sum(
        jnp.where(at_first, gates_ref[0:1, :], 0.0) + jnp.where(at_second, gates_ref[1:2, :], 0.0),
        axis=1,
        keepdims=True,
    )
    rows_ref[:, :width] = mxu(pick, x_ref[...], NN).astype(bf16)
    rows_ref[:, width:] = (gate * mxu(pick, g_ref[...], NN)).astype(bf16)


def pack_rows(id_rows, gate_rows, tokens, out_grad, expert_count, capacity):
    tok_count, width = tokens.shape
    slots = expert_count * capacity
    return pl.pallas_call(
        functools.partial(pack_kernel, expert_count, capacity),
        out_shape=(
            jax.ShapeDtypeStruct((slots, 2 * width), bf16),
            jax.ShapeDtypeStruct((2, tok_count), jnp.int32),
        ),
        name="pack_rows",
    )(id_rows, gate_rows, tokens, out_grad)


def pre_tile(rows, w_in, w_out, pre_ref):
    per, width = rows[0].shape[0], rows[0].shape[1] // 2
    for b, block in enumerate(rows):
        pre_act = mxu(block[:, :width], w_in, NN)
        act_grad = mxu(block[:, width:], w_out, NT)
        pre_ref[b * per : (b + 1) * per, :] = (act_grad * gelu_slope(pre_act)).astype(bf16)


def first_kernel(blocks, *refs):
    rows = refs[:blocks]
    w_in_ref, w_out_ref, m_ref, v_ref, adam_ref, pre_ref, xt_ref = refs[blocks:]
    width, per = m_ref.shape[0], rows[0].shape[0]
    for b in range(blocks):
        xt_ref[:, b * per : (b + 1) * per] = rows[b][:, :width].T
    pre_tile(rows, w_in_ref[...], w_out_ref[...], pre_ref)
    weight_grad = mxu(xt_ref[...], pre_ref[...], NN)
    adam_ref[...] = adam_step(weight_grad, m_ref[...], v_ref[...])


def first_step(rows, w_in, w_out, first_moment, second_moment, tile):
    per, width = rows[0].shape[0], rows[0].shape[1] // 2
    total = len(rows) * per
    corner = lambda i: (0, 0)
    columns = pl.BlockSpec((width, tile), corner)
    return pl.pallas_call(
        functools.partial(first_kernel, len(rows)),
        grid=(1,),
        in_specs=[pl.BlockSpec(r.shape, corner) for r in rows]
        + [columns, pl.BlockSpec((tile, width), corner), columns, columns],
        out_specs=[
            columns,
            pl.BlockSpec((total, tile), corner),
            pl.BlockSpec((width, total), corner),
        ],
        out_shape=[
            jax.ShapeDtypeStruct((width, tile), bf16),
            jax.ShapeDtypeStruct((total, tile), bf16),
            jax.ShapeDtypeStruct((width, total), bf16),
        ],
        compiler_params=pltpu.CompilerParams(vmem_limit_bytes=VMEM_LIMIT),
        cost_estimate=pl.CostEstimate(
            flops=6 * total * width * tile, bytes_accessed=14 * tile * width, transcendentals=0
        ),
        name="first_step",
    )(*rows, w_in, w_out, first_moment, second_moment)


def rest_kernel(blocks, *refs):
    rows = refs[:blocks]
    first_ref, w_first_ref, w_in_ref, w_out_ref, pre_ref = refs[blocks : blocks + 5]
    parts = refs[blocks + 5 : -1]
    total_ref = refs[-1]
    per = rows[0].shape[0]
    step = pl.program_id(0)

    @pl.when(step == 0)
    def _():
        total_ref[...] = mxu(first_ref[...], w_first_ref[...], NT)

    pre_tile(rows, w_in_ref[...], w_out_ref[...], pre_ref)
    total_ref[...] += mxu(pre_ref[...], w_in_ref[...], NT)

    @pl.when(step == pl.num_programs(0) - 1)
    def _():
        for b in range(blocks):
            parts[b][...] = total_ref[b * per : (b + 1) * per, :].astype(bf16)


def rest_step(rows, pre_first, w_in, w_out, tile):
    per, width = rows[0].shape[0], rows[0].shape[1] // 2
    total = len(rows) * per
    tiles = w_in.shape[1] // tile - 1
    corner = lambda j: (0, 0)
    return pl.pallas_call(
        functools.partial(rest_kernel, len(rows)),
        grid=(tiles,),
        in_specs=[pl.BlockSpec(r.shape, corner) for r in rows]
        + [
            pl.BlockSpec((total, tile), corner),
            pl.BlockSpec((width, tile), corner),
            pl.BlockSpec((width, tile), lambda j: (0, j + 1)),
            pl.BlockSpec((tile, width), lambda j: (j + 1, 0)),
        ],
        out_specs=[pl.BlockSpec((total, tile), lambda j: (0, j))]
        + [pl.BlockSpec((per, width), corner) for _ in rows],
        out_shape=[jax.ShapeDtypeStruct((total, tiles * tile), bf16)]
        + [jax.ShapeDtypeStruct((per, width), bf16) for _ in rows],
        scratch_shapes=[pltpu.VMEM((total, width), f32)],
        compiler_params=pltpu.CompilerParams(vmem_limit_bytes=VMEM_LIMIT),
        cost_estimate=pl.CostEstimate(
            flops=6 * total * width * tile * tiles,
            bytes_accessed=4 * tile * width * tiles,
            transcendentals=0,
        ),
        name="rest_step",
    )(*rows, pre_first, w_in, w_in, w_out)


def adam_kernel(xt_ref, pre_ref, m_ref, v_ref, out_ref):
    weight_grad = mxu(xt_ref[...], pre_ref[...], NN)
    out_ref[...] = adam_step(weight_grad, m_ref[...], v_ref[...])


def adam_block(x_t, pre_rest, first_moment, second_moment, start, tiles, tile, part, parts):
    width, total = x_t.shape
    rows = width // parts
    block = pl.BlockSpec((rows, tile), lambda j: (part, start + j))
    return pl.pallas_call(
        adam_kernel,
        grid=(tiles,),
        in_specs=[
            pl.BlockSpec((rows, total), lambda j: (part, 0)),
            pl.BlockSpec((total, tile), lambda j: (0, start - 1 + j)),
            block,
            block,
        ],
        out_specs=pl.BlockSpec((rows, tile), lambda j: (0, j)),
        out_shape=jax.ShapeDtypeStruct((rows, tiles * tile), bf16),
        compiler_params=pltpu.CompilerParams(vmem_limit_bytes=VMEM_LIMIT),
        cost_estimate=pl.CostEstimate(
            flops=2 * total * rows * tile * tiles,
            bytes_accessed=10 * tile * rows * tiles,
            transcendentals=0,
        ),
    )(x_t, pre_rest, first_moment, second_moment)


def place_kernel(boxes, source_ref, *refs):
    sources, at = [], 0
    for box in boxes:
        sources.append(refs[at : at + box[4]])
        at += box[4]
    out_ref = refs[at]
    bufs = refs[at + 1 : at + 1 + len(boxes)]
    in_sem, out_sem = refs[at + 1 + len(boxes) :]
    for n, arrays in enumerate(sources):
        for k, array in enumerate(arrays):
            last = k == len(arrays) - 1
            wanted = source_ref[0] >= k if last else source_ref[0] == k

            @pl.when(wanted)
            def _(n=n, array=array):
                pltpu.make_async_copy(array, bufs[n], in_sem.at[n]).start()

    puts = []
    for n, (row, col, high, wide, _) in enumerate(boxes):
        pltpu.make_async_copy(sources[n][0], bufs[n], in_sem.at[n]).wait()
        put = pltpu.make_async_copy(
            bufs[n], out_ref.at[pl.ds(row, high), pl.ds(col, wide)], out_sem.at[n]
        )
        put.start()
        puts.append(put)
    for put in puts:
        put.wait()


def place(source, pieces, width, inner):
    boxes = [piece[:4] + (len(piece[4]),) for piece in pieces]
    args = [array for piece in pieces for array in piece[4]]
    return pl.pallas_call(
        functools.partial(place_kernel, boxes),
        in_specs=[pl.BlockSpec(memory_space=pltpu.SMEM)]
        + [pl.BlockSpec(memory_space=pl.ANY) for _ in args],
        out_specs=pl.BlockSpec(memory_space=pl.ANY),
        out_shape=jax.ShapeDtypeStruct((width, inner), bf16),
        scratch_shapes=[pltpu.VMEM((box[2], box[3]), bf16) for box in boxes]
        + [pltpu.SemaphoreType.DMA((len(boxes),)), pltpu.SemaphoreType.DMA((len(boxes),))],
        compiler_params=pltpu.CompilerParams(vmem_limit_bytes=VMEM_LIMIT),
        cost_estimate=pl.CostEstimate(
            flops=0, bytes_accessed=4 * width * inner, transcendentals=0
        ),
        name="place",
    )(source, *args)


def swap_plans(half):
    line = half >> 1
    groups = {}
    for e in range(half):
        groups.setdefault(e & ~(line | 1), []).append(e)
    groups = list(groups.values())
    if half < 4 or len(groups) > 2:
        return []
    forced = {0, half - 1}
    switches = []
    for members in groups:
        must = forced & set(members)
        plans = [
            set(s)
            for k in range(2, len(members) + 1)
            for s in itertools.combinations(members, k)
            if must <= set(s)
        ]
        table = []
        for mask in range(1 << half):
            moved = must | {e for e in members if mask >> e & 1}
            table.append(next(n for n, plan in enumerate(plans) if moved <= plan))
        switches.append((plans, table))
    return switches


def combine_kernel(where_ref, back_ref, out_ref):
    slots, tok_count = back_ref.shape[0], out_ref.shape[0]
    row = lax.broadcasted_iota(jnp.int32, (slots, tok_count), 0)
    pick = (row == where_ref[0:1, :]) | (row == where_ref[1:2, :])
    pick = jnp.where(pick, 1.0, 0.0).astype(bf16)
    out_ref[...] = mxu(pick, back_ref[...], TN).astype(bf16)


def combine_rows(where_to, returned, tok_count):
    return pl.pallas_call(
        combine_kernel,
        out_shape=jax.ShapeDtypeStruct((tok_count, returned.shape[1]), bf16),
        name="combine_rows",
    )(where_to, returned)


def dp_shift(block, apart):
    count = lax.axis_size("dp")
    return lax.ppermute(block, "dp", [(i, i ^ apart) for i in range(count)])


def shards(
    tokens, out_grad, gates, expert_ids, swap_list, w_in, w_out, first_moment, second_moment
):
    expert_count = lax.axis_size("expert")
    dp_count = lax.axis_size("dp")
    half = 1 << (expert_count.bit_length() - 2)
    own_index = lax.axis_index("expert")
    lane_ids = jnp.arange(expert_count, dtype=jnp.int32)
    partner_me = jnp.sum(jnp.where(lane_ids == own_index, swap_list, 0))
    is_moved = (partner_me != own_index).astype(jnp.int32)
    moved_bits = jnp.where((swap_list != lane_ids) & (lane_ids < half), 1 << lane_ids, 0)
    moved_mask = jnp.sum(moved_bits)
    tok_count, width = tokens.shape
    capacity = 3 * tok_count // expert_count
    slots = expert_count * capacity

    rows, where_to = pack_rows(expert_ids.T, gates.T, tokens, out_grad, expert_count, capacity)
    own = lax.all_to_all(
        rows.reshape(expert_count, capacity, 2 * width),
        "expert",
        split_axis=0,
        concat_axis=0,
        tiled=True,
    ).reshape(slots, 2 * width)
    all_rows = [own] + [dp_shift(own, d) for d in range(1, dp_count)]

    inner = w_in.shape[2]
    tile = 256 if inner % 256 == 0 else 128
    tiles = inner // tile
    route = [(e, e ^ half) for e in range(expert_count)]
    across = [(e, e ^ 1) for e in range(expert_count)]

    first, pre_first, x_t = first_step(
        all_rows, w_in[0], w_out[0], first_moment[0], second_moment[0], tile
    )
    first_got = lax.ppermute(first, "expert", route)
    pieces = [(0, 0, width, tile, [first, first_got])]

    pre_rest, *parts = rest_step(all_rows, pre_first, w_in[0], w_out[0], tile)
    total = parts[0].astype(f32)
    for d in range(1, dp_count):
        total = total + dp_shift(parts[d], d).astype(f32)
    returned = lax.all_to_all(
        total.astype(bf16).reshape(expert_count, capacity, width),
        "expert",
        split_axis=0,
        concat_axis=0,
        tiled=True,
    ).reshape(slots, width)

    switches = swap_plans(half) if tiles > 2 else []
    direct = 1 if switches else tiles - 1
    moments = (first_moment[0], second_moment[0])
    second = adam_block(x_t, pre_rest, *moments, 1, direct, tile, 0, 1)
    second_got = lax.ppermute(second, "expert", route)
    pieces.append((0, tile, width, direct * tile, [second, second_got]))
    group = jnp.zeros((), jnp.int32)

    if switches:
        at, left = 1 + direct, tiles - 1 - direct
        far = adam_block(x_t, pre_rest, *moments, at, left, tile, 1, 2)
        lent = lax.ppermute(far, "expert", across)
        near = adam_block(x_t, pre_rest, *moments, at, left, tile, 0, 2)

        def branch(plan):
            pairs = [(e, e ^ half) for p in plan for e in (p, p ^ half)]
            skew = [(e ^ 1, f) for e, f in pairs]

            def run(near, lent):
                return (
                    lax.ppermute(near, "expert", pairs),
                    lax.ppermute(lent, "expert", skew),
                )

            return run

        near_all, far_all = [near], [far]
        for n, (plans, table) in enumerate(switches):
            choice = jnp.asarray(table, jnp.int32)[moved_mask]
            near_got, far_got = lax.switch(choice, [branch(p) for p in plans], near, lent)
            near_all.append(near_got)
            far_all.append(far_got)
            members = {e for plan in plans for p in plan for e in (p, p ^ half)}
            here = jnp.asarray([e in members for e in range(expert_count)])
            group += jnp.sum(jnp.where(here & (lane_ids == own_index), n, 0))
        wide = left * tile
        pieces.append((0, at * tile, width // 2, wide, near_all))
        pieces.append((width // 2, at * tile, width // 2, wide, far_all))

    x_grad = combine_rows(where_to, returned, tok_count)
    source = (is_moved * (1 + group)).reshape(1)
    adam_out = place(source, pieces, width, inner)
    return (x_grad, adam_out[None])


def solution(mesh):
    in_specs = (
        P(("dp", "expert"), None),
        P(("dp", "expert"), None),
        P(("dp", "expert"), None),
        P(("dp", "expert"), None),
        P(),
        P("expert", None, "dp"),
        P("expert", "dp", None),
        P("expert", None, "dp"),
        P("expert", None, "dp"),
    )
    out_specs = (P(("dp", "expert"), None), P("expert", None, "dp"))

    return jax.shard_map(shards, mesh=mesh, in_specs=in_specs, out_specs=out_specs, check_vma=False)
```

```python
import functools
import itertools

import jax
import jax.numpy as jnp
from jax import lax
from jax.experimental import pallas as pl
from jax.experimental.pallas import tpu as pltpu
from jax.sharding import PartitionSpec as P


ADAM_STEP = 100


coef_c = 0.7978845608028654
coef_a = 0.044715
beta_one = 0.9
beta_two = 0.999
adam_eps = 1e-08


MIB = 2**20

f32 = jnp.float32
bf16 = jnp.bfloat16
NN = (((1,), (0,)), ((), ()))
NT = (((1,), (1,)), ((), ()))
TN = (((0,), (0,)), ((), ()))


def mxu(a, b, dims):
    return lax.dot_general(a, b, dims, preferred_element_type=f32)


def gelu_slope(pre_act):
    inner_arg = coef_c * (pre_act + coef_a * pre_act * pre_act * pre_act)
    tanh_val = jnp.tanh(inner_arg)
    return 0.5 * (1.0 + tanh_val) + 0.5 * pre_act * (1.0 - tanh_val * tanh_val) * coef_c * (
        1.0 + 3.0 * coef_a * pre_act * pre_act
    )


def adam_step(weight_grad, first_moment, second_moment):
    first_new = beta_one * first_moment + (1.0 - beta_one) * weight_grad
    second_new = beta_two * second_moment + (1.0 - beta_two) * weight_grad * weight_grad
    return (
        first_new
        / (1.0 - beta_one**ADAM_STEP)
        / (jnp.sqrt(second_new / (1.0 - beta_two**ADAM_STEP)) + adam_eps)
    ).astype(bf16)


def pack_kernel(expert_count, capacity, ids_ref, gates_ref, x_ref, g_ref, rows_ref, where_ref):
    tok_count, width = x_ref.shape
    slots = expert_count * capacity
    first = ids_ref[0:1, :]
    second = ids_ref[1:2, :]
    experts = lax.broadcasted_iota(jnp.int32, (expert_count, tok_count), 0)
    hit_first = experts == first
    hit_second = experts == second
    hits = jnp.where(hit_first | hit_second, 1.0, 0.0).astype(bf16)
    earlier = lax.broadcasted_iota(jnp.int32, (tok_count, tok_count), 0)
    later = lax.broadcasted_iota(jnp.int32, (tok_count, tok_count), 1)
    upper = jnp.where(earlier < later, 1.0, 0.0).astype(bf16)
    before = mxu(hits, upper, NN)
    slot_first = jnp.sum(jnp.where(hit_first, before, 0.0), axis=0, keepdims=True)
    slot_second = jnp.sum(jnp.where(hit_second, before, 0.0), axis=0, keepdims=True)
    pos_first = first * capacity + slot_first.astype(jnp.int32)
    pos_second = second * capacity + slot_second.astype(jnp.int32)
    where_ref[0:1, :] = pos_first
    where_ref[1:2, :] = pos_second
    row = lax.broadcasted_iota(jnp.int32, (slots, tok_count), 0)
    at_first = row == pos_first
    at_second = row == pos_second
    pick = jnp.where(at_first | at_second, 1.0, 0.0).astype(bf16)
    gate = jnp.sum(
        jnp.where(at_first, gates_ref[0:1, :], 0.0) + jnp.where(at_second, gates_ref[1:2, :], 0.0),
        axis=1,
        keepdims=True,
    )
    rows_ref[:, :width] = mxu(pick, x_ref[...], NN).astype(bf16)
    rows_ref[:, width:] = (gate * mxu(pick, g_ref[...], NN)).astype(bf16)


def pack_rows(id_rows, gate_rows, tokens, out_grad, expert_count, capacity):
    tok_count, width = tokens.shape
    slots = expert_count * capacity
    return pl.pallas_call(
        functools.partial(pack_kernel, expert_count, capacity),
        out_shape=(
            jax.ShapeDtypeStruct((slots, 2 * width), bf16),
            jax.ShapeDtypeStruct((2, tok_count), jnp.int32),
        ),
        name="pack_rows",
    )(id_rows, gate_rows, tokens, out_grad)


def pre_tile(rows, w_in, w_out, pre_ref):
    per, width = rows[0].shape[0], rows[0].shape[1] // 2
    for b, block in enumerate(rows):
        pre_act = mxu(block[:, :width], w_in, NN)
        act_grad = mxu(block[:, width:], w_out, NT)
        pre_ref[b * per : (b + 1) * per, :] = (act_grad * gelu_slope(pre_act)).astype(bf16)


def first_kernel(blocks, *refs):
    rows = refs[:blocks]
    w_in_ref, w_out_ref, m_ref, v_ref, adam_ref, pre_ref, xt_ref = refs[blocks:]
    width, per = m_ref.shape[0], rows[0].shape[0]
    for b in range(blocks):
        xt_ref[:, b * per : (b + 1) * per] = rows[b][:, :width].T
    pre_tile(rows, w_in_ref[...], w_out_ref[...], pre_ref)
    weight_grad = mxu(xt_ref[...], pre_ref[...], NN)
    adam_ref[...] = adam_step(weight_grad, m_ref[...], v_ref[...])


def first_step(rows, w_in, w_out, first_moment, second_moment, tile):
    per, width = rows[0].shape[0], rows[0].shape[1] // 2
    total = len(rows) * per
    corner = lambda i: (0, 0)
    columns = pl.BlockSpec((width, tile), corner)
    return pl.pallas_call(
        functools.partial(first_kernel, len(rows)),
        grid=(1,),
        in_specs=[pl.BlockSpec(r.shape, corner) for r in rows]
        + [columns, pl.BlockSpec((tile, width), corner), columns, columns],
        out_specs=[
            columns,
            pl.BlockSpec((total, tile), corner),
            pl.BlockSpec((width, total), corner),
        ],
        out_shape=[
            jax.ShapeDtypeStruct((width, tile), bf16),
            jax.ShapeDtypeStruct((total, tile), bf16),
            jax.ShapeDtypeStruct((width, total), bf16),
        ],
        compiler_params=pltpu.CompilerParams(vmem_limit_bytes=56 * MIB),
        cost_estimate=pl.CostEstimate(
            flops=6 * total * width * tile, bytes_accessed=14 * tile * width, transcendentals=0
        ),
        name="first_step",
    )(*rows, w_in, w_out, first_moment, second_moment)


def rest_kernel(blocks, *refs):
    rows = refs[:blocks]
    first_ref, w_first_ref, w_in_ref, w_out_ref, pre_ref = refs[blocks : blocks + 5]
    parts = refs[blocks + 5 : -1]
    total_ref = refs[-1]
    per = rows[0].shape[0]
    step = pl.program_id(0)

    @pl.when(step == 0)
    def _():
        total_ref[...] = mxu(first_ref[...], w_first_ref[...], NT)

    pre_tile(rows, w_in_ref[...], w_out_ref[...], pre_ref)
    total_ref[...] += mxu(pre_ref[...], w_in_ref[...], NT)

    @pl.when(step == pl.num_programs(0) - 1)
    def _():
        for b in range(blocks):
            parts[b][...] = total_ref[b * per : (b + 1) * per, :].astype(bf16)


def rest_step(rows, pre_first, w_in, w_out, tile):
    per, width = rows[0].shape[0], rows[0].shape[1] // 2
    total = len(rows) * per
    tiles = w_in.shape[1] // tile - 1
    corner = lambda j: (0, 0)
    return pl.pallas_call(
        functools.partial(rest_kernel, len(rows)),
        grid=(tiles,),
        in_specs=[pl.BlockSpec(r.shape, corner) for r in rows]
        + [
            pl.BlockSpec((total, tile), corner),
            pl.BlockSpec((width, tile), corner),
            pl.BlockSpec((width, tile), lambda j: (0, j + 1)),
            pl.BlockSpec((tile, width), lambda j: (j + 1, 0)),
        ],
        out_specs=[pl.BlockSpec((total, tile), lambda j: (0, j))]
        + [pl.BlockSpec((per, width), corner) for _ in rows],
        out_shape=[jax.ShapeDtypeStruct((total, tiles * tile), bf16)]
        + [jax.ShapeDtypeStruct((per, width), bf16) for _ in rows],
        scratch_shapes=[pltpu.VMEM((total, width), f32)],
        compiler_params=pltpu.CompilerParams(vmem_limit_bytes=56 * MIB),
        cost_estimate=pl.CostEstimate(
            flops=6 * total * width * tile * tiles,
            bytes_accessed=4 * tile * width * tiles,
            transcendentals=0,
        ),
        name="rest_step",
    )(*rows, pre_first, w_in, w_in, w_out)


def adam_kernel(xt_ref, pre_ref, m_ref, v_ref, out_ref):
    weight_grad = mxu(xt_ref[...], pre_ref[...], NN)
    out_ref[...] = adam_step(weight_grad, m_ref[...], v_ref[...])


def adam_block(x_t, pre_rest, first_moment, second_moment, start, tiles, tile, part, parts):
    width, total = x_t.shape
    rows = width // parts
    block = pl.BlockSpec((rows, tile), lambda j: (part, start + j))
    return pl.pallas_call(
        adam_kernel,
        grid=(tiles,),
        in_specs=[
            pl.BlockSpec((rows, total), lambda j: (part, 0)),
            pl.BlockSpec((total, tile), lambda j: (0, start - 1 + j)),
            block,
            block,
        ],
        out_specs=pl.BlockSpec((rows, tile), lambda j: (0, j)),
        out_shape=jax.ShapeDtypeStruct((rows, tiles * tile), bf16),
        compiler_params=pltpu.CompilerParams(vmem_limit_bytes=60 * MIB),
        cost_estimate=pl.CostEstimate(
            flops=2 * total * rows * tile * tiles,
            bytes_accessed=10 * tile * rows * tiles,
            transcendentals=0,
        ),
    )(x_t, pre_rest, first_moment, second_moment)


def place_kernel(boxes, source_ref, *refs):
    sources, at = [], 0
    for box in boxes:
        sources.append(refs[at : at + box[4]])
        at += box[4]
    out_ref = refs[at]
    bufs = refs[at + 1 : at + 1 + len(boxes)]
    in_sem, out_sem = refs[at + 1 + len(boxes) :]
    for n, arrays in enumerate(sources):
        for k, array in enumerate(arrays):
            last = k == len(arrays) - 1
            wanted = source_ref[0] >= k if last else source_ref[0] == k

            @pl.when(wanted)
            def _(n=n, array=array):
                pltpu.make_async_copy(array, bufs[n], in_sem.at[n]).start()

    puts = []
    for n, (row, col, high, wide, _) in enumerate(boxes):
        pltpu.make_async_copy(sources[n][0], bufs[n], in_sem.at[n]).wait()
        put = pltpu.make_async_copy(
            bufs[n], out_ref.at[pl.ds(row, high), pl.ds(col, wide)], out_sem.at[n]
        )
        put.start()
        puts.append(put)
    for put in puts:
        put.wait()


def place(source, pieces, width, inner):
    boxes = [piece[:4] + (len(piece[4]),) for piece in pieces]
    args = [array for piece in pieces for array in piece[4]]
    return pl.pallas_call(
        functools.partial(place_kernel, boxes),
        in_specs=[pl.BlockSpec(memory_space=pltpu.SMEM)]
        + [pl.BlockSpec(memory_space=pl.ANY) for _ in args],
        out_specs=pl.BlockSpec(memory_space=pl.ANY),
        out_shape=jax.ShapeDtypeStruct((width, inner), bf16),
        scratch_shapes=[pltpu.VMEM((box[2], box[3]), bf16) for box in boxes]
        + [pltpu.SemaphoreType.DMA((len(boxes),)), pltpu.SemaphoreType.DMA((len(boxes),))],
        compiler_params=pltpu.CompilerParams(vmem_limit_bytes=8 * MIB),
        cost_estimate=pl.CostEstimate(
            flops=0, bytes_accessed=4 * width * inner, transcendentals=0
        ),
        name="place",
    )(source, *args)


def swap_plans(half):
    line = half >> 1
    groups = {}
    for e in range(half):
        groups.setdefault(e & ~(line | 1), []).append(e)
    groups = list(groups.values())
    if half < 4 or len(groups) > 2:
        return []
    forced = {0, half - 1}
    switches = []
    for members in groups:
        must = forced & set(members)
        plans = [
            set(s)
            for k in range(2, len(members) + 1)
            for s in itertools.combinations(members, k)
            if must <= set(s)
        ]
        table = []
        for mask in range(1 << half):
            moved = must | {e for e in members if mask >> e & 1}
            table.append(next(n for n, plan in enumerate(plans) if moved <= plan))
        switches.append((plans, table))
    return switches


def combine_kernel(where_ref, back_ref, out_ref):
    slots, tok_count = back_ref.shape[0], out_ref.shape[0]
    row = lax.broadcasted_iota(jnp.int32, (slots, tok_count), 0)
    pick = (row == where_ref[0:1, :]) | (row == where_ref[1:2, :])
    pick = jnp.where(pick, 1.0, 0.0).astype(bf16)
    out_ref[...] = mxu(pick, back_ref[...], TN).astype(bf16)


def combine_rows(where_to, returned, tok_count):
    return pl.pallas_call(
        combine_kernel,
        out_shape=jax.ShapeDtypeStruct((tok_count, returned.shape[1]), bf16),
        name="combine_rows",
    )(where_to, returned)


def dp_shift(block, apart):
    count = lax.axis_size("dp")
    return lax.ppermute(block, "dp", [(i, i ^ apart) for i in range(count)])


def shards(
    tokens, out_grad, gates, expert_ids, swap_list, w_in, w_out, first_moment, second_moment
):
    expert_count = lax.axis_size("expert")
    dp_count = lax.axis_size("dp")
    half = 1 << (expert_count.bit_length() - 2)
    own_index = lax.axis_index("expert")
    lane_ids = jnp.arange(expert_count, dtype=jnp.int32)
    partner_me = jnp.sum(jnp.where(lane_ids == own_index, swap_list, 0))
    is_moved = (partner_me != own_index).astype(jnp.int32)
    moved_bits = jnp.where((swap_list != lane_ids) & (lane_ids < half), 1 << lane_ids, 0)
    moved_mask = jnp.sum(moved_bits)
    tok_count, width = tokens.shape
    capacity = 3 * tok_count // expert_count
    slots = expert_count * capacity

    rows, where_to = pack_rows(expert_ids.T, gates.T, tokens, out_grad, expert_count, capacity)
    own = lax.all_to_all(
        rows.reshape(expert_count, capacity, 2 * width),
        "expert",
        split_axis=0,
        concat_axis=0,
        tiled=True,
    ).reshape(slots, 2 * width)
    all_rows = [own] + [dp_shift(own, d) for d in range(1, dp_count)]

    inner = w_in.shape[2]
    tile = 256 if inner % 256 == 0 else 128
    tiles = inner // tile
    route = [(e, e ^ half) for e in range(expert_count)]
    across = [(e, e ^ 1) for e in range(expert_count)]

    first, pre_first, x_t = first_step(
        all_rows, w_in[0], w_out[0], first_moment[0], second_moment[0], tile
    )
    first_got = lax.ppermute(first, "expert", route)
    pieces = [(0, 0, width, tile, [first, first_got])]

    pre_rest, *parts = rest_step(all_rows, pre_first, w_in[0], w_out[0], tile)
    total = parts[0].astype(f32)
    for d in range(1, dp_count):
        total = total + dp_shift(parts[d], d).astype(f32)
    returned = lax.all_to_all(
        total.astype(bf16).reshape(expert_count, capacity, width),
        "expert",
        split_axis=0,
        concat_axis=0,
        tiled=True,
    ).reshape(slots, width)

    x_grad = combine_rows(where_to, returned, tok_count)
    switches = swap_plans(half) if tiles > 2 else []
    direct = 1 if switches else tiles - 1
    moments = (first_moment[0], second_moment[0])
    second = adam_block(x_t, pre_rest, *moments, 1, direct, tile, 0, 1)
    second_got = lax.ppermute(second, "expert", route)
    pieces.append((0, tile, width, direct * tile, [second, second_got]))
    group = jnp.zeros((), jnp.int32)

    if switches:
        at, left = 1 + direct, tiles - 1 - direct
        far = adam_block(x_t, pre_rest, *moments, at, left, tile, 1, 2)
        lent = lax.ppermute(far, "expert", across)
        near = adam_block(x_t, pre_rest, *moments, at, left, tile, 0, 2)

        def branch(plan):
            pairs = [(e, e ^ half) for p in plan for e in (p, p ^ half)]
            skew = [(e ^ 1, f) for e, f in pairs]

            def run(near, lent):
                return (
                    lax.ppermute(near, "expert", pairs),
                    lax.ppermute(lent, "expert", skew),
                )

            return run

        near, lent, x_grad = lax.optimization_barrier((near, lent, x_grad))
        near_all, far_all = [near], [far]
        for n, (plans, table) in enumerate(switches):
            choice = jnp.asarray(table, jnp.int32)[moved_mask]
            near_got, far_got = lax.switch(choice, [branch(p) for p in plans], near, lent)
            near_all.append(near_got)
            far_all.append(far_got)
            members = {e for plan in plans for p in plan for e in (p, p ^ half)}
            here = jnp.asarray([e in members for e in range(expert_count)])
            group += jnp.sum(jnp.where(here & (lane_ids == own_index), n, 0))
        wide = left * tile
        pieces.append((0, at * tile, width // 2, wide, near_all))
        pieces.append((width // 2, at * tile, width // 2, wide, far_all))

    source = (is_moved * (1 + group)).reshape(1)
    adam_out = place(source, pieces, width, inner)
    return (x_grad, adam_out[None])


def solution(mesh):
    in_specs = (
        P(("dp", "expert"), None),
        P(("dp", "expert"), None),
        P(("dp", "expert"), None),
        P(("dp", "expert"), None),
        P(),
        P("expert", None, "dp"),
        P("expert", "dp", None),
        P("expert", None, "dp"),
        P("expert", None, "dp"),
    )
    out_specs = (P(("dp", "expert"), None), P("expert", None, "dp"))

    return jax.shard_map(shards, mesh=mesh, in_specs=in_specs, out_specs=out_specs, check_vma=False)
```

```python
import functools
import itertools

import jax
import jax.numpy as jnp
from jax import lax
from jax.experimental import pallas as pl
from jax.experimental.pallas import tpu as pltpu
from jax.sharding import PartitionSpec as P


ADAM_STEP = 100


coef_c = 0.7978845608028654
coef_a = 0.044715
beta_one = 0.9
beta_two = 0.999
adam_eps = 1e-08


MIB = 2**20

f32 = jnp.float32
bf16 = jnp.bfloat16
NN = (((1,), (0,)), ((), ()))
NT = (((1,), (1,)), ((), ()))
TN = (((0,), (0,)), ((), ()))


def mxu(a, b, dims):
    return lax.dot_general(a, b, dims, preferred_element_type=f32)


def gelu_slope(pre_act):
    inner_arg = coef_c * (pre_act + coef_a * pre_act * pre_act * pre_act)
    tanh_val = jnp.tanh(inner_arg)
    return 0.5 * (1.0 + tanh_val) + 0.5 * pre_act * (1.0 - tanh_val * tanh_val) * coef_c * (
        1.0 + 3.0 * coef_a * pre_act * pre_act
    )


def adam_step(weight_grad, first_moment, second_moment):
    first_new = beta_one * first_moment + (1.0 - beta_one) * weight_grad
    second_new = beta_two * second_moment + (1.0 - beta_two) * weight_grad * weight_grad
    return (
        first_new
        / (1.0 - beta_one**ADAM_STEP)
        / (jnp.sqrt(second_new / (1.0 - beta_two**ADAM_STEP)) + adam_eps)
    ).astype(bf16)


def pack_kernel(expert_count, capacity, ids_ref, gates_ref, x_ref, g_ref, rows_ref, where_ref):
    tok_count, width = x_ref.shape
    slots = expert_count * capacity
    first = ids_ref[0:1, :]
    second = ids_ref[1:2, :]
    experts = lax.broadcasted_iota(jnp.int32, (expert_count, tok_count), 0)
    hit_first = experts == first
    hit_second = experts == second
    hits = jnp.where(hit_first | hit_second, 1.0, 0.0).astype(bf16)
    earlier = lax.broadcasted_iota(jnp.int32, (tok_count, tok_count), 0)
    later = lax.broadcasted_iota(jnp.int32, (tok_count, tok_count), 1)
    upper = jnp.where(earlier < later, 1.0, 0.0).astype(bf16)
    before = mxu(hits, upper, NN)
    slot_first = jnp.sum(jnp.where(hit_first, before, 0.0), axis=0, keepdims=True)
    slot_second = jnp.sum(jnp.where(hit_second, before, 0.0), axis=0, keepdims=True)
    pos_first = first * capacity + slot_first.astype(jnp.int32)
    pos_second = second * capacity + slot_second.astype(jnp.int32)
    where_ref[0:1, :] = pos_first
    where_ref[1:2, :] = pos_second
    row = lax.broadcasted_iota(jnp.int32, (slots, tok_count), 0)
    at_first = row == pos_first
    at_second = row == pos_second
    pick = jnp.where(at_first | at_second, 1.0, 0.0).astype(bf16)
    gate = jnp.sum(
        jnp.where(at_first, gates_ref[0:1, :], 0.0) + jnp.where(at_second, gates_ref[1:2, :], 0.0),
        axis=1,
        keepdims=True,
    )
    rows_ref[:, :width] = mxu(pick, x_ref[...], NN).astype(bf16)
    rows_ref[:, width:] = (gate * mxu(pick, g_ref[...], NN)).astype(bf16)


def pack_rows(id_rows, gate_rows, tokens, out_grad, expert_count, capacity):
    tok_count, width = tokens.shape
    slots = expert_count * capacity
    return pl.pallas_call(
        functools.partial(pack_kernel, expert_count, capacity),
        out_shape=(
            jax.ShapeDtypeStruct((slots, 2 * width), bf16),
            jax.ShapeDtypeStruct((2, tok_count), jnp.int32),
        ),
        name="pack_rows",
    )(id_rows, gate_rows, tokens, out_grad)


def pre_tile(rows, w_in, w_out, pre_ref):
    per, width = rows[0].shape[0], rows[0].shape[1] // 2
    for b, block in enumerate(rows):
        pre_act = mxu(block[:, :width], w_in, NN)
        act_grad = mxu(block[:, width:], w_out, NT)
        pre_ref[b * per : (b + 1) * per, :] = (act_grad * gelu_slope(pre_act)).astype(bf16)


def first_kernel(blocks, *refs):
    rows = refs[:blocks]
    w_in_ref, w_out_ref, m_ref, v_ref, adam_ref, pre_ref, xt_ref = refs[blocks:]
    width, per = m_ref.shape[0], rows[0].shape[0]
    for b in range(blocks):
        xt_ref[:, b * per : (b + 1) * per] = rows[b][:, :width].T
    pre_tile(rows, w_in_ref[...], w_out_ref[...], pre_ref)
    weight_grad = mxu(xt_ref[...], pre_ref[...], NN)
    adam_ref[...] = adam_step(weight_grad, m_ref[...], v_ref[...])


def first_step(rows, w_in, w_out, first_moment, second_moment, tile):
    per, width = rows[0].shape[0], rows[0].shape[1] // 2
    total = len(rows) * per
    corner = lambda i: (0, 0)
    columns = pl.BlockSpec((width, tile), corner)
    return pl.pallas_call(
        functools.partial(first_kernel, len(rows)),
        grid=(1,),
        in_specs=[pl.BlockSpec(r.shape, corner) for r in rows]
        + [columns, pl.BlockSpec((tile, width), corner), columns, columns],
        out_specs=[
            columns,
            pl.BlockSpec((total, tile), corner),
            pl.BlockSpec((width, total), corner),
        ],
        out_shape=[
            jax.ShapeDtypeStruct((width, tile), bf16),
            jax.ShapeDtypeStruct((total, tile), bf16),
            jax.ShapeDtypeStruct((width, total), bf16),
        ],
        compiler_params=pltpu.CompilerParams(vmem_limit_bytes=56 * MIB),
        cost_estimate=pl.CostEstimate(
            flops=6 * total * width * tile, bytes_accessed=14 * tile * width, transcendentals=0
        ),
        name="first_step",
    )(*rows, w_in, w_out, first_moment, second_moment)


def rest_kernel(blocks, *refs):
    rows = refs[:blocks]
    first_ref, w_first_ref, w_in_ref, w_out_ref, pre_ref = refs[blocks : blocks + 5]
    parts = refs[blocks + 5 : -1]
    total_ref = refs[-1]
    per = rows[0].shape[0]
    step = pl.program_id(0)

    @pl.when(step == 0)
    def _():
        total_ref[...] = mxu(first_ref[...], w_first_ref[...], NT)

    pre_tile(rows, w_in_ref[...], w_out_ref[...], pre_ref)
    total_ref[...] += mxu(pre_ref[...], w_in_ref[...], NT)

    @pl.when(step == pl.num_programs(0) - 1)
    def _():
        for b in range(blocks):
            parts[b][...] = total_ref[b * per : (b + 1) * per, :].astype(bf16)


def rest_step(rows, pre_first, w_in, w_out, tile):
    per, width = rows[0].shape[0], rows[0].shape[1] // 2
    total = len(rows) * per
    tiles = w_in.shape[1] // tile - 1
    corner = lambda j: (0, 0)
    return pl.pallas_call(
        functools.partial(rest_kernel, len(rows)),
        grid=(tiles,),
        in_specs=[pl.BlockSpec(r.shape, corner) for r in rows]
        + [
            pl.BlockSpec((total, tile), corner),
            pl.BlockSpec((width, tile), corner),
            pl.BlockSpec((width, tile), lambda j: (0, j + 1)),
            pl.BlockSpec((tile, width), lambda j: (j + 1, 0)),
        ],
        out_specs=[pl.BlockSpec((total, tile), lambda j: (0, j))]
        + [pl.BlockSpec((per, width), corner) for _ in rows],
        out_shape=[jax.ShapeDtypeStruct((total, tiles * tile), bf16)]
        + [jax.ShapeDtypeStruct((per, width), bf16) for _ in rows],
        scratch_shapes=[pltpu.VMEM((total, width), f32)],
        compiler_params=pltpu.CompilerParams(vmem_limit_bytes=56 * MIB),
        cost_estimate=pl.CostEstimate(
            flops=6 * total * width * tile * tiles,
            bytes_accessed=4 * tile * width * tiles,
            transcendentals=0,
        ),
        name="rest_step",
    )(*rows, pre_first, w_in, w_in, w_out)


def adam_kernel(xt_ref, pre_ref, m_ref, v_ref, out_ref):
    weight_grad = mxu(xt_ref[...], pre_ref[...], NN)
    out_ref[...] = adam_step(weight_grad, m_ref[...], v_ref[...])


def adam_block(x_t, pre_rest, first_moment, second_moment, start, tiles, tile, part, parts):
    width, total = x_t.shape
    rows = width // parts
    block = pl.BlockSpec((rows, tile), lambda j: (part, start + j))
    return pl.pallas_call(
        adam_kernel,
        grid=(tiles,),
        in_specs=[
            pl.BlockSpec((rows, total), lambda j: (part, 0)),
            pl.BlockSpec((total, tile), lambda j: (0, start - 1 + j)),
            block,
            block,
        ],
        out_specs=pl.BlockSpec((rows, tile), lambda j: (0, j)),
        out_shape=jax.ShapeDtypeStruct((rows, tiles * tile), bf16),
        compiler_params=pltpu.CompilerParams(vmem_limit_bytes=60 * MIB),
        cost_estimate=pl.CostEstimate(
            flops=2 * total * rows * tile * tiles,
            bytes_accessed=10 * tile * rows * tiles,
            transcendentals=0,
        ),
    )(x_t, pre_rest, first_moment, second_moment)


def place_kernel(boxes, source_ref, *refs):
    sources, at = [], 0
    for box in boxes:
        sources.append(refs[at : at + box[4]])
        at += box[4]
    out_ref = refs[at]
    bufs = refs[at + 1 : at + 1 + len(boxes)]
    in_sem, out_sem = refs[at + 1 + len(boxes) :]
    for n, arrays in enumerate(sources):
        for k, array in enumerate(arrays):
            last = k == len(arrays) - 1
            wanted = source_ref[0] >= k if last else source_ref[0] == k

            @pl.when(wanted)
            def _(n=n, array=array):
                pltpu.make_async_copy(array, bufs[n], in_sem.at[n]).start()

    puts = []
    for n, (row, col, high, wide, _) in enumerate(boxes):
        pltpu.make_async_copy(sources[n][0], bufs[n], in_sem.at[n]).wait()
        put = pltpu.make_async_copy(
            bufs[n], out_ref.at[pl.ds(row, high), pl.ds(col, wide)], out_sem.at[n]
        )
        put.start()
        puts.append(put)
    for put in puts:
        put.wait()


def place(source, pieces, width, inner):
    boxes = [piece[:4] + (len(piece[4]),) for piece in pieces]
    args = [array for piece in pieces for array in piece[4]]
    return pl.pallas_call(
        functools.partial(place_kernel, boxes),
        in_specs=[pl.BlockSpec(memory_space=pltpu.SMEM)]
        + [pl.BlockSpec(memory_space=pl.ANY) for _ in args],
        out_specs=pl.BlockSpec(memory_space=pl.ANY),
        out_shape=jax.ShapeDtypeStruct((width, inner), bf16),
        scratch_shapes=[pltpu.VMEM((box[2], box[3]), bf16) for box in boxes]
        + [pltpu.SemaphoreType.DMA((len(boxes),)), pltpu.SemaphoreType.DMA((len(boxes),))],
        compiler_params=pltpu.CompilerParams(vmem_limit_bytes=8 * MIB),
        cost_estimate=pl.CostEstimate(
            flops=0, bytes_accessed=4 * width * inner, transcendentals=0
        ),
        name="place",
    )(source, *args)


def swap_plans(half):
    line = half >> 1
    groups = {}
    for e in range(half):
        groups.setdefault(e & ~(line | 1), []).append(e)
    groups = list(groups.values())
    if half < 4 or len(groups) > 2:
        return []
    forced = {0, half - 1}
    switches = []
    for members in groups:
        must = forced & set(members)
        plans = [
            set(s)
            for k in range(2, len(members) + 1)
            for s in itertools.combinations(members, k)
            if must <= set(s)
        ]
        table = []
        for mask in range(1 << half):
            moved = must | {e for e in members if mask >> e & 1}
            table.append(next(n for n, plan in enumerate(plans) if moved <= plan))
        switches.append((plans, table))
    return switches


def combine_kernel(capacity, half, upper_ref, where_ref, mirror_ref, back_ref, own_ref, sum_ref):
    slots, tok_count = back_ref.shape[0], own_ref.shape[0]
    row = lax.broadcasted_iota(jnp.int32, (slots, tok_count), 0).astype(f32)
    block = jnp.floor((row + 0.5) * (1.0 / capacity))
    expert = jnp.floor(block * 0.5)
    side = block - 2.0 * expert
    upper = upper_ref[0].astype(f32)
    place_of = (expert + half * upper) * capacity + (row - block * capacity)
    for ref, out, wanted in ((where_ref, own_ref, upper), (mirror_ref, sum_ref, 1.0 - upper)):
        first, second = ref[0:1, :].astype(f32), ref[1:2, :].astype(f32)
        hit = ((place_of == first) | (place_of == second)) & (side == wanted)
        pick = jnp.where(hit, 1.0, 0.0).astype(bf16)
        out[...] = mxu(pick, back_ref[...], TN).astype(out.dtype)


def combine_rows(upper, where_to, mirror_to, returned, tok_count, capacity, half):
    width = returned.shape[1]
    vmem = pl.BlockSpec(memory_space=pltpu.VMEM)
    return pl.pallas_call(
        functools.partial(combine_kernel, capacity, half),
        in_specs=[pl.BlockSpec(memory_space=pltpu.SMEM), vmem, vmem, vmem],
        out_shape=(
            jax.ShapeDtypeStruct((tok_count, width), f32),
            jax.ShapeDtypeStruct((tok_count, width), bf16),
        ),
        cost_estimate=pl.CostEstimate(
            flops=4 * tok_count * returned.shape[0] * width,
            bytes_accessed=2 * returned.size + 6 * tok_count * width,
            transcendentals=0,
        ),
        name="combine_rows",
    )(upper, where_to, mirror_to, returned)


def dp_shift(block, apart):
    count = lax.axis_size("dp")
    return lax.ppermute(block, "dp", [(i, i ^ apart) for i in range(count)])


def shards(
    tokens, out_grad, gates, expert_ids, swap_list, w_in, w_out, first_moment, second_moment
):
    expert_count = lax.axis_size("expert")
    dp_count = lax.axis_size("dp")
    half = 1 << (expert_count.bit_length() - 2)
    own_index = lax.axis_index("expert")
    lane_ids = jnp.arange(expert_count, dtype=jnp.int32)
    partner_me = jnp.sum(jnp.where(lane_ids == own_index, swap_list, 0))
    is_moved = (partner_me != own_index).astype(jnp.int32)
    moved_bits = jnp.where((swap_list != lane_ids) & (lane_ids < half), 1 << lane_ids, 0)
    moved_mask = jnp.sum(moved_bits)
    tok_count, width = tokens.shape
    capacity = 3 * tok_count // expert_count
    slots = expert_count * capacity

    rows, where_to = pack_rows(expert_ids.T, gates.T, tokens, out_grad, expert_count, capacity)
    own = lax.all_to_all(
        rows.reshape(expert_count, capacity, 2 * width),
        "expert",
        split_axis=0,
        concat_axis=0,
        tiled=True,
    ).reshape(slots, 2 * width)
    all_rows = [own] + [dp_shift(own, d) for d in range(1, dp_count)]

    inner = w_in.shape[2]
    tile = 256 if inner % 256 == 0 else 128
    tiles = inner // tile
    route = [(e, e ^ half) for e in range(expert_count)]
    across = [(e, e ^ 1) for e in range(expert_count)]

    first, pre_first, x_t = first_step(
        all_rows, w_in[0], w_out[0], first_moment[0], second_moment[0], tile
    )
    first_got = lax.ppermute(first, "expert", route)
    pieces = [(0, 0, width, tile, [first, first_got])]

    pre_rest, *parts = rest_step(all_rows, pre_first, w_in[0], w_out[0], tile)
    total = parts[0].astype(f32)
    for d in range(1, dp_count):
        total = total + dp_shift(parts[d], d).astype(f32)
    total = total.astype(bf16).reshape(2, half, capacity, width).transpose(1, 0, 2, 3)
    returned = lax.all_to_all(
        total.reshape(half, 2 * capacity, width),
        "expert",
        split_axis=0,
        concat_axis=0,
        axis_index_groups=[list(range(half)), list(range(half, expert_count))],
        tiled=True,
    ).reshape(slots, width)
    upper = (own_index >= half).astype(jnp.int32).reshape(1)
    mirror_to = lax.ppermute(where_to, "expert", route)
    own_sum, mirror_sum = combine_rows(
        upper, where_to, mirror_to, returned, tok_count, capacity, half
    )
    x_grad = (own_sum + lax.ppermute(mirror_sum, "expert", route).astype(f32)).astype(bf16)
    switches = swap_plans(half) if tiles > 2 else []
    direct = 1 if switches else tiles - 1
    moments = (first_moment[0], second_moment[0])
    second = adam_block(x_t, pre_rest, *moments, 1, direct, tile, 0, 1)
    second_got = lax.ppermute(second, "expert", route)
    pieces.append((0, tile, width, direct * tile, [second, second_got]))
    group = jnp.zeros((), jnp.int32)

    if switches:
        at, left = 1 + direct, tiles - 1 - direct
        far = adam_block(x_t, pre_rest, *moments, at, left, tile, 1, 2)
        lent = lax.ppermute(far, "expert", across)
        near = adam_block(x_t, pre_rest, *moments, at, left, tile, 0, 2)

        def branch(plan):
            pairs = [(e, e ^ half) for p in plan for e in (p, p ^ half)]
            skew = [(e ^ 1, f) for e, f in pairs]

            def run(near, lent):
                return (
                    lax.ppermute(near, "expert", pairs),
                    lax.ppermute(lent, "expert", skew),
                )

            return run

        near, lent, x_grad = lax.optimization_barrier((near, lent, x_grad))
        near_all, far_all = [near], [far]
        for n, (plans, table) in enumerate(switches):
            choice = jnp.asarray(table, jnp.int32)[moved_mask]
            near_got, far_got = lax.switch(choice, [branch(p) for p in plans], near, lent)
            near_all.append(near_got)
            far_all.append(far_got)
            members = {e for plan in plans for p in plan for e in (p, p ^ half)}
            here = jnp.asarray([e in members for e in range(expert_count)])
            group += jnp.sum(jnp.where(here & (lane_ids == own_index), n, 0))
        wide = left * tile
        pieces.append((0, at * tile, width // 2, wide, near_all))
        pieces.append((width // 2, at * tile, width // 2, wide, far_all))

    source = (is_moved * (1 + group)).reshape(1)
    adam_out = place(source, pieces, width, inner)
    return (x_grad, adam_out[None])


def solution(mesh):
    in_specs = (
        P(("dp", "expert"), None),
        P(("dp", "expert"), None),
        P(("dp", "expert"), None),
        P(("dp", "expert"), None),
        P(),
        P("expert", None, "dp"),
        P("expert", "dp", None),
        P("expert", None, "dp"),
        P("expert", None, "dp"),
    )
    out_specs = (P(("dp", "expert"), None), P("expert", None, "dp"))

    return jax.shard_map(shards, mesh=mesh, in_specs=in_specs, out_specs=out_specs, check_vma=False)
```

```python
import functools
import itertools

import jax
import jax.numpy as jnp
from jax import lax
from jax.experimental import pallas as pl
from jax.experimental.pallas import tpu as pltpu
from jax.sharding import PartitionSpec as P


ADAM_STEP = 100


coef_c = 0.7978845608028654
coef_a = 0.044715
beta_one = 0.9
beta_two = 0.999
adam_eps = 1e-08


MIB = 2**20

f32 = jnp.float32
bf16 = jnp.bfloat16
NN = (((1,), (0,)), ((), ()))
NT = (((1,), (1,)), ((), ()))
TN = (((0,), (0,)), ((), ()))


def mxu(a, b, dims):
    return lax.dot_general(a, b, dims, preferred_element_type=f32)


def gelu_slope(pre_act):
    inner_arg = coef_c * (pre_act + coef_a * pre_act * pre_act * pre_act)
    tanh_val = jnp.tanh(inner_arg)
    return 0.5 * (1.0 + tanh_val) + 0.5 * pre_act * (1.0 - tanh_val * tanh_val) * coef_c * (
        1.0 + 3.0 * coef_a * pre_act * pre_act
    )


def adam_step(weight_grad, first_moment, second_moment):
    first_new = beta_one * first_moment + (1.0 - beta_one) * weight_grad
    second_new = beta_two * second_moment + (1.0 - beta_two) * weight_grad * weight_grad
    return (
        first_new
        / (1.0 - beta_one**ADAM_STEP)
        / (jnp.sqrt(second_new / (1.0 - beta_two**ADAM_STEP)) + adam_eps)
    ).astype(bf16)


def pack_kernel(expert_count, capacity, ids_ref, gates_ref, x_ref, g_ref, rows_ref, where_ref):
    tok_count, width = x_ref.shape
    slots = expert_count * capacity
    first = ids_ref[0:1, :]
    second = ids_ref[1:2, :]
    experts = lax.broadcasted_iota(jnp.int32, (expert_count, tok_count), 0)
    hit_first = experts == first
    hit_second = experts == second
    hits = jnp.where(hit_first | hit_second, 1.0, 0.0).astype(bf16)
    earlier = lax.broadcasted_iota(jnp.int32, (tok_count, tok_count), 0)
    later = lax.broadcasted_iota(jnp.int32, (tok_count, tok_count), 1)
    upper = jnp.where(earlier < later, 1.0, 0.0).astype(bf16)
    before = mxu(hits, upper, NN)
    slot_first = jnp.sum(jnp.where(hit_first, before, 0.0), axis=0, keepdims=True)
    slot_second = jnp.sum(jnp.where(hit_second, before, 0.0), axis=0, keepdims=True)
    pos_first = first * capacity + slot_first.astype(jnp.int32)
    pos_second = second * capacity + slot_second.astype(jnp.int32)
    where_ref[0:1, :] = pos_first
    where_ref[1:2, :] = pos_second
    row = lax.broadcasted_iota(jnp.int32, (slots, tok_count), 0)
    at_first = row == pos_first
    at_second = row == pos_second
    pick = jnp.where(at_first | at_second, 1.0, 0.0).astype(bf16)
    gate = jnp.sum(
        jnp.where(at_first, gates_ref[0:1, :], 0.0) + jnp.where(at_second, gates_ref[1:2, :], 0.0),
        axis=1,
        keepdims=True,
    )
    rows_ref[:, :width] = mxu(pick, x_ref[...], NN).astype(bf16)
    rows_ref[:, width:] = (gate * mxu(pick, g_ref[...], NN)).astype(bf16)


def pack_rows(id_rows, gate_rows, tokens, out_grad, expert_count, capacity):
    tok_count, width = tokens.shape
    slots = expert_count * capacity
    return pl.pallas_call(
        functools.partial(pack_kernel, expert_count, capacity),
        out_shape=(
            jax.ShapeDtypeStruct((slots, 2 * width), bf16),
            jax.ShapeDtypeStruct((2, tok_count), jnp.int32),
        ),
        name="pack_rows",
    )(id_rows, gate_rows, tokens, out_grad)


def pre_tile(rows, w_in, w_out, pre_ref):
    per, width = rows[0].shape[0], rows[0].shape[1] // 2
    for b, block in enumerate(rows):
        pre_act = mxu(block[:, :width], w_in, NN)
        act_grad = mxu(block[:, width:], w_out, NT)
        pre_ref[b * per : (b + 1) * per, :] = (act_grad * gelu_slope(pre_act)).astype(bf16)


def first_kernel(blocks, *refs):
    rows = refs[:blocks]
    w_in_ref, w_out_ref, m_ref, v_ref, adam_ref, pre_ref, xt_ref = refs[blocks:]
    width, per = m_ref.shape[0], rows[0].shape[0]
    for b in range(blocks):
        xt_ref[:, b * per : (b + 1) * per] = rows[b][:, :width].T
    pre_tile(rows, w_in_ref[...], w_out_ref[...], pre_ref)
    weight_grad = mxu(xt_ref[...], pre_ref[...], NN)
    adam_ref[...] = adam_step(weight_grad, m_ref[...], v_ref[...])


def first_step(rows, w_in, w_out, first_moment, second_moment, tile):
    per, width = rows[0].shape[0], rows[0].shape[1] // 2
    total = len(rows) * per
    corner = lambda i: (0, 0)
    columns = pl.BlockSpec((width, tile), corner)
    return pl.pallas_call(
        functools.partial(first_kernel, len(rows)),
        grid=(1,),
        in_specs=[pl.BlockSpec(r.shape, corner) for r in rows]
        + [columns, pl.BlockSpec((tile, width), corner), columns, columns],
        out_specs=[
            columns,
            pl.BlockSpec((total, tile), corner),
            pl.BlockSpec((width, total), corner),
        ],
        out_shape=[
            jax.ShapeDtypeStruct((width, tile), bf16),
            jax.ShapeDtypeStruct((total, tile), bf16),
            jax.ShapeDtypeStruct((width, total), bf16),
        ],
        compiler_params=pltpu.CompilerParams(vmem_limit_bytes=56 * MIB),
        cost_estimate=pl.CostEstimate(
            flops=6 * total * width * tile, bytes_accessed=14 * tile * width, transcendentals=0
        ),
        name="first_step",
    )(*rows, w_in, w_out, first_moment, second_moment)


def rest_kernel(blocks, *refs):
    rows = refs[:blocks]
    first_ref, w_first_ref, w_in_ref, w_out_ref, pre_ref = refs[blocks : blocks + 5]
    parts = refs[blocks + 5 : -1]
    total_ref = refs[-1]
    per = rows[0].shape[0]
    step = pl.program_id(0)

    @pl.when(step == 0)
    def _():
        total_ref[...] = mxu(first_ref[...], w_first_ref[...], NT)

    pre_tile(rows, w_in_ref[...], w_out_ref[...], pre_ref)
    total_ref[...] += mxu(pre_ref[...], w_in_ref[...], NT)

    @pl.when(step == pl.num_programs(0) - 1)
    def _():
        for b in range(blocks):
            parts[b][...] = total_ref[b * per : (b + 1) * per, :].astype(bf16)


def rest_step(rows, pre_first, w_in, w_out, tile):
    per, width = rows[0].shape[0], rows[0].shape[1] // 2
    total = len(rows) * per
    tiles = w_in.shape[1] // tile - 1
    corner = lambda j: (0, 0)
    return pl.pallas_call(
        functools.partial(rest_kernel, len(rows)),
        grid=(tiles,),
        in_specs=[pl.BlockSpec(r.shape, corner) for r in rows]
        + [
            pl.BlockSpec((total, tile), corner),
            pl.BlockSpec((width, tile), corner),
            pl.BlockSpec((width, tile), lambda j: (0, j + 1)),
            pl.BlockSpec((tile, width), lambda j: (j + 1, 0)),
        ],
        out_specs=[pl.BlockSpec((total, tile), lambda j: (0, j))]
        + [pl.BlockSpec((per, width), corner) for _ in rows],
        out_shape=[jax.ShapeDtypeStruct((total, tiles * tile), bf16)]
        + [jax.ShapeDtypeStruct((per, width), bf16) for _ in rows],
        scratch_shapes=[pltpu.VMEM((total, width), f32)],
        compiler_params=pltpu.CompilerParams(vmem_limit_bytes=56 * MIB),
        cost_estimate=pl.CostEstimate(
            flops=6 * total * width * tile * tiles,
            bytes_accessed=4 * tile * width * tiles,
            transcendentals=0,
        ),
        name="rest_step",
    )(*rows, pre_first, w_in, w_in, w_out)


def adam_kernel(xt_ref, pre_ref, m_ref, v_ref, out_ref):
    weight_grad = mxu(xt_ref[...], pre_ref[...], NN)
    out_ref[...] = adam_step(weight_grad, m_ref[...], v_ref[...])


def adam_block(x_t, pre_rest, first_moment, second_moment, start, tiles, tile, part, parts):
    width, total = x_t.shape
    rows = width // parts
    block = pl.BlockSpec((rows, tile), lambda j: (part, start + j))
    return pl.pallas_call(
        adam_kernel,
        grid=(tiles,),
        in_specs=[
            pl.BlockSpec((rows, total), lambda j: (part, 0)),
            pl.BlockSpec((total, tile), lambda j: (0, start - 1 + j)),
            block,
            block,
        ],
        out_specs=pl.BlockSpec((rows, tile), lambda j: (0, j)),
        out_shape=jax.ShapeDtypeStruct((rows, tiles * tile), bf16),
        compiler_params=pltpu.CompilerParams(vmem_limit_bytes=60 * MIB),
        cost_estimate=pl.CostEstimate(
            flops=2 * total * rows * tile * tiles,
            bytes_accessed=10 * tile * rows * tiles,
            transcendentals=0,
        ),
    )(x_t, pre_rest, first_moment, second_moment)


def place_kernel(boxes, source_ref, own_ref, other_ref, *refs):
    sources, at = [], 0
    for box in boxes:
        sources.append(refs[at : at + box[4]])
        at += box[4]
    out_ref, sum_ref = refs[at : at + 2]
    bufs = refs[at + 2 : at + 2 + len(boxes)]
    in_sem, out_sem = refs[at + 2 + len(boxes) :]
    for n, arrays in enumerate(sources):
        for k, array in enumerate(arrays):
            last = k == len(arrays) - 1
            wanted = source_ref[0] >= k if last else source_ref[0] == k

            @pl.when(wanted)
            def _(n=n, array=array):
                pltpu.make_async_copy(array, bufs[n], in_sem.at[n]).start()

    sum_ref[...] = (own_ref[...] + other_ref[...].astype(f32)).astype(bf16)
    puts = []
    for n, (row, col, high, wide, _) in enumerate(boxes):
        pltpu.make_async_copy(sources[n][0], bufs[n], in_sem.at[n]).wait()
        put = pltpu.make_async_copy(
            bufs[n], out_ref.at[pl.ds(row, high), pl.ds(col, wide)], out_sem.at[n]
        )
        put.start()
        puts.append(put)
    for put in puts:
        put.wait()


def place(source, own_sum, other_sum, pieces, width, inner):
    boxes = [piece[:4] + (len(piece[4]),) for piece in pieces]
    args = [array for piece in pieces for array in piece[4]]
    return pl.pallas_call(
        functools.partial(place_kernel, boxes),
        in_specs=[pl.BlockSpec(memory_space=pltpu.SMEM)]
        + [pl.BlockSpec(memory_space=pltpu.VMEM)] * 2
        + [pl.BlockSpec(memory_space=pl.ANY) for _ in args],
        out_specs=[pl.BlockSpec(memory_space=pl.ANY), pl.BlockSpec(memory_space=pltpu.VMEM)],
        out_shape=[
            jax.ShapeDtypeStruct((width, inner), bf16),
            jax.ShapeDtypeStruct(own_sum.shape, bf16),
        ],
        scratch_shapes=[pltpu.VMEM((box[2], box[3]), bf16) for box in boxes]
        + [pltpu.SemaphoreType.DMA((len(boxes),)), pltpu.SemaphoreType.DMA((len(boxes),))],
        compiler_params=pltpu.CompilerParams(vmem_limit_bytes=8 * MIB),
        cost_estimate=pl.CostEstimate(
            flops=0, bytes_accessed=4 * width * inner, transcendentals=0
        ),
        name="place",
    )(source, own_sum, other_sum, *args)


def swap_plans(half):
    line = half >> 1
    groups = {}
    for e in range(half):
        groups.setdefault(e & ~(line | 1), []).append(e)
    groups = list(groups.values())
    if half < 4 or len(groups) > 2:
        return []
    forced = {0, half - 1}
    switches = []
    for members in groups:
        must = forced & set(members)
        plans = [
            set(s)
            for k in range(2, len(members) + 1)
            for s in itertools.combinations(members, k)
            if must <= set(s)
        ]
        table = []
        for mask in range(1 << half):
            moved = must | {e for e in members if mask >> e & 1}
            table.append(next(n for n, plan in enumerate(plans) if moved <= plan))
        switches.append((plans, table))
    return switches


def combine_kernel(capacity, half, upper_ref, where_ref, mirror_ref, back_ref, own_ref, sum_ref):
    slots, tok_count = back_ref.shape[0], own_ref.shape[0]
    row = lax.broadcasted_iota(jnp.int32, (slots, tok_count), 0).astype(f32)
    block = jnp.floor((row + 0.5) * (1.0 / capacity))
    expert = jnp.floor(block * 0.5)
    side = block - 2.0 * expert
    upper = upper_ref[0].astype(f32)
    place_of = (expert + half * upper) * capacity + (row - block * capacity)
    for ref, out, wanted in ((where_ref, own_ref, upper), (mirror_ref, sum_ref, 1.0 - upper)):
        first, second = ref[0:1, :].astype(f32), ref[1:2, :].astype(f32)
        hit = ((place_of == first) | (place_of == second)) & (side == wanted)
        pick = jnp.where(hit, 1.0, 0.0).astype(bf16)
        out[...] = mxu(pick, back_ref[...], TN).astype(out.dtype)


def combine_rows(upper, where_to, mirror_to, returned, tok_count, capacity, half):
    width = returned.shape[1]
    vmem = pl.BlockSpec(memory_space=pltpu.VMEM)
    return pl.pallas_call(
        functools.partial(combine_kernel, capacity, half),
        in_specs=[pl.BlockSpec(memory_space=pltpu.SMEM), vmem, vmem, vmem],
        out_shape=(
            jax.ShapeDtypeStruct((tok_count, width), f32),
            jax.ShapeDtypeStruct((tok_count, width), bf16),
        ),
        cost_estimate=pl.CostEstimate(
            flops=4 * tok_count * returned.shape[0] * width,
            bytes_accessed=2 * returned.size + 6 * tok_count * width,
            transcendentals=0,
        ),
        name="combine_rows",
    )(upper, where_to, mirror_to, returned)


def dp_shift(block, apart):
    count = lax.axis_size("dp")
    return lax.ppermute(block, "dp", [(i, i ^ apart) for i in range(count)])


def shards(
    tokens, out_grad, gates, expert_ids, swap_list, w_in, w_out, first_moment, second_moment
):
    expert_count = lax.axis_size("expert")
    dp_count = lax.axis_size("dp")
    half = 1 << (expert_count.bit_length() - 2)
    own_index = lax.axis_index("expert")
    lane_ids = jnp.arange(expert_count, dtype=jnp.int32)
    partner_me = jnp.sum(jnp.where(lane_ids == own_index, swap_list, 0))
    is_moved = (partner_me != own_index).astype(jnp.int32)
    moved_bits = jnp.where((swap_list != lane_ids) & (lane_ids < half), 1 << lane_ids, 0)
    moved_mask = jnp.sum(moved_bits)
    tok_count, width = tokens.shape
    capacity = 3 * tok_count // expert_count
    slots = expert_count * capacity

    rows, where_to = pack_rows(expert_ids.T, gates.T, tokens, out_grad, expert_count, capacity)
    own = lax.all_to_all(
        rows.reshape(expert_count, capacity, 2 * width),
        "expert",
        split_axis=0,
        concat_axis=0,
        tiled=True,
    ).reshape(slots, 2 * width)
    all_rows = [own] + [dp_shift(own, d) for d in range(1, dp_count)]

    inner = w_in.shape[2]
    tile = 256 if inner % 256 == 0 else 128
    tiles = inner // tile
    route = [(e, e ^ half) for e in range(expert_count)]
    across = [(e, e ^ 1) for e in range(expert_count)]

    first, pre_first, x_t = first_step(
        all_rows, w_in[0], w_out[0], first_moment[0], second_moment[0], tile
    )
    first_got = lax.ppermute(first, "expert", route)
    pieces = [(0, 0, width, tile, [first, first_got])]

    pre_rest, *parts = rest_step(all_rows, pre_first, w_in[0], w_out[0], tile)
    total = parts[0].astype(f32)
    for d in range(1, dp_count):
        total = total + dp_shift(parts[d], d).astype(f32)
    total = total.astype(bf16).reshape(2, half, capacity, width).transpose(1, 0, 2, 3)
    returned = lax.all_to_all(
        total.reshape(half, 2 * capacity, width),
        "expert",
        split_axis=0,
        concat_axis=0,
        axis_index_groups=[list(range(half)), list(range(half, expert_count))],
        tiled=True,
    ).reshape(slots, width)
    upper = (own_index >= half).astype(jnp.int32).reshape(1)
    mirror_to = lax.ppermute(where_to, "expert", route)
    own_sum, mirror_sum = combine_rows(
        upper, where_to, mirror_to, returned, tok_count, capacity, half
    )
    other_sum = lax.ppermute(mirror_sum, "expert", route)
    switches = swap_plans(half) if tiles > 2 else []
    direct = 1 if switches else tiles - 1
    moments = (first_moment[0], second_moment[0])
    second = adam_block(x_t, pre_rest, *moments, 1, direct, tile, 0, 1)
    second_got = lax.ppermute(second, "expert", route)
    pieces.append((0, tile, width, direct * tile, [second, second_got]))
    group = jnp.zeros((), jnp.int32)

    if switches:
        at, left = 1 + direct, tiles - 1 - direct
        far = adam_block(x_t, pre_rest, *moments, at, left, tile, 1, 2)
        lent = lax.ppermute(far, "expert", across)
        near = adam_block(x_t, pre_rest, *moments, at, left, tile, 0, 2)

        def branch(plan):
            pairs = [(e, e ^ half) for p in plan for e in (p, p ^ half)]
            skew = [(e ^ 1, f) for e, f in pairs]

            def run(near, lent):
                return (
                    lax.ppermute(near, "expert", pairs),
                    lax.ppermute(lent, "expert", skew),
                )

            return run

        choices = [
            lax.dynamic_index_in_dim(jnp.asarray(table, jnp.int32), moved_mask, keepdims=False)
            for _, table in switches
        ]
        near, lent, own_sum = lax.optimization_barrier((near, lent, own_sum))
        near_all, far_all = [near], [far]
        for n, (plans, table) in enumerate(switches):
            near_got, far_got = lax.switch(choices[n], [branch(p) for p in plans], near, lent)
            near_all.append(near_got)
            far_all.append(far_got)
            members = {e for plan in plans for p in plan for e in (p, p ^ half)}
            here = jnp.asarray([e in members for e in range(expert_count)])
            group += jnp.sum(jnp.where(here & (lane_ids == own_index), n, 0))
        wide = left * tile
        pieces.append((0, at * tile, width // 2, wide, near_all))
        pieces.append((width // 2, at * tile, width // 2, wide, far_all))

    source = (is_moved * (1 + group)).reshape(1)
    adam_out, x_grad = place(source, own_sum, other_sum, pieces, width, inner)
    return (x_grad, adam_out[None])


def solution(mesh):
    in_specs = (
        P(("dp", "expert"), None),
        P(("dp", "expert"), None),
        P(("dp", "expert"), None),
        P(("dp", "expert"), None),
        P(),
        P("expert", None, "dp"),
        P("expert", "dp", None),
        P("expert", None, "dp"),
        P("expert", None, "dp"),
    )
    out_specs = (P(("dp", "expert"), None), P("expert", None, "dp"))

    return jax.shard_map(shards, mesh=mesh, in_specs=in_specs, out_specs=out_specs, check_vma=False)
```

```python
import functools
import itertools

import jax
import jax.numpy as jnp
from jax import lax
from jax.experimental import pallas as pl
from jax.experimental.pallas import tpu as pltpu
from jax.sharding import PartitionSpec as P


ADAM_STEP = 100


coef_c = 0.7978845608028654
coef_a = 0.044715
beta_one = 0.9
beta_two = 0.999
adam_eps = 1e-08


MIB = 2**20

f32 = jnp.float32
bf16 = jnp.bfloat16
NN = (((1,), (0,)), ((), ()))
NT = (((1,), (1,)), ((), ()))
TN = (((0,), (0,)), ((), ()))


def mxu(a, b, dims):
    return lax.dot_general(a, b, dims, preferred_element_type=f32)


def gelu_slope(pre_act):
    inner_arg = coef_c * (pre_act + coef_a * pre_act * pre_act * pre_act)
    tanh_val = jnp.tanh(inner_arg)
    return 0.5 * (1.0 + tanh_val) + 0.5 * pre_act * (1.0 - tanh_val * tanh_val) * coef_c * (
        1.0 + 3.0 * coef_a * pre_act * pre_act
    )


def adam_step(weight_grad, first_moment, second_moment):
    first_new = beta_one * first_moment + (1.0 - beta_one) * weight_grad
    second_new = beta_two * second_moment + (1.0 - beta_two) * weight_grad * weight_grad
    return (
        first_new
        / (1.0 - beta_one**ADAM_STEP)
        / (jnp.sqrt(second_new / (1.0 - beta_two**ADAM_STEP)) + adam_eps)
    ).astype(bf16)


def pack_kernel(expert_count, capacity, ids_ref, gates_ref, x_ref, g_ref, rows_ref, where_ref):
    tok_count, width = x_ref.shape
    slots = expert_count * capacity
    first = ids_ref[0:1, :]
    second = ids_ref[1:2, :]
    experts = lax.broadcasted_iota(jnp.int32, (expert_count, tok_count), 0)
    hit_first = experts == first
    hit_second = experts == second
    hits = jnp.where(hit_first | hit_second, 1.0, 0.0).astype(bf16)
    earlier = lax.broadcasted_iota(jnp.int32, (tok_count, tok_count), 0)
    later = lax.broadcasted_iota(jnp.int32, (tok_count, tok_count), 1)
    upper = jnp.where(earlier < later, 1.0, 0.0).astype(bf16)
    before = mxu(hits, upper, NN)
    slot_first = jnp.sum(jnp.where(hit_first, before, 0.0), axis=0, keepdims=True)
    slot_second = jnp.sum(jnp.where(hit_second, before, 0.0), axis=0, keepdims=True)
    pos_first = first * capacity + slot_first.astype(jnp.int32)
    pos_second = second * capacity + slot_second.astype(jnp.int32)
    where_ref[0:1, :] = pos_first
    where_ref[1:2, :] = pos_second
    row = lax.broadcasted_iota(jnp.int32, (slots, tok_count), 0)
    at_first = row == pos_first
    at_second = row == pos_second
    pick = jnp.where(at_first | at_second, 1.0, 0.0).astype(bf16)
    gate = jnp.sum(
        jnp.where(at_first, gates_ref[0:1, :], 0.0) + jnp.where(at_second, gates_ref[1:2, :], 0.0),
        axis=1,
        keepdims=True,
    )
    rows_ref[:, :width] = mxu(pick, x_ref[...], NN).astype(bf16)
    rows_ref[:, width:] = (gate * mxu(pick, g_ref[...], NN)).astype(bf16)


def pack_rows(id_rows, gate_rows, tokens, out_grad, expert_count, capacity):
    tok_count, width = tokens.shape
    slots = expert_count * capacity
    return pl.pallas_call(
        functools.partial(pack_kernel, expert_count, capacity),
        out_shape=(
            jax.ShapeDtypeStruct((slots, 2 * width), bf16),
            jax.ShapeDtypeStruct((2, tok_count), jnp.int32),
        ),
        name="pack_rows",
    )(id_rows, gate_rows, tokens, out_grad)


def pre_tile(rows, w_in, w_out, pre_ref):
    per, width = rows[0].shape[0], rows[0].shape[1] // 2
    for b, block in enumerate(rows):
        pre_act = mxu(block[:, :width], w_in, NN)
        act_grad = mxu(block[:, width:], w_out, NT)
        pre_ref[b * per : (b + 1) * per, :] = (act_grad * gelu_slope(pre_act)).astype(bf16)


def first_kernel(blocks, *refs):
    rows = refs[:blocks]
    w_in_ref, w_out_ref, m_ref, v_ref, adam_ref, pre_ref, xt_ref = refs[blocks:]
    width, per = m_ref.shape[0], rows[0].shape[0]
    for b in range(blocks):
        xt_ref[:, b * per : (b + 1) * per] = rows[b][:, :width].T
    pre_tile(rows, w_in_ref[...], w_out_ref[...], pre_ref)
    weight_grad = mxu(xt_ref[...], pre_ref[...], NN)
    adam_ref[...] = adam_step(weight_grad, m_ref[...], v_ref[...])


def first_step(rows, w_in, w_out, first_moment, second_moment, tile):
    per, width = rows[0].shape[0], rows[0].shape[1] // 2
    total = len(rows) * per
    corner = lambda i: (0, 0)
    columns = pl.BlockSpec((width, tile), corner)
    return pl.pallas_call(
        functools.partial(first_kernel, len(rows)),
        grid=(1,),
        in_specs=[pl.BlockSpec(r.shape, corner) for r in rows]
        + [columns, pl.BlockSpec((tile, width), corner), columns, columns],
        out_specs=[
            columns,
            pl.BlockSpec((total, tile), corner),
            pl.BlockSpec((width, total), corner),
        ],
        out_shape=[
            jax.ShapeDtypeStruct((width, tile), bf16),
            jax.ShapeDtypeStruct((total, tile), bf16),
            jax.ShapeDtypeStruct((width, total), bf16),
        ],
        compiler_params=pltpu.CompilerParams(vmem_limit_bytes=56 * MIB),
        cost_estimate=pl.CostEstimate(
            flops=6 * total * width * tile, bytes_accessed=14 * tile * width, transcendentals=0
        ),
        name="first_step",
    )(*rows, w_in, w_out, first_moment, second_moment)


def rest_kernel(blocks, *refs):
    rows = refs[:blocks]
    first_ref, w_first_ref, w_in_ref, w_out_ref, pre_ref = refs[blocks : blocks + 5]
    parts = refs[blocks + 5 : -1]
    total_ref = refs[-1]
    per = rows[0].shape[0]
    step = pl.program_id(0)

    @pl.when(step == 0)
    def _():
        total_ref[...] = mxu(first_ref[...], w_first_ref[...], NT)

    pre_tile(rows, w_in_ref[...], w_out_ref[...], pre_ref)
    total_ref[...] += mxu(pre_ref[...], w_in_ref[...], NT)

    @pl.when(step == pl.num_programs(0) - 1)
    def _():
        for b in range(blocks):
            parts[b][...] = total_ref[b * per : (b + 1) * per, :].astype(bf16)


def rest_step(rows, pre_first, w_in, w_out, tile):
    per, width = rows[0].shape[0], rows[0].shape[1] // 2
    total = len(rows) * per
    tiles = w_in.shape[1] // tile - 1
    corner = lambda j: (0, 0)
    return pl.pallas_call(
        functools.partial(rest_kernel, len(rows)),
        grid=(tiles,),
        in_specs=[pl.BlockSpec(r.shape, corner) for r in rows]
        + [
            pl.BlockSpec((total, tile), corner),
            pl.BlockSpec((width, tile), corner),
            pl.BlockSpec((width, tile), lambda j: (0, j + 1)),
            pl.BlockSpec((tile, width), lambda j: (j + 1, 0)),
        ],
        out_specs=[pl.BlockSpec((total, tile), lambda j: (0, j))]
        + [pl.BlockSpec((per, width), corner) for _ in rows],
        out_shape=[jax.ShapeDtypeStruct((total, tiles * tile), bf16)]
        + [jax.ShapeDtypeStruct((per, width), bf16) for _ in rows],
        scratch_shapes=[pltpu.VMEM((total, width), f32)],
        compiler_params=pltpu.CompilerParams(vmem_limit_bytes=56 * MIB),
        cost_estimate=pl.CostEstimate(
            flops=6 * total * width * tile * tiles,
            bytes_accessed=4 * tile * width * tiles,
            transcendentals=0,
        ),
        name="rest_step",
    )(*rows, pre_first, w_in, w_in, w_out)


def adam_kernel(xt_ref, pre_ref, m_ref, v_ref, out_ref):
    weight_grad = mxu(xt_ref[...], pre_ref[...], NN)
    out_ref[...] = adam_step(weight_grad, m_ref[...], v_ref[...])


def adam_block(x_t, pre_rest, first_moment, second_moment, start, tiles, tile, part, parts):
    width, total = x_t.shape
    rows = width // parts
    block = pl.BlockSpec((rows, tile), lambda j: (part, start + j))
    return pl.pallas_call(
        adam_kernel,
        grid=(tiles,),
        in_specs=[
            pl.BlockSpec((rows, total), lambda j: (part, 0)),
            pl.BlockSpec((total, tile), lambda j: (0, start - 1 + j)),
            block,
            block,
        ],
        out_specs=pl.BlockSpec((rows, tile), lambda j: (0, j)),
        out_shape=jax.ShapeDtypeStruct((rows, tiles * tile), bf16),
        compiler_params=pltpu.CompilerParams(vmem_limit_bytes=60 * MIB),
        cost_estimate=pl.CostEstimate(
            flops=2 * total * rows * tile * tiles,
            bytes_accessed=10 * tile * rows * tiles,
            transcendentals=0,
        ),
    )(x_t, pre_rest, first_moment, second_moment)


def place_kernel(boxes, source_ref, own_ref, other_ref, *refs):
    sources, at = [], 0
    for box in boxes:
        sources.append(refs[at : at + box[4]])
        at += box[4]
    out_ref, sum_ref = refs[at : at + 2]
    bufs = refs[at + 2 : at + 2 + len(boxes)]
    own_buf, other_buf, sum_buf, in_sem, out_sem = refs[at + 2 + len(boxes) :]
    count = len(boxes)
    for n, arrays in enumerate(sources):
        for k, array in enumerate(arrays):
            last = k == len(arrays) - 1
            wanted = source_ref[0] >= k if last else source_ref[0] == k

            @pl.when(wanted)
            def _(n=n, array=array):
                pltpu.make_async_copy(array, bufs[n], in_sem.at[n]).start()

    pltpu.make_async_copy(own_ref, own_buf, in_sem.at[count]).start()
    pltpu.make_async_copy(other_ref, other_buf, in_sem.at[count + 1]).start()
    puts = []
    for n, (row, col, high, wide, _) in enumerate(boxes):
        pltpu.make_async_copy(sources[n][0], bufs[n], in_sem.at[n]).wait()
        put = pltpu.make_async_copy(
            bufs[n], out_ref.at[pl.ds(row, high), pl.ds(col, wide)], out_sem.at[n]
        )
        put.start()
        puts.append(put)
    pltpu.make_async_copy(own_ref, own_buf, in_sem.at[count]).wait()
    pltpu.make_async_copy(other_ref, other_buf, in_sem.at[count + 1]).wait()
    sum_buf[...] = (own_buf[...].astype(f32) + other_buf[...].astype(f32)).astype(bf16)
    put = pltpu.make_async_copy(sum_buf, sum_ref, out_sem.at[count])
    put.start()
    puts.append(put)
    for put in puts:
        put.wait()


def place(source, own_sum, other_sum, pieces, width, inner):
    boxes = [piece[:4] + (len(piece[4]),) for piece in pieces]
    args = [array for piece in pieces for array in piece[4]]
    return pl.pallas_call(
        functools.partial(place_kernel, boxes),
        in_specs=[pl.BlockSpec(memory_space=pltpu.SMEM)]
        + [pl.BlockSpec(memory_space=pl.ANY)] * (2 + len(args)),
        out_specs=[pl.BlockSpec(memory_space=pl.ANY)] * 2,
        out_shape=[
            jax.ShapeDtypeStruct((width, inner), bf16),
            jax.ShapeDtypeStruct(own_sum.shape, bf16),
        ],
        scratch_shapes=[pltpu.VMEM((box[2], box[3]), bf16) for box in boxes]
        + [pltpu.VMEM(own_sum.shape, bf16)] * 3
        + [pltpu.SemaphoreType.DMA((len(boxes) + 2,)), pltpu.SemaphoreType.DMA((len(boxes) + 1,))],
        compiler_params=pltpu.CompilerParams(vmem_limit_bytes=8 * MIB),
        cost_estimate=pl.CostEstimate(
            flops=0, bytes_accessed=4 * width * inner, transcendentals=0
        ),
        name="place",
    )(source, own_sum, other_sum, *args)


def swap_plans(half):
    line = half >> 1
    groups = {}
    for e in range(half):
        groups.setdefault(e & ~(line | 1), []).append(e)
    groups = list(groups.values())
    if half < 4 or len(groups) > 2:
        return []
    forced = {0, half - 1}
    switches = []
    for members in groups:
        must = forced & set(members)
        plans = [
            set(s)
            for k in range(2, len(members) + 1)
            for s in itertools.combinations(members, k)
            if must <= set(s)
        ]
        table = []
        for mask in range(1 << half):
            moved = must | {e for e in members if mask >> e & 1}
            table.append(next(n for n, plan in enumerate(plans) if moved <= plan))
        switches.append((plans, table))
    return switches


def combine_kernel(capacity, half, upper_ref, where_ref, mirror_ref, back_ref, own_ref, sum_ref):
    slots, tok_count = back_ref.shape[0], own_ref.shape[0]
    row = lax.broadcasted_iota(jnp.int32, (slots, tok_count), 0).astype(f32)
    block = jnp.floor((row + 0.5) * (1.0 / capacity))
    expert = jnp.floor(block * 0.5)
    side = block - 2.0 * expert
    upper = upper_ref[0].astype(f32)
    place_of = (expert + half * upper) * capacity + (row - block * capacity)
    for ref, out, wanted in ((where_ref, own_ref, upper), (mirror_ref, sum_ref, 1.0 - upper)):
        first, second = ref[0:1, :].astype(f32), ref[1:2, :].astype(f32)
        hit = ((place_of == first) | (place_of == second)) & (side == wanted)
        pick = jnp.where(hit, 1.0, 0.0).astype(bf16)
        out[...] = mxu(pick, back_ref[...], TN).astype(out.dtype)


def combine_rows(upper, where_to, mirror_to, returned, tok_count, capacity, half):
    width = returned.shape[1]
    vmem = pl.BlockSpec(memory_space=pltpu.VMEM)
    return pl.pallas_call(
        functools.partial(combine_kernel, capacity, half),
        in_specs=[pl.BlockSpec(memory_space=pltpu.SMEM), vmem, vmem, vmem],
        out_shape=(
            jax.ShapeDtypeStruct((tok_count, width), bf16),
            jax.ShapeDtypeStruct((tok_count, width), bf16),
        ),
        cost_estimate=pl.CostEstimate(
            flops=4 * tok_count * returned.shape[0] * width,
            bytes_accessed=2 * returned.size + 6 * tok_count * width,
            transcendentals=0,
        ),
        name="combine_rows",
    )(upper, where_to, mirror_to, returned)


def dp_shift(block, apart):
    count = lax.axis_size("dp")
    return lax.ppermute(block, "dp", [(i, i ^ apart) for i in range(count)])


def shards(
    tokens, out_grad, gates, expert_ids, swap_list, w_in, w_out, first_moment, second_moment
):
    expert_count = lax.axis_size("expert")
    dp_count = lax.axis_size("dp")
    half = 1 << (expert_count.bit_length() - 2)
    own_index = lax.axis_index("expert")
    lane_ids = jnp.arange(expert_count, dtype=jnp.int32)
    partner_me = jnp.sum(jnp.where(lane_ids == own_index, swap_list, 0))
    is_moved = (partner_me != own_index).astype(jnp.int32)
    moved_bits = jnp.where((swap_list != lane_ids) & (lane_ids < half), 1 << lane_ids, 0)
    moved_mask = jnp.sum(moved_bits)
    tok_count, width = tokens.shape
    capacity = 3 * tok_count // expert_count
    slots = expert_count * capacity

    rows, where_to = pack_rows(expert_ids.T, gates.T, tokens, out_grad, expert_count, capacity)
    own = lax.all_to_all(
        rows.reshape(expert_count, capacity, 2 * width),
        "expert",
        split_axis=0,
        concat_axis=0,
        tiled=True,
    ).reshape(slots, 2 * width)
    all_rows = [own] + [dp_shift(own, d) for d in range(1, dp_count)]

    inner = w_in.shape[2]
    tile = 256 if inner % 256 == 0 else 128
    tiles = inner // tile
    route = [(e, e ^ half) for e in range(expert_count)]
    across = [(e, e ^ 1) for e in range(expert_count)]

    first, pre_first, x_t = first_step(
        all_rows, w_in[0], w_out[0], first_moment[0], second_moment[0], tile
    )
    first_got = lax.ppermute(first, "expert", route)
    pieces = [(0, 0, width, tile, [first, first_got])]

    pre_rest, *parts = rest_step(all_rows, pre_first, w_in[0], w_out[0], tile)
    total = parts[0].astype(f32)
    for d in range(1, dp_count):
        total = total + dp_shift(parts[d], d).astype(f32)
    total = total.astype(bf16).reshape(2, half, capacity, width).transpose(1, 0, 2, 3)
    returned = lax.all_to_all(
        total.reshape(half, 2 * capacity, width),
        "expert",
        split_axis=0,
        concat_axis=0,
        axis_index_groups=[list(range(half)), list(range(half, expert_count))],
        tiled=True,
    ).reshape(slots, width)
    upper = (own_index >= half).astype(jnp.int32).reshape(1)
    mirror_to = lax.ppermute(where_to, "expert", route)
    own_sum, mirror_sum = combine_rows(
        upper, where_to, mirror_to, returned, tok_count, capacity, half
    )
    other_sum = lax.ppermute(mirror_sum, "expert", route)
    switches = swap_plans(half) if tiles > 2 else []
    direct = 1 if switches else tiles - 1
    moments = (first_moment[0], second_moment[0])
    second = adam_block(x_t, pre_rest, *moments, 1, direct, tile, 0, 1)
    second_got = lax.ppermute(second, "expert", route)
    pieces.append((0, tile, width, direct * tile, [second, second_got]))
    group = jnp.zeros((), jnp.int32)

    if switches:
        at, left = 1 + direct, tiles - 1 - direct
        far = adam_block(x_t, pre_rest, *moments, at, left, tile, 1, 2)
        lent = lax.ppermute(far, "expert", across)
        near = adam_block(x_t, pre_rest, *moments, at, left, tile, 0, 2)

        def branch(plan):
            pairs = [(e, e ^ half) for p in plan for e in (p, p ^ half)]
            skew = [(e ^ 1, f) for e, f in pairs]

            def run(near, lent):
                return (
                    lax.ppermute(near, "expert", pairs),
                    lax.ppermute(lent, "expert", skew),
                )

            return run

        choices = [
            lax.dynamic_index_in_dim(jnp.asarray(table, jnp.int32), moved_mask, keepdims=False)
            for _, table in switches
        ]
        near, lent, own_sum = lax.optimization_barrier((near, lent, own_sum))
        near_all, far_all = [near], [far]
        for n, (plans, table) in enumerate(switches):
            near_got, far_got = lax.switch(choices[n], [branch(p) for p in plans], near, lent)
            near_all.append(near_got)
            far_all.append(far_got)
            members = {e for plan in plans for p in plan for e in (p, p ^ half)}
            here = jnp.asarray([e in members for e in range(expert_count)])
            group += jnp.sum(jnp.where(here & (lane_ids == own_index), n, 0))
        wide = left * tile
        pieces.append((0, at * tile, width // 2, wide, near_all))
        pieces.append((width // 2, at * tile, width // 2, wide, far_all))

    source = (is_moved * (1 + group)).reshape(1)
    adam_out, x_grad = place(source, own_sum, other_sum, pieces, width, inner)
    return (x_grad, adam_out[None])


def solution(mesh):
    in_specs = (
        P(("dp", "expert"), None),
        P(("dp", "expert"), None),
        P(("dp", "expert"), None),
        P(("dp", "expert"), None),
        P(),
        P("expert", None, "dp"),
        P("expert", "dp", None),
        P("expert", None, "dp"),
        P("expert", None, "dp"),
    )
    out_specs = (P(("dp", "expert"), None), P("expert", None, "dp"))

    return jax.shard_map(shards, mesh=mesh, in_specs=in_specs, out_specs=out_specs, check_vma=False)
```

```python
import functools
import itertools

import jax
import jax.numpy as jnp
from jax import lax
from jax.experimental import pallas as pl
from jax.experimental.pallas import tpu as pltpu
from jax.sharding import PartitionSpec as P


ADAM_STEP = 100


coef_c = 0.7978845608028654
coef_a = 0.044715
beta_one = 0.9
beta_two = 0.999
adam_eps = 1e-08


MIB = 2**20

f32 = jnp.float32
bf16 = jnp.bfloat16
NN = (((1,), (0,)), ((), ()))
NT = (((1,), (1,)), ((), ()))
TN = (((0,), (0,)), ((), ()))


def mxu(a, b, dims):
    return lax.dot_general(a, b, dims, preferred_element_type=f32)


def gelu_slope(pre_act):
    inner_arg = coef_c * (pre_act + coef_a * pre_act * pre_act * pre_act)
    tanh_val = jnp.tanh(inner_arg)
    return 0.5 * (1.0 + tanh_val) + 0.5 * pre_act * (1.0 - tanh_val * tanh_val) * coef_c * (
        1.0 + 3.0 * coef_a * pre_act * pre_act
    )


def adam_step(weight_grad, first_moment, second_moment):
    first_new = beta_one * first_moment + (1.0 - beta_one) * weight_grad
    second_new = beta_two * second_moment + (1.0 - beta_two) * weight_grad * weight_grad
    return (
        first_new
        / (1.0 - beta_one**ADAM_STEP)
        / (jnp.sqrt(second_new / (1.0 - beta_two**ADAM_STEP)) + adam_eps)
    ).astype(bf16)


def pack_kernel(expert_count, capacity, ids_ref, gates_ref, x_ref, g_ref, rows_ref, where_ref):
    tok_count, width = x_ref.shape
    slots = expert_count * capacity
    first = ids_ref[0:1, :]
    second = ids_ref[1:2, :]
    experts = lax.broadcasted_iota(jnp.int32, (expert_count, tok_count), 0)
    hit_first = experts == first
    hit_second = experts == second
    hits = jnp.where(hit_first | hit_second, 1.0, 0.0).astype(bf16)
    earlier = lax.broadcasted_iota(jnp.int32, (tok_count, tok_count), 0)
    later = lax.broadcasted_iota(jnp.int32, (tok_count, tok_count), 1)
    upper = jnp.where(earlier < later, 1.0, 0.0).astype(bf16)
    before = mxu(hits, upper, NN)
    slot_first = jnp.sum(jnp.where(hit_first, before, 0.0), axis=0, keepdims=True)
    slot_second = jnp.sum(jnp.where(hit_second, before, 0.0), axis=0, keepdims=True)
    pos_first = first * capacity + slot_first.astype(jnp.int32)
    pos_second = second * capacity + slot_second.astype(jnp.int32)
    where_ref[0:1, :] = pos_first
    where_ref[1:2, :] = pos_second
    row = lax.broadcasted_iota(jnp.int32, (slots, tok_count), 0)
    at_first = row == pos_first
    at_second = row == pos_second
    pick = jnp.where(at_first | at_second, 1.0, 0.0).astype(bf16)
    gate = jnp.sum(
        jnp.where(at_first, gates_ref[0:1, :], 0.0) + jnp.where(at_second, gates_ref[1:2, :], 0.0),
        axis=1,
        keepdims=True,
    )
    rows_ref[:, :width] = mxu(pick, x_ref[...], NN).astype(bf16)
    rows_ref[:, width:] = (gate * mxu(pick, g_ref[...], NN)).astype(bf16)


def pack_rows(id_rows, gate_rows, tokens, out_grad, expert_count, capacity):
    tok_count, width = tokens.shape
    slots = expert_count * capacity
    return pl.pallas_call(
        functools.partial(pack_kernel, expert_count, capacity),
        out_shape=(
            jax.ShapeDtypeStruct((slots, 2 * width), bf16),
            jax.ShapeDtypeStruct((2, tok_count), jnp.int32),
        ),
        name="pack_rows",
    )(id_rows, gate_rows, tokens, out_grad)


def pre_tile(rows, w_in, w_out, pre_ref):
    per, width = rows[0].shape[0], rows[0].shape[1] // 2
    for b, block in enumerate(rows):
        pre_act = mxu(block[:, :width], w_in, NN)
        act_grad = mxu(block[:, width:], w_out, NT)
        pre_ref[b * per : (b + 1) * per, :] = (act_grad * gelu_slope(pre_act)).astype(bf16)


def first_kernel(blocks, *refs):
    rows = refs[:blocks]
    w_in_ref, w_out_ref, m_ref, v_ref, adam_ref, pre_ref, xt_ref = refs[blocks:]
    width, per = m_ref.shape[0], rows[0].shape[0]
    for b in range(blocks):
        xt_ref[:, b * per : (b + 1) * per] = rows[b][:, :width].T
    pre_tile(rows, w_in_ref[...], w_out_ref[...], pre_ref)
    weight_grad = mxu(xt_ref[...], pre_ref[...], NN)
    adam_ref[...] = adam_step(weight_grad, m_ref[...], v_ref[...])


def first_step(rows, w_in, w_out, first_moment, second_moment, tile):
    per, width = rows[0].shape[0], rows[0].shape[1] // 2
    total = len(rows) * per
    corner = lambda i: (0, 0)
    columns = pl.BlockSpec((width, tile), corner)
    return pl.pallas_call(
        functools.partial(first_kernel, len(rows)),
        grid=(1,),
        in_specs=[pl.BlockSpec(r.shape, corner) for r in rows]
        + [columns, pl.BlockSpec((tile, width), corner), columns, columns],
        out_specs=[
            columns,
            pl.BlockSpec((total, tile), corner),
            pl.BlockSpec((width, total), corner),
        ],
        out_shape=[
            jax.ShapeDtypeStruct((width, tile), bf16),
            jax.ShapeDtypeStruct((total, tile), bf16),
            jax.ShapeDtypeStruct((width, total), bf16),
        ],
        compiler_params=pltpu.CompilerParams(vmem_limit_bytes=56 * MIB),
        cost_estimate=pl.CostEstimate(
            flops=6 * total * width * tile, bytes_accessed=14 * tile * width, transcendentals=0
        ),
        name="first_step",
    )(*rows, w_in, w_out, first_moment, second_moment)


def rest_kernel(blocks, *refs):
    rows = refs[:blocks]
    first_ref, w_first_ref, w_in_ref, w_out_ref, pre_ref = refs[blocks : blocks + 5]
    parts = refs[blocks + 5 : -1]
    total_ref = refs[-1]
    per = rows[0].shape[0]
    step = pl.program_id(0)

    @pl.when(step == 0)
    def _():
        total_ref[...] = mxu(first_ref[...], w_first_ref[...], NT)

    pre_tile(rows, w_in_ref[...], w_out_ref[...], pre_ref)
    total_ref[...] += mxu(pre_ref[...], w_in_ref[...], NT)

    @pl.when(step == pl.num_programs(0) - 1)
    def _():
        for b in range(blocks):
            parts[b][...] = total_ref[b * per : (b + 1) * per, :].astype(bf16)


def rest_step(rows, pre_first, w_in, w_out, tile):
    per, width = rows[0].shape[0], rows[0].shape[1] // 2
    total = len(rows) * per
    tiles = w_in.shape[1] // tile - 1
    corner = lambda j: (0, 0)
    return pl.pallas_call(
        functools.partial(rest_kernel, len(rows)),
        grid=(tiles,),
        in_specs=[pl.BlockSpec(r.shape, corner) for r in rows]
        + [
            pl.BlockSpec((total, tile), corner),
            pl.BlockSpec((width, tile), corner),
            pl.BlockSpec((width, tile), lambda j: (0, j + 1)),
            pl.BlockSpec((tile, width), lambda j: (j + 1, 0)),
        ],
        out_specs=[pl.BlockSpec((total, tile), lambda j: (0, j))]
        + [pl.BlockSpec((per, width), corner) for _ in rows],
        out_shape=[jax.ShapeDtypeStruct((total, tiles * tile), bf16)]
        + [jax.ShapeDtypeStruct((per, width), bf16) for _ in rows],
        scratch_shapes=[pltpu.VMEM((total, width), f32)],
        compiler_params=pltpu.CompilerParams(vmem_limit_bytes=56 * MIB),
        cost_estimate=pl.CostEstimate(
            flops=6 * total * width * tile * tiles,
            bytes_accessed=4 * tile * width * tiles,
            transcendentals=0,
        ),
        name="rest_step",
    )(*rows, pre_first, w_in, w_in, w_out)


def adam_kernel(xt_ref, pre_ref, m_ref, v_ref, out_ref):
    weight_grad = mxu(xt_ref[...], pre_ref[...], NN)
    out_ref[...] = adam_step(weight_grad, m_ref[...], v_ref[...])


def adam_block(x_t, pre_rest, first_moment, second_moment, start, tiles, tile, part, parts):
    width, total = x_t.shape
    rows = width // parts
    block = pl.BlockSpec((rows, tile), lambda j: (part, start + j))
    return pl.pallas_call(
        adam_kernel,
        grid=(tiles,),
        in_specs=[
            pl.BlockSpec((rows, total), lambda j: (part, 0)),
            pl.BlockSpec((total, tile), lambda j: (0, start - 1 + j)),
            block,
            block,
        ],
        out_specs=pl.BlockSpec((rows, tile), lambda j: (0, j)),
        out_shape=jax.ShapeDtypeStruct((rows, tiles * tile), bf16),
        compiler_params=pltpu.CompilerParams(vmem_limit_bytes=60 * MIB),
        cost_estimate=pl.CostEstimate(
            flops=2 * total * rows * tile * tiles,
            bytes_accessed=10 * tile * rows * tiles,
            transcendentals=0,
        ),
    )(x_t, pre_rest, first_moment, second_moment)


def place_kernel(boxes, source_ref, *refs):
    sources, at = [], 0
    for box in boxes:
        sources.append(refs[at : at + box[5]])
        at += box[5]
    out_ref = refs[at]
    bufs = refs[at + 1 : at + 1 + len(boxes)]
    in_sem, out_sem = refs[at + 1 + len(boxes) :]
    for n, arrays in enumerate(sources):
        start, high = boxes[n][2], boxes[n][3]
        for k, array in enumerate(arrays):
            last = k == len(arrays) - 1
            wanted = source_ref[0] >= k if last else source_ref[0] == k

            @pl.when(wanted)
            def _(n=n, array=array, start=start, high=high):
                pltpu.make_async_copy(
                    array.at[pl.ds(start, high)], bufs[n], in_sem.at[n]
                ).start()

    puts = []
    for n, (row, col, start, high, wide, _) in enumerate(boxes):
        pltpu.make_async_copy(
            sources[n][0].at[pl.ds(start, high)], bufs[n], in_sem.at[n]
        ).wait()
        put = pltpu.make_async_copy(
            bufs[n], out_ref.at[pl.ds(row + start, high), pl.ds(col, wide)], out_sem.at[n]
        )
        put.start()
        puts.append(put)
    for put in puts:
        put.wait()


def place(source, pieces, width, inner):
    boxes = [piece[:5] + (len(piece[5]),) for piece in pieces]
    args = [array for piece in pieces for array in piece[5]]
    return pl.pallas_call(
        functools.partial(place_kernel, boxes),
        in_specs=[pl.BlockSpec(memory_space=pltpu.SMEM)]
        + [pl.BlockSpec(memory_space=pl.ANY) for _ in args],
        out_specs=pl.BlockSpec(memory_space=pl.ANY),
        out_shape=jax.ShapeDtypeStruct((width, inner), bf16),
        scratch_shapes=[pltpu.VMEM((box[3], box[4]), bf16) for box in boxes]
        + [pltpu.SemaphoreType.DMA((len(boxes),)), pltpu.SemaphoreType.DMA((len(boxes),))],
        compiler_params=pltpu.CompilerParams(vmem_limit_bytes=8 * MIB),
        cost_estimate=pl.CostEstimate(
            flops=0, bytes_accessed=4 * width * inner, transcendentals=0
        ),
        name="place",
    )(source, *args)


def swap_plans(half):
    line = half >> 1
    groups = {}
    for e in range(half):
        groups.setdefault(e & ~(line | 1), []).append(e)
    groups = list(groups.values())
    if half < 4 or len(groups) > 2:
        return []
    forced = {0, half - 1}
    switches = []
    for members in groups:
        must = forced & set(members)
        plans = [
            set(s)
            for k in range(2, len(members) + 1)
            for s in itertools.combinations(members, k)
            if must <= set(s)
        ]
        table = []
        for mask in range(1 << half):
            moved = must | {e for e in members if mask >> e & 1}
            table.append(next(n for n, plan in enumerate(plans) if moved <= plan))
        switches.append((plans, table))
    return switches


def combine_kernel(where_ref, back_ref, out_ref):
    slots, tok_count = back_ref.shape[0], out_ref.shape[0]
    row = lax.broadcasted_iota(jnp.int32, (slots, tok_count), 0)
    pick = (row == where_ref[0:1, :]) | (row == where_ref[1:2, :])
    pick = jnp.where(pick, 1.0, 0.0).astype(bf16)
    out_ref[...] = mxu(pick, back_ref[...], TN).astype(bf16)


def combine_rows(where_to, returned, tok_count):
    return pl.pallas_call(
        combine_kernel,
        out_shape=jax.ShapeDtypeStruct((tok_count, returned.shape[1]), bf16),
        name="combine_rows",
    )(where_to, returned)


def dp_shift(block, apart):
    count = lax.axis_size("dp")
    return lax.ppermute(block, "dp", [(i, i ^ apart) for i in range(count)])


def shards(
    tokens, out_grad, gates, expert_ids, swap_list, w_in, w_out, first_moment, second_moment
):
    expert_count = lax.axis_size("expert")
    dp_count = lax.axis_size("dp")
    half = 1 << (expert_count.bit_length() - 2)
    own_index = lax.axis_index("expert")
    lane_ids = jnp.arange(expert_count, dtype=jnp.int32)
    partner_me = jnp.sum(jnp.where(lane_ids == own_index, swap_list, 0))
    is_moved = (partner_me != own_index).astype(jnp.int32)
    moved_bits = jnp.where((swap_list != lane_ids) & (lane_ids < half), 1 << lane_ids, 0)
    moved_mask = jnp.sum(moved_bits)
    tok_count, width = tokens.shape
    capacity = 3 * tok_count // expert_count
    slots = expert_count * capacity

    rows, where_to = pack_rows(expert_ids.T, gates.T, tokens, out_grad, expert_count, capacity)
    own = lax.all_to_all(
        rows.reshape(expert_count, capacity, 2 * width),
        "expert",
        split_axis=0,
        concat_axis=0,
        tiled=True,
    ).reshape(slots, 2 * width)
    all_rows = [own] + [dp_shift(own, d) for d in range(1, dp_count)]
    if dp_count == 2:
        all_rows = [pltpu.with_memory_space_constraint(r, pltpu.VMEM) for r in all_rows]

    inner = w_in.shape[2]
    tile = 256 if inner % 256 == 0 else 128
    tiles = inner // tile
    route = [(e, e ^ half) for e in range(expert_count)]
    across = [(e, e ^ 1) for e in range(expert_count)]

    first, pre_first, x_t = first_step(
        all_rows, w_in[0], w_out[0], first_moment[0], second_moment[0], tile
    )
    first_got = lax.ppermute(first, "expert", route)
    pieces = [(0, 0, width, tile, [first, first_got])]

    pre_rest, *parts = rest_step(all_rows, pre_first, w_in[0], w_out[0], tile)
    total = parts[0].astype(f32)
    for d in range(1, dp_count):
        total = total + dp_shift(parts[d], d).astype(f32)
    returned = lax.all_to_all(
        total.astype(bf16).reshape(expert_count, capacity, width),
        "expert",
        split_axis=0,
        concat_axis=0,
        tiled=True,
    ).reshape(slots, width)

    x_grad = combine_rows(where_to, returned, tok_count)
    switches = swap_plans(half) if tiles > 2 else []
    direct = 1 if switches else tiles - 1
    moments = (first_moment[0], second_moment[0])
    second = adam_block(x_t, pre_rest, *moments, 1, direct, tile, 0, 1)
    second_got = lax.ppermute(second, "expert", route)
    pieces.append((0, tile, width, direct * tile, [second, second_got]))
    group = jnp.zeros((), jnp.int32)

    if switches:
        at, left = 1 + direct, tiles - 1 - direct
        far = adam_block(x_t, pre_rest, *moments, at, left, tile, 1, 2)
        lent = lax.ppermute(far, "expert", across)
        near = adam_block(x_t, pre_rest, *moments, at, left, tile, 0, 2)

        def branch(plan):
            pairs = [(e, e ^ half) for p in plan for e in (p, p ^ half)]
            skew = [(e ^ 1, f) for e, f in pairs]

            def run(near, lent):
                return (
                    lax.ppermute(near, "expert", pairs),
                    lax.ppermute(lent, "expert", skew),
                )

            return run

        near, lent, x_grad = lax.optimization_barrier((near, lent, x_grad))
        near_all, far_all = [near], [far]
        for n, (plans, table) in enumerate(switches):
            choice = jnp.asarray(table, jnp.int32)[moved_mask]
            near_got, far_got = lax.switch(choice, [branch(p) for p in plans], near, lent)
            near_all.append(near_got)
            far_all.append(far_got)
            members = {e for plan in plans for p in plan for e in (p, p ^ half)}
            here = jnp.asarray([e in members for e in range(expert_count)])
            group += jnp.sum(jnp.where(here & (lane_ids == own_index), n, 0))
        wide = left * tile
        pieces.append((0, at * tile, width // 2, wide, near_all))
        pieces.append((width // 2, at * tile, width // 2, wide, far_all))

    source = (is_moved * (1 + group)).reshape(1)
    cut = []
    for row, col, high, wide, arrays in pieces:
        step = width // 4
        for at in range(0, high, step):
            cut.append((row, col, at, min(step, high - at), wide, arrays))
    adam_out = place(source, cut, width, inner)
    return (x_grad, adam_out[None])


def solution(mesh):
    in_specs = (
        P(("dp", "expert"), None),
        P(("dp", "expert"), None),
        P(("dp", "expert"), None),
        P(("dp", "expert"), None),
        P(),
        P("expert", None, "dp"),
        P("expert", "dp", None),
        P("expert", None, "dp"),
        P("expert", None, "dp"),
    )
    out_specs = (P(("dp", "expert"), None), P("expert", None, "dp"))

    return jax.shard_map(shards, mesh=mesh, in_specs=in_specs, out_specs=out_specs, check_vma=False)
```

```python
import functools
import itertools

import jax
import jax.numpy as jnp
from jax import lax
from jax.experimental import pallas as pl
from jax.experimental.pallas import tpu as pltpu
from jax.sharding import PartitionSpec as P


ADAM_STEP = 100


coef_c = 0.7978845608028654
coef_a = 0.044715
beta_one = 0.9
beta_two = 0.999
adam_eps = 1e-08


MIB = 2**20

f32 = jnp.float32
bf16 = jnp.bfloat16
NN = (((1,), (0,)), ((), ()))
NT = (((1,), (1,)), ((), ()))
TN = (((0,), (0,)), ((), ()))


def mxu(a, b, dims):
    return lax.dot_general(a, b, dims, preferred_element_type=f32)


def gelu_slope(pre_act):
    square = pre_act * pre_act
    tanh_val = jnp.tanh(pre_act * (coef_c + coef_c * coef_a * square))
    bend = pre_act * (coef_c + 3.0 * coef_c * coef_a * square)
    return 0.5 + 0.5 * (tanh_val + bend * (1.0 - tanh_val * tanh_val))


def adam_step(weight_grad, first_moment, second_moment):
    unbias_one = 1.0 / (1.0 - beta_one**ADAM_STEP)
    unbias_two = 1.0 / (1.0 - beta_two**ADAM_STEP)
    first_hat = (beta_one * unbias_one) * first_moment + ((1.0 - beta_one) * unbias_one) * weight_grad
    second_hat = (beta_two * unbias_two) * second_moment + (
        (1.0 - beta_two) * unbias_two
    ) * (weight_grad * weight_grad)
    return (first_hat / (jnp.sqrt(second_hat) + adam_eps)).astype(bf16)


def pack_kernel(expert_count, capacity, ids_ref, gates_ref, x_ref, g_ref, rows_ref, where_ref):
    tok_count, width = x_ref.shape
    slots = expert_count * capacity
    first = ids_ref[0:1, :]
    second = ids_ref[1:2, :]
    experts = lax.broadcasted_iota(jnp.int32, (expert_count, tok_count), 0)
    hit_first = experts == first
    hit_second = experts == second
    hits = jnp.where(hit_first | hit_second, 1.0, 0.0).astype(bf16)
    earlier = lax.broadcasted_iota(jnp.int32, (tok_count, tok_count), 0)
    later = lax.broadcasted_iota(jnp.int32, (tok_count, tok_count), 1)
    upper = jnp.where(earlier < later, 1.0, 0.0).astype(bf16)
    before = mxu(hits, upper, NN)
    slot_first = jnp.sum(jnp.where(hit_first, before, 0.0), axis=0, keepdims=True)
    slot_second = jnp.sum(jnp.where(hit_second, before, 0.0), axis=0, keepdims=True)
    pos_first = first * capacity + slot_first.astype(jnp.int32)
    pos_second = second * capacity + slot_second.astype(jnp.int32)
    where_ref[0:1, :] = pos_first
    where_ref[1:2, :] = pos_second
    row = lax.broadcasted_iota(jnp.int32, (slots, tok_count), 0)
    at_first = row == pos_first
    at_second = row == pos_second
    pick = jnp.where(at_first | at_second, 1.0, 0.0).astype(bf16)
    gate = jnp.sum(
        jnp.where(at_first, gates_ref[0:1, :], 0.0) + jnp.where(at_second, gates_ref[1:2, :], 0.0),
        axis=1,
        keepdims=True,
    )
    rows_ref[:, :width] = mxu(pick, x_ref[...], NN).astype(bf16)
    rows_ref[:, width:] = (gate * mxu(pick, g_ref[...], NN)).astype(bf16)


def pack_rows(id_rows, gate_rows, tokens, out_grad, expert_count, capacity):
    tok_count, width = tokens.shape
    slots = expert_count * capacity
    return pl.pallas_call(
        functools.partial(pack_kernel, expert_count, capacity),
        out_shape=(
            jax.ShapeDtypeStruct((slots, 2 * width), bf16),
            jax.ShapeDtypeStruct((2, tok_count), jnp.int32),
        ),
        name="pack_rows",
    )(id_rows, gate_rows, tokens, out_grad)


def pre_tile(rows, w_in, w_out, pre_ref):
    per, width = rows[0].shape[0], rows[0].shape[1] // 2
    for b, block in enumerate(rows):
        pre_act = mxu(block[:, :width], w_in, NN)
        act_grad = mxu(block[:, width:], w_out, NT)
        pre_ref[b * per : (b + 1) * per, :] = (act_grad * gelu_slope(pre_act)).astype(bf16)


def first_kernel(blocks, *refs):
    rows = refs[:blocks]
    w_in_ref, w_out_ref, m_ref, v_ref, adam_ref, pre_ref, xt_ref = refs[blocks:]
    width, per = m_ref.shape[0], rows[0].shape[0]
    for b in range(blocks):
        xt_ref[:, b * per : (b + 1) * per] = rows[b][:, :width].T
    pre_tile(rows, w_in_ref[...], w_out_ref[...], pre_ref)
    weight_grad = mxu(xt_ref[...], pre_ref[...], NN)
    adam_ref[...] = adam_step(weight_grad, m_ref[...], v_ref[...])


def first_step(rows, w_in, w_out, first_moment, second_moment, tile):
    per, width = rows[0].shape[0], rows[0].shape[1] // 2
    total = len(rows) * per
    corner = lambda i: (0, 0)
    columns = pl.BlockSpec((width, tile), corner)
    return pl.pallas_call(
        functools.partial(first_kernel, len(rows)),
        grid=(1,),
        in_specs=[pl.BlockSpec(r.shape, corner) for r in rows]
        + [columns, pl.BlockSpec((tile, width), corner), columns, columns],
        out_specs=[
            columns,
            pl.BlockSpec((total, tile), corner),
            pl.BlockSpec((width, total), corner),
        ],
        out_shape=[
            jax.ShapeDtypeStruct((width, tile), bf16),
            jax.ShapeDtypeStruct((total, tile), bf16),
            jax.ShapeDtypeStruct((width, total), bf16),
        ],
        compiler_params=pltpu.CompilerParams(vmem_limit_bytes=56 * MIB),
        cost_estimate=pl.CostEstimate(
            flops=6 * total * width * tile, bytes_accessed=14 * tile * width, transcendentals=0
        ),
        name="first_step",
    )(*rows, w_in, w_out, first_moment, second_moment)


def rest_kernel(blocks, *refs):
    rows = refs[:blocks]
    first_ref, w_first_ref, w_in_ref, w_out_ref, pre_ref = refs[blocks : blocks + 5]
    parts = refs[blocks + 5 : -1]
    total_ref = refs[-1]
    per = rows[0].shape[0]
    step = pl.program_id(0)

    @pl.when(step == 0)
    def _():
        total_ref[...] = mxu(first_ref[...], w_first_ref[...], NT)

    pre_tile(rows, w_in_ref[...], w_out_ref[...], pre_ref)
    total_ref[...] += mxu(pre_ref[...], w_in_ref[...], NT)

    @pl.when(step == pl.num_programs(0) - 1)
    def _():
        for b in range(blocks):
            parts[b][...] = total_ref[b * per : (b + 1) * per, :].astype(bf16)


def rest_step(rows, pre_first, w_in, w_out, tile):
    per, width = rows[0].shape[0], rows[0].shape[1] // 2
    total = len(rows) * per
    tiles = w_in.shape[1] // tile - 1
    corner = lambda j: (0, 0)
    return pl.pallas_call(
        functools.partial(rest_kernel, len(rows)),
        grid=(tiles,),
        in_specs=[pl.BlockSpec(r.shape, corner) for r in rows]
        + [
            pl.BlockSpec((total, tile), corner),
            pl.BlockSpec((width, tile), corner),
            pl.BlockSpec((width, tile), lambda j: (0, j + 1)),
            pl.BlockSpec((tile, width), lambda j: (j + 1, 0)),
        ],
        out_specs=[pl.BlockSpec((total, tile), lambda j: (0, j))]
        + [pl.BlockSpec((per, width), corner) for _ in rows],
        out_shape=[jax.ShapeDtypeStruct((total, tiles * tile), bf16)]
        + [jax.ShapeDtypeStruct((per, width), bf16) for _ in rows],
        scratch_shapes=[pltpu.VMEM((total, width), f32)],
        compiler_params=pltpu.CompilerParams(vmem_limit_bytes=56 * MIB),
        cost_estimate=pl.CostEstimate(
            flops=6 * total * width * tile * tiles,
            bytes_accessed=4 * tile * width * tiles,
            transcendentals=0,
        ),
        name="rest_step",
    )(*rows, pre_first, w_in, w_in, w_out)


def adam_kernel(xt_ref, pre_ref, m_ref, v_ref, out_ref):
    weight_grad = mxu(xt_ref[...], pre_ref[...], NN)
    out_ref[...] = adam_step(weight_grad, m_ref[...], v_ref[...])


def adam_block(x_t, pre_rest, first_moment, second_moment, start, tiles, tile, part, parts):
    width, total = x_t.shape
    rows = width // parts
    block = pl.BlockSpec((rows, tile), lambda j: (part, start + j))
    return pl.pallas_call(
        adam_kernel,
        grid=(tiles,),
        in_specs=[
            pl.BlockSpec((rows, total), lambda j: (part, 0)),
            pl.BlockSpec((total, tile), lambda j: (0, start - 1 + j)),
            block,
            block,
        ],
        out_specs=pl.BlockSpec((rows, tile), lambda j: (0, j)),
        out_shape=jax.ShapeDtypeStruct((rows, tiles * tile), bf16),
        compiler_params=pltpu.CompilerParams(vmem_limit_bytes=60 * MIB),
        cost_estimate=pl.CostEstimate(
            flops=2 * total * rows * tile * tiles,
            bytes_accessed=10 * tile * rows * tiles,
            transcendentals=0,
        ),
    )(x_t, pre_rest, first_moment, second_moment)


def place_kernel(boxes, source_ref, *refs):
    sources, at = [], 0
    for box in boxes:
        sources.append(refs[at : at + box[5]])
        at += box[5]
    out_ref = refs[at]
    bufs = refs[at + 1 : at + 1 + len(boxes)]
    in_sem, out_sem = refs[at + 1 + len(boxes) :]
    most = max(len(arrays) for arrays in sources)
    for k in range(most):

        @pl.when(source_ref[0] == k)
        def _(k=k):
            for n, arrays in enumerate(sources):
                array = arrays[min(k, len(arrays) - 1)]
                start, high = boxes[n][2], boxes[n][3]
                pltpu.make_async_copy(
                    array.at[pl.ds(start, high)], bufs[n], in_sem.at[n]
                ).start()

    puts = []
    for n, (row, col, start, high, wide, _) in enumerate(boxes):
        pltpu.make_async_copy(
            sources[n][0].at[pl.ds(start, high)], bufs[n], in_sem.at[n]
        ).wait()
        put = pltpu.make_async_copy(
            bufs[n], out_ref.at[pl.ds(row + start, high), pl.ds(col, wide)], out_sem.at[n]
        )
        put.start()
        puts.append(put)
    for put in puts:
        put.wait()


def place(source, pieces, width, inner):
    boxes = [piece[:5] + (len(piece[5]),) for piece in pieces]
    args = [array for piece in pieces for array in piece[5]]
    return pl.pallas_call(
        functools.partial(place_kernel, boxes),
        in_specs=[pl.BlockSpec(memory_space=pltpu.SMEM)]
        + [pl.BlockSpec(memory_space=pl.ANY) for _ in args],
        out_specs=pl.BlockSpec(memory_space=pl.ANY),
        out_shape=jax.ShapeDtypeStruct((width, inner), bf16),
        scratch_shapes=[pltpu.VMEM((box[3], box[4]), bf16) for box in boxes]
        + [pltpu.SemaphoreType.DMA((len(boxes),)), pltpu.SemaphoreType.DMA((len(boxes),))],
        compiler_params=pltpu.CompilerParams(vmem_limit_bytes=8 * MIB),
        cost_estimate=pl.CostEstimate(
            flops=0, bytes_accessed=4 * width * inner, transcendentals=0
        ),
        name="place",
    )(source, *args)


def swap_plans(half):
    line = half >> 1
    groups = {}
    for e in range(half):
        groups.setdefault(e & ~(line | 1), []).append(e)
    groups = list(groups.values())
    if half < 4 or len(groups) > 2:
        return []
    forced = {0, half - 1}
    switches = []
    for members in groups:
        must = forced & set(members)
        plans = [
            set(s)
            for k in range(2, len(members) + 1)
            for s in itertools.combinations(members, k)
            if must <= set(s)
        ]
        table = []
        for mask in range(1 << half):
            moved = must | {e for e in members if mask >> e & 1}
            table.append(next(n for n, plan in enumerate(plans) if moved <= plan))
        switches.append((plans, table))
    return switches


def combine_kernel(where_ref, back_ref, out_ref):
    slots, tok_count = back_ref.shape[0], out_ref.shape[0]
    row = lax.broadcasted_iota(jnp.int32, (slots, tok_count), 0)
    pick = (row == where_ref[0:1, :]) | (row == where_ref[1:2, :])
    pick = jnp.where(pick, 1.0, 0.0).astype(bf16)
    out_ref[...] = mxu(pick, back_ref[...], TN).astype(bf16)


def combine_rows(where_to, returned, tok_count):
    return pl.pallas_call(
        combine_kernel,
        out_shape=jax.ShapeDtypeStruct((tok_count, returned.shape[1]), bf16),
        name="combine_rows",
    )(where_to, returned)


def dp_shift(block, apart):
    count = lax.axis_size("dp")
    return lax.ppermute(block, "dp", [(i, i ^ apart) for i in range(count)])


def shards(
    tokens, out_grad, gates, expert_ids, swap_list, w_in, w_out, first_moment, second_moment
):
    expert_count = lax.axis_size("expert")
    dp_count = lax.axis_size("dp")
    half = 1 << (expert_count.bit_length() - 2)
    own_index = lax.axis_index("expert")
    lane_ids = jnp.arange(expert_count, dtype=jnp.int32)
    partner_me = jnp.sum(jnp.where(lane_ids == own_index, swap_list, 0))
    is_moved = (partner_me != own_index).astype(jnp.int32)
    moved_bits = jnp.where((swap_list != lane_ids) & (lane_ids < half), 1 << lane_ids, 0)
    moved_mask = jnp.sum(moved_bits)
    tok_count, width = tokens.shape
    capacity = 3 * tok_count // expert_count
    slots = expert_count * capacity

    rows, where_to = pack_rows(expert_ids.T, gates.T, tokens, out_grad, expert_count, capacity)
    own = lax.all_to_all(
        rows.reshape(expert_count, capacity, 2 * width),
        "expert",
        split_axis=0,
        concat_axis=0,
        tiled=True,
    ).reshape(slots, 2 * width)
    all_rows = [own] + [dp_shift(own, d) for d in range(1, dp_count)]
    if dp_count == 2:
        all_rows = [pltpu.with_memory_space_constraint(r, pltpu.VMEM) for r in all_rows]

    inner = w_in.shape[2]
    tile = 256 if inner % 256 == 0 else 128
    tiles = inner // tile
    route = [(e, e ^ half) for e in range(expert_count)]
    across = [(e, e ^ 1) for e in range(expert_count)]

    first, pre_first, x_t = first_step(
        all_rows, w_in[0], w_out[0], first_moment[0], second_moment[0], tile
    )
    first_got = lax.ppermute(first, "expert", route)
    pieces = [(0, 0, width, tile, [first, first_got])]

    pre_rest, *parts = rest_step(all_rows, pre_first, w_in[0], w_out[0], tile)
    total = parts[0].astype(f32)
    for d in range(1, dp_count):
        total = total + dp_shift(parts[d], d).astype(f32)
    returned = lax.all_to_all(
        total.astype(bf16).reshape(expert_count, capacity, width),
        "expert",
        split_axis=0,
        concat_axis=0,
        tiled=True,
    ).reshape(slots, width)

    x_grad = combine_rows(where_to, returned, tok_count)
    switches = swap_plans(half) if tiles > 2 else []
    direct = 1 if switches else tiles - 1
    moments = (first_moment[0], second_moment[0])
    second = adam_block(x_t, pre_rest, *moments, 1, direct, tile, 0, 1)
    second_got = lax.ppermute(second, "expert", route)
    pieces.append((0, tile, width, direct * tile, [second, second_got]))
    group = jnp.zeros((), jnp.int32)

    if switches:
        at, left = 1 + direct, tiles - 1 - direct
        far = adam_block(x_t, pre_rest, *moments, at, left, tile, 1, 2)
        lent = lax.ppermute(far, "expert", across)
        near = adam_block(x_t, pre_rest, *moments, at, left, tile, 0, 2)

        def branch(plan):
            pairs = [(e, e ^ half) for p in plan for e in (p, p ^ half)]
            skew = [(e ^ 1, f) for e, f in pairs]

            def run(near, lent):
                return (
                    lax.ppermute(near, "expert", pairs),
                    lax.ppermute(lent, "expert", skew),
                )

            return run

        near, lent, x_grad = lax.optimization_barrier((near, lent, x_grad))
        near_all, far_all = [near], [far]
        for n, (plans, table) in enumerate(switches):
            choice = jnp.asarray(table, jnp.int32)[moved_mask]
            near_got, far_got = lax.switch(choice, [branch(p) for p in plans], near, lent)
            near_all.append(near_got)
            far_all.append(far_got)
            members = {e for plan in plans for p in plan for e in (p, p ^ half)}
            here = jnp.asarray([e in members for e in range(expert_count)])
            group += jnp.sum(jnp.where(here & (lane_ids == own_index), n, 0))
        wide = left * tile
        pieces.append((0, at * tile, width // 2, wide, near_all))
        pieces.append((width // 2, at * tile, width // 2, wide, far_all))

    source = (is_moved * (1 + group)).reshape(1)
    cut = []
    for row, col, high, wide, arrays in pieces:
        step = width
        for at in range(0, high, step):
            cut.append((row, col, at, min(step, high - at), wide, arrays))
    adam_out = place(source, cut, width, inner)
    return (x_grad, adam_out[None])


def solution(mesh):
    in_specs = (
        P(("dp", "expert"), None),
        P(("dp", "expert"), None),
        P(("dp", "expert"), None),
        P(("dp", "expert"), None),
        P(),
        P("expert", None, "dp"),
        P("expert", "dp", None),
        P("expert", None, "dp"),
        P("expert", None, "dp"),
    )
    out_specs = (P(("dp", "expert"), None), P("expert", None, "dp"))

    return jax.shard_map(shards, mesh=mesh, in_specs=in_specs, out_specs=out_specs, check_vma=False)
```

```python
import functools
import itertools

import jax
import jax.numpy as jnp
from jax import lax
from jax.experimental import pallas as pl
from jax.experimental.pallas import tpu as pltpu
from jax.sharding import PartitionSpec as P


ADAM_STEP = 100


coef_c = 0.7978845608028654
coef_a = 0.044715
beta_one = 0.9
beta_two = 0.999
adam_eps = 1e-08


MIB = 2**20

f32 = jnp.float32
bf16 = jnp.bfloat16
NN = (((1,), (0,)), ((), ()))
NT = (((1,), (1,)), ((), ()))
TN = (((0,), (0,)), ((), ()))


def mxu(a, b, dims):
    return lax.dot_general(a, b, dims, preferred_element_type=f32)


def gelu_slope(pre_act):
    square = pre_act * pre_act
    tanh_val = jnp.tanh(pre_act * (coef_c + coef_c * coef_a * square))
    bend = pre_act * (coef_c + 3.0 * coef_c * coef_a * square)
    return 0.5 + 0.5 * (tanh_val + bend * (1.0 - tanh_val * tanh_val))


def adam_step(weight_grad, first_moment, second_moment):
    unbias_one = 1.0 / (1.0 - beta_one**ADAM_STEP)
    unbias_two = 1.0 / (1.0 - beta_two**ADAM_STEP)
    first_hat = (beta_one * unbias_one) * first_moment + ((1.0 - beta_one) * unbias_one) * weight_grad
    second_hat = (beta_two * unbias_two) * second_moment + (
        (1.0 - beta_two) * unbias_two
    ) * (weight_grad * weight_grad)
    root = second_hat * lax.rsqrt(second_hat)
    return (first_hat / (root + adam_eps)).astype(bf16)


def pack_kernel(expert_count, capacity, ids_ref, gates_ref, x_ref, g_ref, rows_ref, where_ref):
    tok_count, width = x_ref.shape
    slots = expert_count * capacity
    first = ids_ref[0:1, :]
    second = ids_ref[1:2, :]
    experts = lax.broadcasted_iota(jnp.int32, (expert_count, tok_count), 0)
    hit_first = experts == first
    hit_second = experts == second
    hits = jnp.where(hit_first | hit_second, 1.0, 0.0).astype(bf16)
    earlier = lax.broadcasted_iota(jnp.int32, (tok_count, tok_count), 0)
    later = lax.broadcasted_iota(jnp.int32, (tok_count, tok_count), 1)
    upper = jnp.where(earlier < later, 1.0, 0.0).astype(bf16)
    before = mxu(hits, upper, NN)
    slot_first = jnp.sum(jnp.where(hit_first, before, 0.0), axis=0, keepdims=True)
    slot_second = jnp.sum(jnp.where(hit_second, before, 0.0), axis=0, keepdims=True)
    pos_first = first * capacity + slot_first.astype(jnp.int32)
    pos_second = second * capacity + slot_second.astype(jnp.int32)
    where_ref[0:1, :] = pos_first
    where_ref[1:2, :] = pos_second
    row = lax.broadcasted_iota(jnp.int32, (slots, tok_count), 0)
    at_first = row == pos_first
    at_second = row == pos_second
    pick = jnp.where(at_first | at_second, 1.0, 0.0).astype(bf16)
    gate = jnp.sum(
        jnp.where(at_first, gates_ref[0:1, :], 0.0) + jnp.where(at_second, gates_ref[1:2, :], 0.0),
        axis=1,
        keepdims=True,
    )
    rows_ref[:, :width] = mxu(pick, x_ref[...], NN).astype(bf16)
    rows_ref[:, width:] = (gate * mxu(pick, g_ref[...], NN)).astype(bf16)


def pack_rows(id_rows, gate_rows, tokens, out_grad, expert_count, capacity):
    tok_count, width = tokens.shape
    slots = expert_count * capacity
    return pl.pallas_call(
        functools.partial(pack_kernel, expert_count, capacity),
        out_shape=(
            jax.ShapeDtypeStruct((slots, 2 * width), bf16),
            jax.ShapeDtypeStruct((2, tok_count), jnp.int32),
        ),
        name="pack_rows",
    )(id_rows, gate_rows, tokens, out_grad)


def pre_block(block, w_in, w_out):
    width = block.shape[1] // 2
    pre_act = mxu(block[:, :width], w_in, NN)
    act_grad = mxu(block[:, width:], w_out, NT)
    return (act_grad * gelu_slope(pre_act)).astype(bf16)


def pre_tile(rows, w_in, w_out, pre_ref):
    per = rows[0].shape[0]
    for b, block in enumerate(rows):
        pre_ref[b * per : (b + 1) * per, :] = pre_block(block, w_in, w_out)


def own_kernel(rows_ref, w_in_ref, w_out_ref, pre_ref, xt_ref):
    xt_ref[...] = rows_ref[:, : xt_ref.shape[0]].T
    pre_ref[...] = pre_block(rows_ref, w_in_ref[...], w_out_ref[...])


def own_step(rows, w_in, w_out, tile):
    per, width = rows.shape[0], rows.shape[1] // 2
    corner = lambda i: (0, 0)
    return pl.pallas_call(
        own_kernel,
        grid=(1,),
        in_specs=[
            pl.BlockSpec(rows.shape, corner),
            pl.BlockSpec((width, tile), corner),
            pl.BlockSpec((tile, width), corner),
        ],
        out_specs=[pl.BlockSpec((per, tile), corner), pl.BlockSpec((width, per), corner)],
        out_shape=[
            jax.ShapeDtypeStruct((per, tile), bf16),
            jax.ShapeDtypeStruct((width, per), bf16),
        ],
        compiler_params=pltpu.CompilerParams(vmem_limit_bytes=48 * MIB),
        cost_estimate=pl.CostEstimate(
            flops=4 * per * width * tile, bytes_accessed=4 * tile * width, transcendentals=0
        ),
        name="own_step",
    )(rows, w_in, w_out)


def first_kernel(others, *refs):
    rows = refs[:others]
    pre_own, xt_own, w_in_ref, w_out_ref, m_ref, v_ref, adam_ref, pre_ref, xt_ref = refs[
        others : others + 9
    ]
    m_buf, v_buf, pre_buf, xt_buf, sems = refs[others + 9 :]
    width, tile = m_buf.shape
    per = xt_own.shape[1]
    gets = [
        pltpu.make_async_copy(array.at[:, pl.ds(0, tile)], buf, sems.at[n])
        for n, (array, buf) in enumerate(((m_ref, m_buf), (v_ref, v_buf)))
    ]
    for get in gets:
        get.start()
    xt_buf[:, :per] = xt_own[...]
    pre_buf[:per, :] = pre_own[...]
    for b in range(others):
        part = slice((b + 1) * per, (b + 2) * per)
        xt_buf[:, part] = rows[b][:, :width].T
        pre_buf[part, :] = pre_block(rows[b], w_in_ref[...], w_out_ref[...])
    puts = [
        pltpu.make_async_copy(xt_buf, xt_ref, sems.at[2]),
        pltpu.make_async_copy(pre_buf, pre_ref, sems.at[3]),
    ]
    for put in puts:
        put.start()
    weight_grad = mxu(xt_buf[...], pre_buf[...], NN)
    for get in gets:
        get.wait()
    adam_ref[...] = adam_step(weight_grad, m_buf[...], v_buf[...])
    for put in puts:
        put.wait()


def first_step(rows, pre_own, xt_own, w_in, w_out, first_moment, second_moment, tile):
    width, per = xt_own.shape
    total = (len(rows) + 1) * per
    corner = lambda i: (0, 0)
    anywhere = pl.BlockSpec(memory_space=pl.ANY)
    return pl.pallas_call(
        functools.partial(first_kernel, len(rows)),
        grid=(1,),
        in_specs=[pl.BlockSpec(r.shape, corner) for r in rows]
        + [
            pl.BlockSpec((per, tile), corner),
            pl.BlockSpec((width, per), corner),
            pl.BlockSpec((width, tile), corner),
            pl.BlockSpec((tile, width), corner),
            anywhere,
            anywhere,
        ],
        out_specs=[pl.BlockSpec((width, tile), corner), anywhere, anywhere],
        out_shape=[
            jax.ShapeDtypeStruct((width, tile), bf16),
            jax.ShapeDtypeStruct((total, tile), bf16),
            jax.ShapeDtypeStruct((width, total), bf16),
        ],
        scratch_shapes=[
            pltpu.VMEM((width, tile), f32),
            pltpu.VMEM((width, tile), f32),
            pltpu.VMEM((total, tile), bf16),
            pltpu.VMEM((width, total), bf16),
            pltpu.SemaphoreType.DMA((4,)),
        ],
        compiler_params=pltpu.CompilerParams(vmem_limit_bytes=56 * MIB),
        cost_estimate=pl.CostEstimate(
            flops=6 * total * width * tile, bytes_accessed=14 * tile * width, transcendentals=0
        ),
        name="first_step",
    )(*rows, pre_own, xt_own, w_in, w_out, first_moment, second_moment)


def rest_kernel(blocks, *refs):
    rows = refs[:blocks]
    first_ref, w_first_ref, w_in_ref, w_out_ref, pre_ref = refs[blocks : blocks + 5]
    parts = refs[blocks + 5 : -1]
    total_ref = refs[-1]
    per = rows[0].shape[0]
    step = pl.program_id(0)

    @pl.when(step == 0)
    def _():
        total_ref[...] = mxu(first_ref[...], w_first_ref[...], NT)

    pre_tile(rows, w_in_ref[...], w_out_ref[...], pre_ref)
    total_ref[...] += mxu(pre_ref[...], w_in_ref[...], NT)

    @pl.when(step == pl.num_programs(0) - 1)
    def _():
        for b in range(blocks):
            parts[b][...] = total_ref[b * per : (b + 1) * per, :].astype(bf16)


def rest_step(rows, pre_first, w_in, w_out, tile):
    per, width = rows[0].shape[0], rows[0].shape[1] // 2
    total = len(rows) * per
    tiles = w_in.shape[1] // tile - 1
    corner = lambda j: (0, 0)
    return pl.pallas_call(
        functools.partial(rest_kernel, len(rows)),
        grid=(tiles,),
        in_specs=[pl.BlockSpec(r.shape, corner) for r in rows]
        + [
            pl.BlockSpec((total, tile), corner),
            pl.BlockSpec((width, tile), corner),
            pl.BlockSpec((width, tile), lambda j: (0, j + 1)),
            pl.BlockSpec((tile, width), lambda j: (j + 1, 0)),
        ],
        out_specs=[pl.BlockSpec((total, tile), lambda j: (0, j))]
        + [pl.BlockSpec((per, width), corner) for _ in rows],
        out_shape=[jax.ShapeDtypeStruct((total, tiles * tile), bf16)]
        + [jax.ShapeDtypeStruct((per, width), bf16) for _ in rows],
        scratch_shapes=[pltpu.VMEM((total, width), f32)],
        compiler_params=pltpu.CompilerParams(vmem_limit_bytes=56 * MIB),
        cost_estimate=pl.CostEstimate(
            flops=6 * total * width * tile * tiles,
            bytes_accessed=4 * tile * width * tiles,
            transcendentals=0,
        ),
        name="rest_step",
    )(*rows, pre_first, w_in, w_in, w_out)


def adam_kernel(xt_ref, pre_ref, m_ref, v_ref, out_ref):
    weight_grad = mxu(xt_ref[...], pre_ref[...], NN)
    out_ref[...] = adam_step(weight_grad, m_ref[...], v_ref[...])


def adam_block(x_t, pre_rest, first_moment, second_moment, start, tiles, tile, part, parts):
    width, total = x_t.shape
    rows = width // parts
    block = pl.BlockSpec((rows, tile), lambda j: (part, start + j))
    return pl.pallas_call(
        adam_kernel,
        grid=(tiles,),
        in_specs=[
            pl.BlockSpec((rows, total), lambda j: (part, 0)),
            pl.BlockSpec((total, tile), lambda j: (0, start - 1 + j)),
            block,
            block,
        ],
        out_specs=pl.BlockSpec((rows, tile), lambda j: (0, j)),
        out_shape=jax.ShapeDtypeStruct((rows, tiles * tile), bf16),
        compiler_params=pltpu.CompilerParams(vmem_limit_bytes=60 * MIB),
        cost_estimate=pl.CostEstimate(
            flops=2 * total * rows * tile * tiles,
            bytes_accessed=10 * tile * rows * tiles,
            transcendentals=0,
        ),
    )(x_t, pre_rest, first_moment, second_moment)


def place_kernel(boxes, source_ref, *refs):
    sources, at = [], 0
    for box in boxes:
        sources.append(refs[at : at + box[5]])
        at += box[5]
    out_ref = refs[at]
    bufs = refs[at + 1 : at + 1 + len(boxes)]
    in_sem, out_sem = refs[at + 1 + len(boxes) :]
    most = max(len(arrays) for arrays in sources)
    for k in range(most):

        @pl.when(source_ref[0] == k)
        def _(k=k):
            for n, arrays in enumerate(sources):
                array = arrays[min(k, len(arrays) - 1)]
                start, high = boxes[n][2], boxes[n][3]
                pltpu.make_async_copy(
                    array.at[pl.ds(start, high)], bufs[n], in_sem.at[n]
                ).start()

    puts = []
    for n, (row, col, start, high, wide, _) in enumerate(boxes):
        pltpu.make_async_copy(
            sources[n][0].at[pl.ds(start, high)], bufs[n], in_sem.at[n]
        ).wait()
        put = pltpu.make_async_copy(
            bufs[n], out_ref.at[pl.ds(row + start, high), pl.ds(col, wide)], out_sem.at[n]
        )
        put.start()
        puts.append(put)
    for put in puts:
        put.wait()


def place(source, pieces, width, inner):
    boxes = [piece[:5] + (len(piece[5]),) for piece in pieces]
    args = [array for piece in pieces for array in piece[5]]
    return pl.pallas_call(
        functools.partial(place_kernel, boxes),
        in_specs=[pl.BlockSpec(memory_space=pltpu.SMEM)]
        + [pl.BlockSpec(memory_space=pl.ANY) for _ in args],
        out_specs=pl.BlockSpec(memory_space=pl.ANY),
        out_shape=jax.ShapeDtypeStruct((width, inner), bf16),
        scratch_shapes=[pltpu.VMEM((box[3], box[4]), bf16) for box in boxes]
        + [pltpu.SemaphoreType.DMA((len(boxes),)), pltpu.SemaphoreType.DMA((len(boxes),))],
        compiler_params=pltpu.CompilerParams(vmem_limit_bytes=8 * MIB),
        cost_estimate=pl.CostEstimate(
            flops=0, bytes_accessed=4 * width * inner, transcendentals=0
        ),
        name="place",
    )(source, *args)


def swap_plans(half):
    line = half >> 1
    groups = {}
    for e in range(half):
        groups.setdefault(e & ~(line | 1), []).append(e)
    groups = list(groups.values())
    if half < 4 or len(groups) > 2:
        return []
    forced = {0, half - 1}
    switches = []
    for members in groups:
        must = forced & set(members)
        plans = [
            set(s)
            for k in range(2, len(members) + 1)
            for s in itertools.combinations(members, k)
            if must <= set(s)
        ]
        table = []
        for mask in range(1 << half):
            moved = must | {e for e in members if mask >> e & 1}
            table.append(next(n for n, plan in enumerate(plans) if moved <= plan))
        switches.append((plans, table))
    return switches


def combine_kernel(where_ref, back_ref, out_ref):
    slots, tok_count = back_ref.shape[0], out_ref.shape[0]
    row = lax.broadcasted_iota(jnp.int32, (slots, tok_count), 0)
    pick = (row == where_ref[0:1, :]) | (row == where_ref[1:2, :])
    pick = jnp.where(pick, 1.0, 0.0).astype(bf16)
    out_ref[...] = mxu(pick, back_ref[...], TN).astype(bf16)


def combine_rows(where_to, returned, tok_count):
    return pl.pallas_call(
        combine_kernel,
        out_shape=jax.ShapeDtypeStruct((tok_count, returned.shape[1]), bf16),
        name="combine_rows",
    )(where_to, returned)


def dp_shift(block, apart):
    count = lax.axis_size("dp")
    return lax.ppermute(block, "dp", [(i, i ^ apart) for i in range(count)])


def shards(
    tokens, out_grad, gates, expert_ids, swap_list, w_in, w_out, first_moment, second_moment
):
    expert_count = lax.axis_size("expert")
    dp_count = lax.axis_size("dp")
    half = 1 << (expert_count.bit_length() - 2)
    own_index = lax.axis_index("expert")
    lane_ids = jnp.arange(expert_count, dtype=jnp.int32)
    partner_me = jnp.sum(jnp.where(lane_ids == own_index, swap_list, 0))
    is_moved = (partner_me != own_index).astype(jnp.int32)
    moved_bits = jnp.where((swap_list != lane_ids) & (lane_ids < half), 1 << lane_ids, 0)
    moved_mask = jnp.sum(moved_bits)
    tok_count, width = tokens.shape
    capacity = 3 * tok_count // expert_count
    slots = expert_count * capacity

    rows, where_to = pack_rows(expert_ids.T, gates.T, tokens, out_grad, expert_count, capacity)
    own = lax.all_to_all(
        rows.reshape(expert_count, capacity, 2 * width),
        "expert",
        split_axis=0,
        concat_axis=0,
        tiled=True,
    ).reshape(slots, 2 * width)
    all_rows = [own] + [dp_shift(own, d) for d in range(1, dp_count)]
    if dp_count == 2:
        all_rows = [pltpu.with_memory_space_constraint(r, pltpu.VMEM) for r in all_rows]

    inner = w_in.shape[2]
    tile = 256 if inner % 256 == 0 else 128
    tiles = inner // tile
    route = [(e, e ^ half) for e in range(expert_count)]
    across = [(e, e ^ 1) for e in range(expert_count)]

    pre_own, xt_own = own_step(all_rows[0], w_in[0], w_out[0], tile)
    if dp_count == 2:
        pre_own = pltpu.with_memory_space_constraint(pre_own, pltpu.VMEM)
        xt_own = pltpu.with_memory_space_constraint(xt_own, pltpu.VMEM)
    first, pre_first, x_t = first_step(
        all_rows[1:], pre_own, xt_own, w_in[0], w_out[0], first_moment[0], second_moment[0], tile
    )
    first_got = lax.ppermute(first, "expert", route)
    pieces = [(0, 0, width, tile, [first, first_got])]

    pre_rest, *parts = rest_step(all_rows, pre_first, w_in[0], w_out[0], tile)
    total = parts[0].astype(f32)
    for d in range(1, dp_count):
        total = total + dp_shift(parts[d], d).astype(f32)
    returned = lax.all_to_all(
        total.astype(bf16).reshape(expert_count, capacity, width),
        "expert",
        split_axis=0,
        concat_axis=0,
        tiled=True,
    ).reshape(slots, width)

    x_grad = combine_rows(where_to, returned, tok_count)
    switches = swap_plans(half) if tiles > 2 else []
    direct = 1 if switches else tiles - 1
    moments = (first_moment[0], second_moment[0])
    second = adam_block(x_t, pre_rest, *moments, 1, direct, tile, 0, 1)
    second_got = lax.ppermute(second, "expert", route)
    pieces.append((0, tile, width, direct * tile, [second, second_got]))
    group = jnp.zeros((), jnp.int32)

    if switches:
        at, left = 1 + direct, tiles - 1 - direct
        far = adam_block(x_t, pre_rest, *moments, at, left, tile, 1, 2)
        lent = lax.ppermute(far, "expert", across)
        near = adam_block(x_t, pre_rest, *moments, at, left, tile, 0, 2)

        def branch(plan):
            pairs = [(e, e ^ half) for p in plan for e in (p, p ^ half)]
            skew = [(e ^ 1, f) for e, f in pairs]

            def run(near, lent):
                return (
                    lax.ppermute(near, "expert", pairs),
                    lax.ppermute(lent, "expert", skew),
                )

            return run

        near, lent, x_grad = lax.optimization_barrier((near, lent, x_grad))
        near_all, far_all = [near], [far]
        for n, (plans, table) in enumerate(switches):
            choice = jnp.asarray(table, jnp.int32)[moved_mask]
            near_got, far_got = lax.switch(choice, [branch(p) for p in plans], near, lent)
            near_all.append(near_got)
            far_all.append(far_got)
            members = {e for plan in plans for p in plan for e in (p, p ^ half)}
            here = jnp.asarray([e in members for e in range(expert_count)])
            group += jnp.sum(jnp.where(here & (lane_ids == own_index), n, 0))
        wide = left * tile
        pieces.append((0, at * tile, width // 2, wide, near_all))
        pieces.append((width // 2, at * tile, width // 2, wide, far_all))

    source = (is_moved * (1 + group)).reshape(1)
    cut = []
    for row, col, high, wide, arrays in pieces:
        step = width
        for at in range(0, high, step):
            cut.append((row, col, at, min(step, high - at), wide, arrays))
    adam_out = place(source, cut, width, inner)
    return (x_grad, adam_out[None])


def solution(mesh):
    in_specs = (
        P(("dp", "expert"), None),
        P(("dp", "expert"), None),
        P(("dp", "expert"), None),
        P(("dp", "expert"), None),
        P(),
        P("expert", None, "dp"),
        P("expert", "dp", None),
        P("expert", None, "dp"),
        P("expert", None, "dp"),
    )
    out_specs = (P(("dp", "expert"), None), P("expert", None, "dp"))

    return jax.shard_map(shards, mesh=mesh, in_specs=in_specs, out_specs=out_specs, check_vma=False)
```

```python
import functools
import itertools

import jax
import jax.numpy as jnp
from jax import lax
from jax.experimental import pallas as pl
from jax.experimental.pallas import tpu as pltpu
from jax.sharding import PartitionSpec as P


ADAM_STEP = 100


coef_c = 0.7978845608028654
coef_a = 0.044715
beta_one = 0.9
beta_two = 0.999
adam_eps = 1e-08


MIB = 2**20

f32 = jnp.float32
bf16 = jnp.bfloat16
NN = (((1,), (0,)), ((), ()))
NT = (((1,), (1,)), ((), ()))
TN = (((0,), (0,)), ((), ()))


def mxu(a, b, dims):
    return lax.dot_general(a, b, dims, preferred_element_type=f32)


def gelu_slope(pre_act):
    square = pre_act * pre_act
    tanh_val = jnp.tanh(pre_act * (coef_c + coef_c * coef_a * square))
    bend = pre_act * (coef_c + 3.0 * coef_c * coef_a * square)
    return 0.5 + 0.5 * (tanh_val + bend * (1.0 - tanh_val * tanh_val))


def adam_step(weight_grad, first_moment, second_moment):
    unbias_one = 1.0 / (1.0 - beta_one**ADAM_STEP)
    unbias_two = 1.0 / (1.0 - beta_two**ADAM_STEP)
    first_hat = (beta_one * unbias_one) * first_moment + ((1.0 - beta_one) * unbias_one) * weight_grad
    second_hat = (beta_two * unbias_two) * second_moment + (
        (1.0 - beta_two) * unbias_two
    ) * (weight_grad * weight_grad)
    root = second_hat * lax.rsqrt(second_hat)
    return (first_hat / (root + adam_eps)).astype(bf16)


def pack_kernel(expert_count, capacity, ids_ref, gates_ref, x_ref, g_ref, rows_ref, where_ref):
    tok_count, width = x_ref.shape
    slots = expert_count * capacity
    first = ids_ref[0:1, :]
    second = ids_ref[1:2, :]
    experts = lax.broadcasted_iota(jnp.int32, (expert_count, tok_count), 0)
    hit_first = experts == first
    hit_second = experts == second
    hits = jnp.where(hit_first | hit_second, 1.0, 0.0).astype(bf16)
    earlier = lax.broadcasted_iota(jnp.int32, (tok_count, tok_count), 0)
    later = lax.broadcasted_iota(jnp.int32, (tok_count, tok_count), 1)
    upper = jnp.where(earlier < later, 1.0, 0.0).astype(bf16)
    before = mxu(hits, upper, NN)
    slot_first = jnp.sum(jnp.where(hit_first, before, 0.0), axis=0, keepdims=True)
    slot_second = jnp.sum(jnp.where(hit_second, before, 0.0), axis=0, keepdims=True)
    pos_first = first * capacity + slot_first.astype(jnp.int32)
    pos_second = second * capacity + slot_second.astype(jnp.int32)
    where_ref[0:1, :] = pos_first
    where_ref[1:2, :] = pos_second
    row = lax.broadcasted_iota(jnp.int32, (slots, tok_count), 0)
    at_first = row == pos_first
    at_second = row == pos_second
    pick = jnp.where(at_first | at_second, 1.0, 0.0).astype(bf16)
    gate = jnp.sum(
        jnp.where(at_first, gates_ref[0:1, :], 0.0) + jnp.where(at_second, gates_ref[1:2, :], 0.0),
        axis=1,
        keepdims=True,
    )
    rows_ref[:, :width] = mxu(pick, x_ref[...], NN).astype(bf16)
    rows_ref[:, width:] = (gate * mxu(pick, g_ref[...], NN)).astype(bf16)


def pack_rows(id_rows, gate_rows, tokens, out_grad, expert_count, capacity):
    tok_count, width = tokens.shape
    slots = expert_count * capacity
    return pl.pallas_call(
        functools.partial(pack_kernel, expert_count, capacity),
        out_shape=(
            jax.ShapeDtypeStruct((slots, 2 * width), bf16),
            jax.ShapeDtypeStruct((2, tok_count), jnp.int32),
        ),
        name="pack_rows",
    )(id_rows, gate_rows, tokens, out_grad)


def pre_block(block, w_in, w_out):
    width = block.shape[1] // 2
    pre_act = mxu(block[:, :width], w_in, NN)
    act_grad = mxu(block[:, width:], w_out, NT)
    return (act_grad * gelu_slope(pre_act)).astype(bf16)


def pre_tile(rows, w_in, w_out, pre_ref):
    per = rows[0].shape[0]
    for b, block in enumerate(rows):
        pre_ref[b * per : (b + 1) * per, :] = pre_block(block, w_in, w_out)


def own_kernel(rows_ref, w_in_ref, w_out_ref, pre_ref, xt_ref, w_in_buf, w_out_buf, sems):
    tile = pre_ref.shape[1]
    gets = [
        pltpu.make_async_copy(w_in_ref.at[:, pl.ds(0, tile)], w_in_buf, sems.at[0]),
        pltpu.make_async_copy(w_out_ref.at[pl.ds(0, tile), :], w_out_buf, sems.at[1]),
    ]
    for get in gets:
        get.start()
    xt_ref[...] = rows_ref[:, : xt_ref.shape[0]].T
    for get in gets:
        get.wait()
    pre_ref[...] = pre_block(rows_ref, w_in_buf[...], w_out_buf[...])


def own_step(rows, w_in, w_out, tile):
    per, width = rows.shape[0], rows.shape[1] // 2
    vmem = pl.BlockSpec(memory_space=pltpu.VMEM)
    anywhere = pl.BlockSpec(memory_space=pl.ANY)
    return pl.pallas_call(
        own_kernel,
        in_specs=[vmem, anywhere, anywhere],
        out_specs=[vmem, vmem],
        out_shape=[
            jax.ShapeDtypeStruct((per, tile), bf16),
            jax.ShapeDtypeStruct((width, per), bf16),
        ],
        scratch_shapes=[
            pltpu.VMEM((width, tile), bf16),
            pltpu.VMEM((tile, width), bf16),
            pltpu.SemaphoreType.DMA((2,)),
        ],
        compiler_params=pltpu.CompilerParams(vmem_limit_bytes=48 * MIB),
        cost_estimate=pl.CostEstimate(
            flops=4 * per * width * tile, bytes_accessed=4 * tile * width, transcendentals=0
        ),
        name="own_step",
    )(rows, w_in, w_out)


def first_kernel(others, *refs):
    rows = refs[:others]
    pre_own, xt_own, w_in_ref, w_out_ref, m_ref, v_ref, adam_ref, pre_ref, xt_ref = refs[
        others : others + 9
    ]
    w_in_buf, w_out_buf, m_buf, v_buf, pre_buf, xt_buf, sems = refs[others + 9 :]
    width, tile = m_buf.shape
    per = xt_own.shape[1]
    gets = [
        pltpu.make_async_copy(w_in_ref.at[:, pl.ds(0, tile)], w_in_buf, sems.at[0]),
        pltpu.make_async_copy(w_out_ref.at[pl.ds(0, tile), :], w_out_buf, sems.at[1]),
        pltpu.make_async_copy(m_ref.at[:, pl.ds(0, tile)], m_buf, sems.at[2]),
        pltpu.make_async_copy(v_ref.at[:, pl.ds(0, tile)], v_buf, sems.at[3]),
    ]
    for get in gets:
        get.start()
    xt_buf[:, :per] = xt_own[...]
    pre_buf[:per, :] = pre_own[...]
    for b in range(others):
        xt_buf[:, (b + 1) * per : (b + 2) * per] = rows[b][:, :width].T
    for get in gets[:2]:
        get.wait()
    for b in range(others):
        pre_buf[(b + 1) * per : (b + 2) * per, :] = pre_block(
            rows[b], w_in_buf[...], w_out_buf[...]
        )
    puts = [
        pltpu.make_async_copy(xt_buf, xt_ref, sems.at[4]),
        pltpu.make_async_copy(pre_buf, pre_ref, sems.at[5]),
    ]
    for put in puts:
        put.start()
    weight_grad = mxu(xt_buf[...], pre_buf[...], NN)
    for get in gets[2:]:
        get.wait()
    adam_ref[...] = adam_step(weight_grad, m_buf[...], v_buf[...])
    for put in puts:
        put.wait()


def first_step(rows, pre_own, xt_own, w_in, w_out, first_moment, second_moment, tile):
    width, per = xt_own.shape
    total = (len(rows) + 1) * per
    vmem = pl.BlockSpec(memory_space=pltpu.VMEM)
    anywhere = pl.BlockSpec(memory_space=pl.ANY)
    return pl.pallas_call(
        functools.partial(first_kernel, len(rows)),
        in_specs=[vmem] * (len(rows) + 2) + [anywhere] * 4,
        out_specs=[vmem, anywhere, anywhere],
        out_shape=[
            jax.ShapeDtypeStruct((width, tile), bf16),
            jax.ShapeDtypeStruct((total, tile), bf16),
            jax.ShapeDtypeStruct((width, total), bf16),
        ],
        scratch_shapes=[
            pltpu.VMEM((width, tile), bf16),
            pltpu.VMEM((tile, width), bf16),
            pltpu.VMEM((width, tile), f32),
            pltpu.VMEM((width, tile), f32),
            pltpu.VMEM((total, tile), bf16),
            pltpu.VMEM((width, total), bf16),
            pltpu.SemaphoreType.DMA((6,)),
        ],
        compiler_params=pltpu.CompilerParams(vmem_limit_bytes=56 * MIB),
        cost_estimate=pl.CostEstimate(
            flops=6 * total * width * tile, bytes_accessed=14 * tile * width, transcendentals=0
        ),
        name="first_step",
    )(*rows, pre_own, xt_own, w_in, w_out, first_moment, second_moment)


def rest_kernel(blocks, *refs):
    rows = refs[:blocks]
    first_ref, w_first_ref, w_in_ref, w_out_ref, pre_ref = refs[blocks : blocks + 5]
    parts = refs[blocks + 5 : -1]
    total_ref = refs[-1]
    per = rows[0].shape[0]
    step = pl.program_id(0)

    @pl.when(step == 0)
    def _():
        total_ref[...] = mxu(first_ref[...], w_first_ref[...], NT)

    pre_tile(rows, w_in_ref[...], w_out_ref[...], pre_ref)
    total_ref[...] += mxu(pre_ref[...], w_in_ref[...], NT)

    @pl.when(step == pl.num_programs(0) - 1)
    def _():
        for b in range(blocks):
            parts[b][...] = total_ref[b * per : (b + 1) * per, :].astype(bf16)


def rest_step(rows, pre_first, w_in, w_out, tile):
    per, width = rows[0].shape[0], rows[0].shape[1] // 2
    total = len(rows) * per
    tiles = w_in.shape[1] // tile - 1
    corner = lambda j: (0, 0)
    return pl.pallas_call(
        functools.partial(rest_kernel, len(rows)),
        grid=(tiles,),
        in_specs=[pl.BlockSpec(r.shape, corner) for r in rows]
        + [
            pl.BlockSpec((total, tile), corner),
            pl.BlockSpec((width, tile), corner),
            pl.BlockSpec((width, tile), lambda j: (0, j + 1)),
            pl.BlockSpec((tile, width), lambda j: (j + 1, 0)),
        ],
        out_specs=[pl.BlockSpec((total, tile), lambda j: (0, j))]
        + [pl.BlockSpec((per, width), corner) for _ in rows],
        out_shape=[jax.ShapeDtypeStruct((total, tiles * tile), bf16)]
        + [jax.ShapeDtypeStruct((per, width), bf16) for _ in rows],
        scratch_shapes=[pltpu.VMEM((total, width), f32)],
        compiler_params=pltpu.CompilerParams(vmem_limit_bytes=56 * MIB),
        cost_estimate=pl.CostEstimate(
            flops=6 * total * width * tile * tiles,
            bytes_accessed=4 * tile * width * tiles,
            transcendentals=0,
        ),
        name="rest_step",
    )(*rows, pre_first, w_in, w_in, w_out)


def adam_kernel(xt_ref, pre_ref, m_ref, v_ref, out_ref):
    weight_grad = mxu(xt_ref[...], pre_ref[...], NN)
    out_ref[...] = adam_step(weight_grad, m_ref[...], v_ref[...])


def adam_block(x_t, pre_rest, first_moment, second_moment, start, tiles, tile, part, parts):
    width, total = x_t.shape
    rows = width // parts
    block = pl.BlockSpec((rows, tile), lambda j: (part, start + j))
    return pl.pallas_call(
        adam_kernel,
        grid=(tiles,),
        in_specs=[
            pl.BlockSpec((rows, total), lambda j: (part, 0)),
            pl.BlockSpec((total, tile), lambda j: (0, start - 1 + j)),
            block,
            block,
        ],
        out_specs=pl.BlockSpec((rows, tile), lambda j: (0, j)),
        out_shape=jax.ShapeDtypeStruct((rows, tiles * tile), bf16),
        compiler_params=pltpu.CompilerParams(vmem_limit_bytes=60 * MIB),
        cost_estimate=pl.CostEstimate(
            flops=2 * total * rows * tile * tiles,
            bytes_accessed=10 * tile * rows * tiles,
            transcendentals=0,
        ),
    )(x_t, pre_rest, first_moment, second_moment)


def place_kernel(boxes, source_ref, *refs):
    sources, at = [], 0
    for box in boxes:
        sources.append(refs[at : at + box[5]])
        at += box[5]
    out_ref = refs[at]
    bufs = refs[at + 1 : at + 1 + len(boxes)]
    in_sem, out_sem = refs[at + 1 + len(boxes) :]
    most = max(len(arrays) for arrays in sources)
    for k in range(most):

        @pl.when(source_ref[0] == k)
        def _(k=k):
            for n, arrays in enumerate(sources):
                array = arrays[min(k, len(arrays) - 1)]
                start, high = boxes[n][2], boxes[n][3]
                pltpu.make_async_copy(
                    array.at[pl.ds(start, high)], bufs[n], in_sem.at[n]
                ).start()

    puts = []
    for n, (row, col, start, high, wide, _) in enumerate(boxes):
        pltpu.make_async_copy(
            sources[n][0].at[pl.ds(start, high)], bufs[n], in_sem.at[n]
        ).wait()
        put = pltpu.make_async_copy(
            bufs[n], out_ref.at[pl.ds(row + start, high), pl.ds(col, wide)], out_sem.at[n]
        )
        put.start()
        puts.append(put)
    for put in puts:
        put.wait()


def place(source, pieces, width, inner):
    boxes = [piece[:5] + (len(piece[5]),) for piece in pieces]
    args = [array for piece in pieces for array in piece[5]]
    return pl.pallas_call(
        functools.partial(place_kernel, boxes),
        in_specs=[pl.BlockSpec(memory_space=pltpu.SMEM)]
        + [pl.BlockSpec(memory_space=pl.ANY) for _ in args],
        out_specs=pl.BlockSpec(memory_space=pl.ANY),
        out_shape=jax.ShapeDtypeStruct((width, inner), bf16),
        scratch_shapes=[pltpu.VMEM((box[3], box[4]), bf16) for box in boxes]
        + [pltpu.SemaphoreType.DMA((len(boxes),)), pltpu.SemaphoreType.DMA((len(boxes),))],
        compiler_params=pltpu.CompilerParams(vmem_limit_bytes=8 * MIB),
        cost_estimate=pl.CostEstimate(
            flops=0, bytes_accessed=4 * width * inner, transcendentals=0
        ),
        name="place",
    )(source, *args)


def swap_plans(half):
    line = half >> 1
    groups = {}
    for e in range(half):
        groups.setdefault(e & ~(line | 1), []).append(e)
    groups = list(groups.values())
    if half < 4 or len(groups) > 2:
        return []
    forced = {0, half - 1}
    switches = []
    for members in groups:
        must = forced & set(members)
        plans = [
            set(s)
            for k in range(2, len(members) + 1)
            for s in itertools.combinations(members, k)
            if must <= set(s)
        ]
        table = []
        for mask in range(1 << half):
            moved = must | {e for e in members if mask >> e & 1}
            table.append(next(n for n, plan in enumerate(plans) if moved <= plan))
        switches.append((plans, table))
    return switches


def combine_kernel(where_ref, back_ref, out_ref):
    slots, tok_count = back_ref.shape[0], out_ref.shape[0]
    row = lax.broadcasted_iota(jnp.int32, (slots, tok_count), 0)
    pick = (row == where_ref[0:1, :]) | (row == where_ref[1:2, :])
    pick = jnp.where(pick, 1.0, 0.0).astype(bf16)
    out_ref[...] = mxu(pick, back_ref[...], TN).astype(bf16)


def combine_rows(where_to, returned, tok_count):
    return pl.pallas_call(
        combine_kernel,
        out_shape=jax.ShapeDtypeStruct((tok_count, returned.shape[1]), bf16),
        name="combine_rows",
    )(where_to, returned)


def dp_shift(block, apart):
    count = lax.axis_size("dp")
    return lax.ppermute(block, "dp", [(i, i ^ apart) for i in range(count)])


def shards(
    tokens, out_grad, gates, expert_ids, swap_list, w_in, w_out, first_moment, second_moment
):
    expert_count = lax.axis_size("expert")
    dp_count = lax.axis_size("dp")
    half = 1 << (expert_count.bit_length() - 2)
    own_index = lax.axis_index("expert")
    lane_ids = jnp.arange(expert_count, dtype=jnp.int32)
    partner_me = jnp.sum(jnp.where(lane_ids == own_index, swap_list, 0))
    is_moved = (partner_me != own_index).astype(jnp.int32)
    moved_bits = jnp.where((swap_list != lane_ids) & (lane_ids < half), 1 << lane_ids, 0)
    moved_mask = jnp.sum(moved_bits)
    tok_count, width = tokens.shape
    capacity = 3 * tok_count // expert_count
    slots = expert_count * capacity

    rows, where_to = pack_rows(expert_ids.T, gates.T, tokens, out_grad, expert_count, capacity)
    own = lax.all_to_all(
        rows.reshape(expert_count, capacity, 2 * width),
        "expert",
        split_axis=0,
        concat_axis=0,
        tiled=True,
    ).reshape(slots, 2 * width)
    all_rows = [own] + [dp_shift(own, d) for d in range(1, dp_count)]
    if dp_count == 2:
        all_rows = [pltpu.with_memory_space_constraint(r, pltpu.VMEM) for r in all_rows]

    inner = w_in.shape[2]
    tile = 256 if inner % 256 == 0 else 128
    tiles = inner // tile
    route = [(e, e ^ half) for e in range(expert_count)]
    across = [(e, e ^ 1) for e in range(expert_count)]

    pre_own, xt_own = own_step(all_rows[0], w_in[0], w_out[0], tile)
    if dp_count == 2:
        pre_own = pltpu.with_memory_space_constraint(pre_own, pltpu.VMEM)
        xt_own = pltpu.with_memory_space_constraint(xt_own, pltpu.VMEM)
    first, pre_first, x_t = first_step(
        all_rows[1:], pre_own, xt_own, w_in[0], w_out[0], first_moment[0], second_moment[0], tile
    )
    first_got = lax.ppermute(first, "expert", route)
    pieces = [(0, 0, width, tile, [first, first_got])]

    pre_rest, *parts = rest_step(all_rows, pre_first, w_in[0], w_out[0], tile)
    total = parts[0].astype(f32)
    for d in range(1, dp_count):
        total = total + dp_shift(parts[d], d).astype(f32)
    returned = lax.all_to_all(
        total.astype(bf16).reshape(expert_count, capacity, width),
        "expert",
        split_axis=0,
        concat_axis=0,
        tiled=True,
    ).reshape(slots, width)

    x_grad = combine_rows(where_to, returned, tok_count)
    switches = swap_plans(half) if tiles > 2 else []
    direct = 1 if switches else tiles - 1
    moments = (first_moment[0], second_moment[0])
    second = adam_block(x_t, pre_rest, *moments, 1, direct, tile, 0, 1)
    second_got = lax.ppermute(second, "expert", route)
    pieces.append((0, tile, width, direct * tile, [second, second_got]))
    group = jnp.zeros((), jnp.int32)

    if switches:
        at, left = 1 + direct, tiles - 1 - direct
        far = adam_block(x_t, pre_rest, *moments, at, left, tile, 1, 2)
        lent = lax.ppermute(far, "expert", across)
        near = adam_block(x_t, pre_rest, *moments, at, left, tile, 0, 2)

        def branch(plan):
            pairs = [(e, e ^ half) for p in plan for e in (p, p ^ half)]
            skew = [(e ^ 1, f) for e, f in pairs]

            def run(near, lent):
                return (
                    lax.ppermute(near, "expert", pairs),
                    lax.ppermute(lent, "expert", skew),
                )

            return run

        near, lent, x_grad = lax.optimization_barrier((near, lent, x_grad))
        near_all, far_all = [near], [far]
        for n, (plans, table) in enumerate(switches):
            choice = jnp.asarray(table, jnp.int32)[moved_mask]
            near_got, far_got = lax.switch(choice, [branch(p) for p in plans], near, lent)
            near_all.append(near_got)
            far_all.append(far_got)
            members = {e for plan in plans for p in plan for e in (p, p ^ half)}
            here = jnp.asarray([e in members for e in range(expert_count)])
            group += jnp.sum(jnp.where(here & (lane_ids == own_index), n, 0))
        wide = left * tile
        pieces.append((0, at * tile, width // 2, wide, near_all))
        pieces.append((width // 2, at * tile, width // 2, wide, far_all))

    source = (is_moved * (1 + group)).reshape(1)
    cut = []
    for row, col, high, wide, arrays in pieces:
        step = width
        for at in range(0, high, step):
            cut.append((row, col, at, min(step, high - at), wide, arrays))
    adam_out = place(source, cut, width, inner)
    return (x_grad, adam_out[None])


def solution(mesh):
    in_specs = (
        P(("dp", "expert"), None),
        P(("dp", "expert"), None),
        P(("dp", "expert"), None),
        P(("dp", "expert"), None),
        P(),
        P("expert", None, "dp"),
        P("expert", "dp", None),
        P("expert", None, "dp"),
        P("expert", None, "dp"),
    )
    out_specs = (P(("dp", "expert"), None), P("expert", None, "dp"))

    return jax.shard_map(shards, mesh=mesh, in_specs=in_specs, out_specs=out_specs, check_vma=False)
```

```python
import functools
import itertools

import jax
import jax.numpy as jnp
from jax import lax
from jax.experimental import pallas as pl
from jax.experimental.pallas import tpu as pltpu
from jax.sharding import PartitionSpec as P


ADAM_STEP = 100


coef_c = 0.7978845608028654
coef_a = 0.044715
beta_one = 0.9
beta_two = 0.999
adam_eps = 1e-08


MIB = 2**20

f32 = jnp.float32
bf16 = jnp.bfloat16
NN = (((1,), (0,)), ((), ()))
NT = (((1,), (1,)), ((), ()))
TN = (((0,), (0,)), ((), ()))


def mxu(a, b, dims):
    return lax.dot_general(a, b, dims, preferred_element_type=f32)


def gelu_slope(pre_act):
    square = pre_act * pre_act
    tanh_val = jnp.tanh(pre_act * (coef_c + coef_c * coef_a * square))
    bend = pre_act * (coef_c + 3.0 * coef_c * coef_a * square)
    return 0.5 + 0.5 * (tanh_val + bend * (1.0 - tanh_val * tanh_val))


def adam_step(weight_grad, first_moment, second_moment):
    unbias_one = 1.0 / (1.0 - beta_one**ADAM_STEP)
    unbias_two = 1.0 / (1.0 - beta_two**ADAM_STEP)
    first_hat = (beta_one * unbias_one) * first_moment + ((1.0 - beta_one) * unbias_one) * weight_grad
    second_hat = (beta_two * unbias_two) * second_moment + (
        (1.0 - beta_two) * unbias_two
    ) * (weight_grad * weight_grad)
    root = second_hat * lax.rsqrt(second_hat)
    return (first_hat / (root + adam_eps)).astype(bf16)


def pack_kernel(expert_count, capacity, ids_ref, gates_ref, x_ref, g_ref, rows_ref, where_ref):
    tok_count, width = x_ref.shape
    slots = expert_count * capacity
    first = ids_ref[0:1, :]
    second = ids_ref[1:2, :]
    experts = lax.broadcasted_iota(jnp.int32, (expert_count, tok_count), 0)
    hit_first = experts == first
    hit_second = experts == second
    hits = jnp.where(hit_first | hit_second, 1.0, 0.0).astype(bf16)
    earlier = lax.broadcasted_iota(jnp.int32, (tok_count, tok_count), 0)
    later = lax.broadcasted_iota(jnp.int32, (tok_count, tok_count), 1)
    upper = jnp.where(earlier < later, 1.0, 0.0).astype(bf16)
    before = mxu(hits, upper, NN)
    slot_first = jnp.sum(jnp.where(hit_first, before, 0.0), axis=0, keepdims=True)
    slot_second = jnp.sum(jnp.where(hit_second, before, 0.0), axis=0, keepdims=True)
    pos_first = first * capacity + slot_first.astype(jnp.int32)
    pos_second = second * capacity + slot_second.astype(jnp.int32)
    where_ref[0:1, :] = pos_first
    where_ref[1:2, :] = pos_second
    row = lax.broadcasted_iota(jnp.int32, (slots, tok_count), 0)
    at_first = row == pos_first
    at_second = row == pos_second
    pick = jnp.where(at_first | at_second, 1.0, 0.0).astype(bf16)
    gate = jnp.sum(
        jnp.where(at_first, gates_ref[0:1, :], 0.0) + jnp.where(at_second, gates_ref[1:2, :], 0.0),
        axis=1,
        keepdims=True,
    )
    rows_ref[:, :width] = mxu(pick, x_ref[...], NN).astype(bf16)
    rows_ref[:, width:] = (gate * mxu(pick, g_ref[...], NN)).astype(bf16)


def pack_rows(id_rows, gate_rows, tokens, out_grad, expert_count, capacity):
    tok_count, width = tokens.shape
    slots = expert_count * capacity
    return pl.pallas_call(
        functools.partial(pack_kernel, expert_count, capacity),
        out_shape=(
            jax.ShapeDtypeStruct((slots, 2 * width), bf16),
            jax.ShapeDtypeStruct((2, tok_count), jnp.int32),
        ),
        name="pack_rows",
    )(id_rows, gate_rows, tokens, out_grad)


def pre_block(block, w_in, w_out):
    width = block.shape[1] // 2
    pre_act = mxu(block[:, :width], w_in, NN)
    act_grad = mxu(block[:, width:], w_out, NT)
    return (act_grad * gelu_slope(pre_act)).astype(bf16)


def pre_tile(rows, w_in, w_out, pre_ref):
    per = rows[0].shape[0]
    for b, block in enumerate(rows):
        pre_ref[b * per : (b + 1) * per, :] = pre_block(block, w_in, w_out)


def own_kernel(rows_ref, w_in_ref, w_out_ref, pre_ref, xt_ref, w_in_buf, w_out_buf, sems):
    tile = pre_ref.shape[1]
    gets = [
        pltpu.make_async_copy(w_in_ref.at[:, pl.ds(0, tile)], w_in_buf, sems.at[0]),
        pltpu.make_async_copy(w_out_ref.at[pl.ds(0, tile), :], w_out_buf, sems.at[1]),
    ]
    for get in gets:
        get.start()
    xt_ref[...] = rows_ref[:, : xt_ref.shape[0]].T
    for get in gets:
        get.wait()
    pre_ref[...] = pre_block(rows_ref, w_in_buf[...], w_out_buf[...])


def own_step(rows, w_in, w_out, tile):
    per, width = rows.shape[0], rows.shape[1] // 2
    vmem = pl.BlockSpec(memory_space=pltpu.VMEM)
    anywhere = pl.BlockSpec(memory_space=pl.ANY)
    return pl.pallas_call(
        own_kernel,
        in_specs=[vmem, anywhere, anywhere],
        out_specs=[vmem, vmem],
        out_shape=[
            jax.ShapeDtypeStruct((per, tile), bf16),
            jax.ShapeDtypeStruct((width, per), bf16),
        ],
        scratch_shapes=[
            pltpu.VMEM((width, tile), bf16),
            pltpu.VMEM((tile, width), bf16),
            pltpu.SemaphoreType.DMA((2,)),
        ],
        compiler_params=pltpu.CompilerParams(vmem_limit_bytes=48 * MIB),
        cost_estimate=pl.CostEstimate(
            flops=4 * per * width * tile, bytes_accessed=4 * tile * width, transcendentals=0
        ),
        name="own_step",
    )(rows, w_in, w_out)


def first_kernel(others, *refs):
    rows = refs[:others]
    pre_own, xt_own, w_in_ref, w_out_ref, m_ref, v_ref, adam_ref, pre_ref, xt_ref = refs[
        others : others + 9
    ]
    w_in_buf, w_out_buf, m_buf, v_buf, pre_buf, xt_buf, sems = refs[others + 9 :]
    width, tile = m_buf.shape
    per = xt_own.shape[1]
    gets = [
        pltpu.make_async_copy(w_in_ref.at[:, pl.ds(0, tile)], w_in_buf, sems.at[0]),
        pltpu.make_async_copy(w_out_ref.at[pl.ds(0, tile), :], w_out_buf, sems.at[1]),
        pltpu.make_async_copy(m_ref.at[:, pl.ds(0, tile)], m_buf, sems.at[2]),
        pltpu.make_async_copy(v_ref.at[:, pl.ds(0, tile)], v_buf, sems.at[3]),
    ]
    for get in gets:
        get.start()
    xt_buf[:, :per] = xt_own[...]
    pre_buf[:per, :] = pre_own[...]
    for b in range(others):
        xt_buf[:, (b + 1) * per : (b + 2) * per] = rows[b][:, :width].T
    for get in gets[:2]:
        get.wait()
    for b in range(others):
        pre_buf[(b + 1) * per : (b + 2) * per, :] = pre_block(
            rows[b], w_in_buf[...], w_out_buf[...]
        )
    puts = [
        pltpu.make_async_copy(xt_buf, xt_ref, sems.at[4]),
        pltpu.make_async_copy(pre_buf, pre_ref, sems.at[5]),
    ]
    for put in puts:
        put.start()
    weight_grad = mxu(xt_buf[...], pre_buf[...], NN)
    for get in gets[2:]:
        get.wait()
    adam_ref[...] = adam_step(weight_grad, m_buf[...], v_buf[...])
    for put in puts:
        put.wait()


def first_step(rows, pre_own, xt_own, w_in, w_out, first_moment, second_moment, tile):
    width, per = xt_own.shape
    total = (len(rows) + 1) * per
    vmem = pl.BlockSpec(memory_space=pltpu.VMEM)
    anywhere = pl.BlockSpec(memory_space=pl.ANY)
    return pl.pallas_call(
        functools.partial(first_kernel, len(rows)),
        in_specs=[vmem] * (len(rows) + 2) + [anywhere] * 4,
        out_specs=[vmem, anywhere, anywhere],
        out_shape=[
            jax.ShapeDtypeStruct((width, tile), bf16),
            jax.ShapeDtypeStruct((total, tile), bf16),
            jax.ShapeDtypeStruct((width, total), bf16),
        ],
        scratch_shapes=[
            pltpu.VMEM((width, tile), bf16),
            pltpu.VMEM((tile, width), bf16),
            pltpu.VMEM((width, tile), f32),
            pltpu.VMEM((width, tile), f32),
            pltpu.VMEM((total, tile), bf16),
            pltpu.VMEM((width, total), bf16),
            pltpu.SemaphoreType.DMA((6,)),
        ],
        compiler_params=pltpu.CompilerParams(vmem_limit_bytes=56 * MIB),
        cost_estimate=pl.CostEstimate(
            flops=6 * total * width * tile, bytes_accessed=14 * tile * width, transcendentals=0
        ),
        name="first_step",
    )(*rows, pre_own, xt_own, w_in, w_out, first_moment, second_moment)


def rest_kernel(blocks, *refs):
    rows = refs[:blocks]
    first_ref, w_first_ref, w_in_ref, w_out_ref, pre_ref = refs[blocks : blocks + 5]
    parts = refs[blocks + 5 : -1]
    total_ref = refs[-1]
    per = rows[0].shape[0]
    step = pl.program_id(0)

    @pl.when(step == 0)
    def _():
        total_ref[...] = mxu(first_ref[...], w_first_ref[...], NT)

    pre_tile(rows, w_in_ref[...], w_out_ref[...], pre_ref)
    total_ref[...] += mxu(pre_ref[...], w_in_ref[...], NT)

    @pl.when(step == pl.num_programs(0) - 1)
    def _():
        for b in range(blocks):
            parts[b][...] = total_ref[b * per : (b + 1) * per, :].astype(bf16)


def rest_step(rows, pre_first, w_in, w_out, tile):
    per, width = rows[0].shape[0], rows[0].shape[1] // 2
    total = len(rows) * per
    tiles = w_in.shape[1] // tile - 1
    corner = lambda j: (0, 0)
    return pl.pallas_call(
        functools.partial(rest_kernel, len(rows)),
        grid=(tiles,),
        in_specs=[pl.BlockSpec(r.shape, corner) for r in rows]
        + [
            pl.BlockSpec((total, tile), corner),
            pl.BlockSpec((width, tile), corner),
            pl.BlockSpec((width, tile), lambda j: (0, j + 1)),
            pl.BlockSpec((tile, width), lambda j: (j + 1, 0)),
        ],
        out_specs=[pl.BlockSpec((total, tile), lambda j: (0, j))]
        + [pl.BlockSpec((per, width), corner) for _ in rows],
        out_shape=[jax.ShapeDtypeStruct((total, tiles * tile), bf16)]
        + [jax.ShapeDtypeStruct((per, width), bf16) for _ in rows],
        scratch_shapes=[pltpu.VMEM((total, width), f32)],
        compiler_params=pltpu.CompilerParams(vmem_limit_bytes=56 * MIB),
        cost_estimate=pl.CostEstimate(
            flops=6 * total * width * tile * tiles,
            bytes_accessed=4 * tile * width * tiles,
            transcendentals=0,
        ),
        name="rest_step",
    )(*rows, pre_first, w_in, w_in, w_out)


def adam_kernel(xt_ref, pre_ref, m_ref, v_ref, out_ref):
    weight_grad = mxu(xt_ref[...], pre_ref[...], NN)
    out_ref[...] = adam_step(weight_grad, m_ref[...], v_ref[...])


def adam_block(x_t, pre_rest, first_moment, second_moment, start, tiles, tile, part, parts):
    width, total = x_t.shape
    rows = width // parts
    block = pl.BlockSpec((rows, tile), lambda j: (part, start + j))
    return pl.pallas_call(
        adam_kernel,
        grid=(tiles,),
        in_specs=[
            pl.BlockSpec((rows, total), lambda j: (part, 0)),
            pl.BlockSpec((total, tile), lambda j: (0, start - 1 + j)),
            block,
            block,
        ],
        out_specs=pl.BlockSpec((rows, tile), lambda j: (0, j)),
        out_shape=jax.ShapeDtypeStruct((rows, tiles * tile), bf16),
        compiler_params=pltpu.CompilerParams(vmem_limit_bytes=60 * MIB),
        cost_estimate=pl.CostEstimate(
            flops=2 * total * rows * tile * tiles,
            bytes_accessed=10 * tile * rows * tiles,
            transcendentals=0,
        ),
    )(x_t, pre_rest, first_moment, second_moment)


def place_kernel(boxes, source_ref, *refs):
    sources, at = [], 0
    for box in boxes:
        sources.append(refs[at : at + box[5]])
        at += box[5]
    out_ref = refs[at]
    bufs = refs[at + 1 : at + 1 + len(boxes)]
    in_sem, out_sem = refs[at + 1 + len(boxes) :]
    most = max(len(arrays) for arrays in sources)
    for k in range(most):

        @pl.when(source_ref[0] == k)
        def _(k=k):
            for n, arrays in enumerate(sources):
                array = arrays[min(k, len(arrays) - 1)]
                start, high = boxes[n][2], boxes[n][3]
                pltpu.make_async_copy(
                    array.at[pl.ds(start, high)], bufs[n], in_sem.at[n]
                ).start()

    puts = []
    for n, (row, col, start, high, wide, _) in enumerate(boxes):
        pltpu.make_async_copy(
            sources[n][0].at[pl.ds(start, high)], bufs[n], in_sem.at[n]
        ).wait()
        put = pltpu.make_async_copy(
            bufs[n], out_ref.at[pl.ds(row + start, high), pl.ds(col, wide)], out_sem.at[n]
        )
        put.start()
        puts.append(put)
    for put in puts:
        put.wait()


def place(source, pieces, width, inner):
    boxes = [piece[:5] + (len(piece[5]),) for piece in pieces]
    args = [array for piece in pieces for array in piece[5]]
    return pl.pallas_call(
        functools.partial(place_kernel, boxes),
        in_specs=[pl.BlockSpec(memory_space=pltpu.SMEM)]
        + [pl.BlockSpec(memory_space=pl.ANY) for _ in args],
        out_specs=pl.BlockSpec(memory_space=pl.ANY),
        out_shape=jax.ShapeDtypeStruct((width, inner), bf16),
        scratch_shapes=[pltpu.VMEM((box[3], box[4]), bf16) for box in boxes]
        + [pltpu.SemaphoreType.DMA((len(boxes),)), pltpu.SemaphoreType.DMA((len(boxes),))],
        compiler_params=pltpu.CompilerParams(vmem_limit_bytes=8 * MIB),
        cost_estimate=pl.CostEstimate(
            flops=0, bytes_accessed=4 * width * inner, transcendentals=0
        ),
        name="place",
    )(source, *args)


def swap_plans(half):
    line = half >> 1
    groups = {}
    for e in range(half):
        groups.setdefault(e & ~(line | 1), []).append(e)
    groups = list(groups.values())
    if half < 4 or len(groups) > 2:
        return []
    forced = {0, half - 1}
    switches = []
    for members in groups:
        must = forced & set(members)
        plans = [
            set(s)
            for k in range(2, len(members) + 1)
            for s in itertools.combinations(members, k)
            if must <= set(s)
        ]
        table = []
        for mask in range(1 << half):
            moved = must | {e for e in members if mask >> e & 1}
            table.append(next(n for n, plan in enumerate(plans) if moved <= plan))
        switches.append((plans, table))
    return switches


def combine_kernel(capacity, half, upper_ref, where_ref, mirror_ref, back_ref, own_ref, sum_ref):
    slots, tok_count = back_ref.shape[0], own_ref.shape[0]
    row = lax.broadcasted_iota(jnp.int32, (slots, tok_count), 0).astype(f32)
    block = jnp.floor((row + 0.5) * (1.0 / capacity))
    expert = jnp.floor(block * 0.5)
    side = block - 2.0 * expert
    upper = upper_ref[0].astype(f32)
    place_of = (expert + half * upper) * capacity + (row - block * capacity)
    for ref, out, wanted in ((where_ref, own_ref, upper), (mirror_ref, sum_ref, 1.0 - upper)):
        first, second = ref[0:1, :].astype(f32), ref[1:2, :].astype(f32)
        hit = ((place_of == first) | (place_of == second)) & (side == wanted)
        pick = jnp.where(hit, 1.0, 0.0).astype(bf16)
        out[...] = mxu(pick, back_ref[...], TN).astype(out.dtype)


def combine_rows(upper, where_to, mirror_to, returned, tok_count, capacity, half):
    width = returned.shape[1]
    vmem = pl.BlockSpec(memory_space=pltpu.VMEM)
    return pl.pallas_call(
        functools.partial(combine_kernel, capacity, half),
        in_specs=[pl.BlockSpec(memory_space=pltpu.SMEM), vmem, vmem, vmem],
        out_shape=(
            jax.ShapeDtypeStruct((tok_count, width), bf16),
            jax.ShapeDtypeStruct((tok_count, width), bf16),
        ),
        cost_estimate=pl.CostEstimate(
            flops=4 * tok_count * returned.shape[0] * width,
            bytes_accessed=2 * returned.size + 6 * tok_count * width,
            transcendentals=0,
        ),
        name="combine_rows",
    )(upper, where_to, mirror_to, returned)


def dp_shift(block, apart):
    count = lax.axis_size("dp")
    return lax.ppermute(block, "dp", [(i, i ^ apart) for i in range(count)])


def shards(
    tokens, out_grad, gates, expert_ids, swap_list, w_in, w_out, first_moment, second_moment
):
    expert_count = lax.axis_size("expert")
    dp_count = lax.axis_size("dp")
    half = 1 << (expert_count.bit_length() - 2)
    own_index = lax.axis_index("expert")
    lane_ids = jnp.arange(expert_count, dtype=jnp.int32)
    partner_me = jnp.sum(jnp.where(lane_ids == own_index, swap_list, 0))
    is_moved = (partner_me != own_index).astype(jnp.int32)
    moved_bits = jnp.where((swap_list != lane_ids) & (lane_ids < half), 1 << lane_ids, 0)
    moved_mask = jnp.sum(moved_bits)
    tok_count, width = tokens.shape
    capacity = 3 * tok_count // expert_count
    slots = expert_count * capacity

    rows, where_to = pack_rows(expert_ids.T, gates.T, tokens, out_grad, expert_count, capacity)
    own = lax.all_to_all(
        rows.reshape(expert_count, capacity, 2 * width),
        "expert",
        split_axis=0,
        concat_axis=0,
        tiled=True,
    ).reshape(slots, 2 * width)
    all_rows = [own] + [dp_shift(own, d) for d in range(1, dp_count)]
    if dp_count == 2:
        all_rows = [pltpu.with_memory_space_constraint(r, pltpu.VMEM) for r in all_rows]

    inner = w_in.shape[2]
    tile = 256 if inner % 256 == 0 else 128
    tiles = inner // tile
    route = [(e, e ^ half) for e in range(expert_count)]
    across = [(e, e ^ 1) for e in range(expert_count)]

    pre_own, xt_own = own_step(all_rows[0], w_in[0], w_out[0], tile)
    if dp_count == 2:
        pre_own = pltpu.with_memory_space_constraint(pre_own, pltpu.VMEM)
        xt_own = pltpu.with_memory_space_constraint(xt_own, pltpu.VMEM)
    first, pre_first, x_t = first_step(
        all_rows[1:], pre_own, xt_own, w_in[0], w_out[0], first_moment[0], second_moment[0], tile
    )
    first_got = lax.ppermute(first, "expert", route)
    pieces = [(0, 0, width, tile, [first, first_got])]

    pre_rest, *parts = rest_step(all_rows, pre_first, w_in[0], w_out[0], tile)
    total = parts[0].astype(f32)
    for d in range(1, dp_count):
        total = total + dp_shift(parts[d], d).astype(f32)
    total = total.astype(bf16).reshape(2, half, capacity, width).transpose(1, 0, 2, 3)
    returned = lax.all_to_all(
        total.reshape(half, 2 * capacity, width),
        "expert",
        split_axis=0,
        concat_axis=0,
        axis_index_groups=[list(range(half)), list(range(half, expert_count))],
        tiled=True,
    ).reshape(slots, width)
    upper = (own_index >= half).astype(jnp.int32).reshape(1)
    mirror_to = lax.ppermute(where_to, "expert", route)
    own_sum, mirror_sum = combine_rows(
        upper, where_to, mirror_to, returned, tok_count, capacity, half
    )
    other_sum = lax.ppermute(mirror_sum, "expert", route)
    switches = swap_plans(half) if tiles > 2 else []
    direct = 1 if switches else tiles - 1
    moments = (first_moment[0], second_moment[0])
    second = adam_block(x_t, pre_rest, *moments, 1, direct, tile, 0, 1)
    second_got = lax.ppermute(second, "expert", route)
    pieces.append((0, tile, width, direct * tile, [second, second_got]))
    group = jnp.zeros((), jnp.int32)

    if switches:
        at, left = 1 + direct, tiles - 1 - direct
        far = adam_block(x_t, pre_rest, *moments, at, left, tile, 1, 2)
        lent = lax.ppermute(far, "expert", across)
        near = adam_block(x_t, pre_rest, *moments, at, left, tile, 0, 2)

        def branch(plan):
            pairs = [(e, e ^ half) for p in plan for e in (p, p ^ half)]
            skew = [(e ^ 1, f) for e, f in pairs]

            def run(near, lent):
                return (
                    lax.ppermute(near, "expert", pairs),
                    lax.ppermute(lent, "expert", skew),
                )

            return run

        near, lent, own_sum = lax.optimization_barrier((near, lent, own_sum))
        near_all, far_all = [near], [far]
        for n, (plans, table) in enumerate(switches):
            choice = jnp.asarray(table, jnp.int32)[moved_mask]
            near_got, far_got = lax.switch(choice, [branch(p) for p in plans], near, lent)
            near_all.append(near_got)
            far_all.append(far_got)
            members = {e for plan in plans for p in plan for e in (p, p ^ half)}
            here = jnp.asarray([e in members for e in range(expert_count)])
            group += jnp.sum(jnp.where(here & (lane_ids == own_index), n, 0))
        far_all[-1], own_sum = lax.optimization_barrier((far_all[-1], own_sum))
        wide = left * tile
        pieces.append((0, at * tile, width // 2, wide, near_all))
        pieces.append((width // 2, at * tile, width // 2, wide, far_all))

    source = (is_moved * (1 + group)).reshape(1)
    cut = []
    for row, col, high, wide, arrays in pieces:
        step = width
        for at in range(0, high, step):
            cut.append((row, col, at, min(step, high - at), wide, arrays))
    adam_out = place(source, cut, width, inner)
    x_grad = (own_sum.astype(f32) + other_sum.astype(f32)).astype(bf16)
    return (x_grad, adam_out[None])


def solution(mesh):
    in_specs = (
        P(("dp", "expert"), None),
        P(("dp", "expert"), None),
        P(("dp", "expert"), None),
        P(("dp", "expert"), None),
        P(),
        P("expert", None, "dp"),
        P("expert", "dp", None),
        P("expert", None, "dp"),
        P("expert", None, "dp"),
    )
    out_specs = (P(("dp", "expert"), None), P("expert", None, "dp"))

    return jax.shard_map(shards, mesh=mesh, in_specs=in_specs, out_specs=out_specs, check_vma=False)
```
